256 devices in a mesh: tile: 32 (over x_lo, z, core), mlp: 8 (over y, x_hi).
Axes of the slice: x: 4 (x_hi: 2, x_lo: 2; x = x_hi * 2 + x_lo), y: 4, z: 8, core: 2. Of those that a mesh axis runs over, the one named last changes fastest.
Arguments:
- features: bfloat16 [32, 512, 2, 2, 256], P('tile', 'mlp'), may hold values from -6 to 6
- w_in: bfloat16 [256, 1024], P(None, 'mlp'), may hold values from -0.375 to 0.375
- w_out: bfloat16 [1024, 256], P('mlp'), may hold values from -0.1875 to 0.1875
- bilinear: bfloat16 [256, 256], replicated, may hold values from -0.375 to 0.375
- partner: int32 [32, 2, 512], replicated, may hold values from 0 to 13823
- counts: int32 [32, 2, 2], replicated, may hold values from 128 to 512
Outputs:
- pair_loss: float32 [], replicated
- grad_in: float32 [256, 1024], P(None, 'mlp')
- grad_out: float32 [1024, 256], P('mlp')
- grad_bilinear: float32 [256, 256], replicated
The draws below stay inside these ranges and needn't reach their ends.
All inputs are finite; a program needn't handle non-finite values.
Results may differ from the reference program's by a relative error of at most 0.0024.
The reference program's roundings to bfloat16 on the way (of `active`, `embedded`, `query`, `slope`, `query_grad`, `embed_grad` and `hidden_grad`) count: a program that leaves them out, or rounds other values in their place, can miss the bound.
Values may be sent and summed in bfloat16 or wider, within the bound.
A program may use at most 64 MiB of HBM per device.

```python
import jax
import jax.numpy as jnp

F = 256
HID = 1024
S = 512
BLOCKS = 32
HEAVY = 3456
PRE_SITES = 32768


def draw_counts(key, part):
    values = jax.random.randint(key, (BLOCKS, 2, 2), S // 4, S + 1, dtype=jnp.int32)
    values = values.at[0, 0, 0].set(S)
    return values.at[0, 1, 1].set(S // 4)


def with_ends(drawn, key, least, high):
    spot = [jax.random.randint(jax.random.fold_in(key, axis), (), 0, length) for axis, length in enumerate(drawn.shape)]
    widest = drawn.shape.index(max(drawn.shape))
    next_to = spot[:widest] + [(spot[widest] + 1) % drawn.shape[widest]] + spot[widest + 1:]
    return drawn.at[tuple(spot)].set(least).at[tuple(next_to)].set(high)


def block_levels(own_key, dims, pieces, smallest, top_value):
    factor_of, own = 1.0, jax.random.fold_in(own_key, 6)
    for position, blocks in pieces:
        draws = jnp.exp(jax.random.uniform(jax.random.fold_in(own, position), (blocks,), jnp.float32, smallest / len(pieces), top_value / len(pieces)))
        factor_of = factor_of * jnp.repeat(draws, dims[position] // blocks).reshape([-1 if axis == position else 1 for axis in range(len(dims))])
    return factor_of


def centred(stream_key, dims, scale, limit, pieces=(), kind=jnp.bfloat16):
    factor_of = block_levels(stream_key, dims, pieces, -0.22, 0.18) if pieces else 1.0
    drawn = jax.random.normal(stream_key, dims, jnp.float32) * scale * factor_of
    return jnp.minimum(jnp.maximum(drawn, -limit), limit).astype(kind)


def setup_inputs(seed: int = 0) -> dict:
    splits = jax.random.split(jax.random.key(seed), 7)
    features = centred(splits[0], (BLOCKS, S, 2, 2, F), 1.0, 6.0, ((0, 32), (1, 8)))
    w_in = centred(splits[1], (F, HID), F ** -0.5, 0.375, ((1, 8),))
    w_out = centred(splits[2], (HID, F), HID ** -0.5, 0.1875, ((0, 8),))
    bilinear = centred(splits[3], (F, F), F ** -0.5, 0.375)
    partner = with_ends(jax.random.randint(splits[4], (BLOCKS, 2, S), 0, 27 * S), jax.random.fold_in(splits[4], 1), 0, (27 * S) - 1).astype(jnp.int32)
    counts = draw_counts(jax.random.fold_in(splits[6], 71), 0)
    return {"features": features, "w_in": w_in, "w_out": w_out, "bilinear": bilinear, "partner": partner, "counts": counts}


def to_grid(array):
    depth_count = array.shape[0] // 8
    rest_shape = array.shape[2:]
    shaped = array.reshape((2, 4, depth_count, 2) + rest_shape)
    moved = jnp.moveaxis(shaped, 3, 1)
    return moved.reshape((4, 4, depth_count) + rest_shape)

def from_grid(grid):
    depth_count = grid.shape[2]
    rest_shape = grid.shape[3:]
    shaped = grid.reshape((2, 2, 4, depth_count) + rest_shape)
    moved = jnp.moveaxis(shaped, 1, 3)
    return moved.reshape((8 * depth_count, 2) + rest_shape)

def shifted(grid, step_x, step_y, step_z):
    padding = [(1, 1)] * 3 + [(0, 0)] * (grid.ndim - 3)
    padded = jnp.pad(grid, padding)
    return padded[1 + step_x:1 + step_x + grid.shape[0], 1 + step_y:1 + step_y + grid.shape[1], 1 + step_z:1 + step_z + grid.shape[2]]

def reference(features, w_in, w_out, bilinear, partner, counts):
    blocks_here = features.shape[0]
    inputs = features.reshape(blocks_here, S, 4, F).astype(jnp.float32)
    hidden = jnp.einsum('bscf,fh->bsch', inputs, w_in.astype(jnp.float32))
    active = jax.nn.gelu(hidden).astype(jnp.bfloat16)
    mixed_rows = jnp.einsum('bsch,hf->bscf', active.astype(jnp.float32), w_out.astype(jnp.float32))
    embedded = (inputs + mixed_rows).astype(jnp.bfloat16)
    pre_rows = embedded[:, :, 0::2]
    post_rows = embedded[:, :, 1::2]
    query = jnp.einsum('bsuf,fg->bsug', pre_rows.astype(jnp.float32), bilinear.astype(jnp.float32)).astype(jnp.bfloat16)
    query_grid = to_grid(jnp.moveaxis(query, 2, 1)).astype(jnp.float32)
    post_grid = to_grid(jnp.moveaxis(post_rows, 2, 1)).astype(jnp.float32)
    partner_grid = to_grid(partner)
    pre_count = to_grid(counts[:, :, 0])
    post_count = to_grid(counts[:, :, 1])
    site_index = jnp.arange(S, dtype=jnp.int32)
    pre_valid = site_index < pre_count[..., None]
    score_scale = F ** (-0.5)
    factor = score_scale / PRE_SITES
    loss_sum = jnp.zeros((), jnp.float32)
    query_grad = jnp.zeros(query_grid.shape, jnp.float32)
    post_grad = jnp.zeros(post_grid.shape, jnp.float32)
    for step_x in (-1, 0, 1):
        for step_y in (-1, 0, 1):
            for step_z in (-1, 0, 1):
                others = shifted(post_grid, step_x, step_y, step_z)
                other_valid = site_index < shifted(post_count, step_x, step_y, step_z)[..., None]
                code = (step_x + 1) * 9 + (step_y + 1) * 3 + step_z + 1
                score = jnp.einsum('xyzif,xyzjf->xyzij', query_grid, others) * score_scale
                target = (partner_grid[..., :, None] == code * S + site_index).astype(jnp.float32)
                weight = (pre_valid[..., :, None] & other_valid[..., None, :]).astype(jnp.float32)
                chance = jax.nn.sigmoid(score)
                missed = HEAVY * target * jnp.log1p(jnp.exp(-score))
                spurious = (1.0 - target) * jnp.log1p(jnp.exp(score))
                loss_sum = loss_sum + jnp.sum(weight * (missed + spurious))
                signed = (1.0 - target) * chance - HEAVY * target * (1.0 - chance)
                slope = (weight * signed * factor).astype(jnp.bfloat16).astype(jnp.float32)
                query_grad = query_grad + jnp.einsum('xyzij,xyzjf->xyzif', slope, others)
                back = jnp.einsum('xyzij,xyzif->xyzjf', slope, query_grid)
                post_grad = post_grad + shifted(back, -step_x, -step_y, -step_z)
    query_back = jnp.moveaxis(from_grid(query_grad), 1, 2).astype(jnp.bfloat16).astype(jnp.float32)
    post_back = jnp.moveaxis(from_grid(post_grad), 1, 2)
    grad_bilinear = jnp.einsum('bsuf,bsug->fg', pre_rows.astype(jnp.float32), query_back)
    pre_back = jnp.einsum('bsug,fg->bsuf', query_back, bilinear.astype(jnp.float32))
    embed_grad = jnp.stack([pre_back[:, :, 0], post_back[:, :, 0], pre_back[:, :, 1], post_back[:, :, 1]], axis=2).astype(jnp.bfloat16).astype(jnp.float32)
    active_grad = jnp.einsum('bscf,hf->bsch', embed_grad, w_out.astype(jnp.float32))
    unused, pullback = jax.vjp(jax.nn.gelu, hidden)
    hidden_grad = pullback(active_grad)[0].astype(jnp.bfloat16).astype(jnp.float32)
    grad_in = jnp.einsum('bscf,bsch->fh', inputs, hidden_grad)
    grad_out = jnp.einsum('bsch,bscf->hf', active.astype(jnp.float32), embed_grad)
    pair_loss = loss_sum / (PRE_SITES * 27 * S)
    return (pair_loss, grad_in, grad_out, grad_bilinear)
```

```python
import jax
import jax.numpy as jnp
from jax import lax
from jax.sharding import PartitionSpec as P

column_plan = ((-1, 1), (0, 0), (0, 1), (1, 0))


def shifted(array, axis, by):
    peers = lax.axis_size(axis)
    pairs = [(i, i + by) for i in range(peers) if 0 <= i + by < peers]
    return lax.ppermute(array, axis, pairs)


def butterfly_sum(x, axis):
    peers = lax.axis_size(axis)
    step = 1
    while step < peers:
        x = x + lax.ppermute(x, axis, [(i, i ^ step) for i in range(peers)])
        step *= 2
    return x


def butterfly_gather(x, axis):
    peers = lax.axis_size(axis)
    me = lax.axis_index(axis)
    step = 1
    while step < peers:
        other = lax.ppermute(x, axis, [(i, i ^ step) for i in range(peers)])
        low = (me & step) == 0
        x = jnp.where(low, jnp.concatenate([x, other], 0), jnp.concatenate([other, x], 0))
        step *= 2
    return x


def butterfly_scatter(x, axis):
    peers = lax.axis_size(axis)
    me = lax.axis_index(axis)
    step = peers // 2
    while step >= 1:
        half = x.shape[0] // 2
        upper = (me & step) != 0
        send = jnp.where(upper, x[:half], x[half:])
        keep = jnp.where(upper, x[half:], x[:half])
        x = keep + lax.ppermute(send, axis, [(i, i ^ step) for i in range(peers)])
        step //= 2
    return x


def pair_slope(raw_score, target, weight, heavy_weight, factor):
    chance = jax.nn.sigmoid(raw_score)
    signed = (1.0 - target) * chance - heavy_weight * target * (1.0 - chance)
    return (weight * signed * factor).astype(jnp.bfloat16)


def pair_cost(raw_score, target, weight, heavy_weight):
    missed = heavy_weight * target * jnp.log1p(jnp.exp(-raw_score))
    spurious = (1.0 - target) * jnp.log1p(jnp.exp(raw_score))
    return jnp.sum(weight * (missed + spurious))


def local(features, w_in, w_out, bilinear, partner, counts):
    row_part = features.shape[1]
    feature_width = features.shape[4]
    groups = lax.axis_size("mlp")
    site_rows = row_part * groups
    tile_count = lax.axis_size("tile")
    grid_depth = tile_count // 8
    tile_here = lax.axis_index("tile")
    member = lax.axis_index("mlp")
    block_x = tile_here // (4 * grid_depth)
    block_y = tile_here // grid_depth % 4
    block_z = tile_here % grid_depth
    heavy_weight = 27 * site_rows // 4
    score_scale = feature_width ** (-0.5)
    factor = score_scale / (2 * tile_count * site_rows)
    own_rows = member * row_part + jnp.arange(row_part, dtype=jnp.int32)
    all_rows = jnp.arange(site_rows, dtype=jnp.int32)
    mine_counts = lax.dynamic_index_in_dim(counts, tile_here, 0, keepdims=False)
    mine_partner = lax.dynamic_index_in_dim(partner, tile_here, 0, keepdims=False)
    own_partner = lax.dynamic_slice_in_dim(mine_partner, member * row_part, row_part, 1)
    own_pre_ok = own_rows[None, :] < mine_counts[:, 0:1]
    own_post_ok = own_rows[None, :] < mine_counts[:, 1:2]
    local_x = features.reshape(row_part, 4, feature_width)
    whole_x = butterfly_gather(local_x, "mlp")
    hidden_pre = jnp.einsum("rcf,fh->rch", whole_x, w_in, preferred_element_type=jnp.float32)
    active = jax.nn.gelu(hidden_pre).astype(jnp.bfloat16)
    mixed_rows = butterfly_scatter(
        jnp.einsum("rch,hf->rcf", active, w_out, preferred_element_type=jnp.float32), "mlp"
    )
    embedded = (local_x.astype(jnp.float32) + mixed_rows).astype(jnp.bfloat16)
    pre_local = embedded[:, 0::2]
    post_local = embedded[:, 1::2]
    query_local = jnp.einsum(
        "ruf,fg->rug", pre_local, bilinear, preferred_element_type=jnp.float32
    ).astype(jnp.bfloat16)

    def pair_code(step_x, step_y, step_z):
        return ((step_x + 1) * 9 + (step_y + 1) * 3 + step_z + 1) * site_rows

    loss_sum = jnp.zeros((), jnp.float32)
    post_grads = [
        jnp.zeros((row_part, feature_width), jnp.float32),
        jnp.zeros((row_part, feature_width), jnp.float32),
    ]
    post_whole, query_whole = (
        butterfly_gather(post_local, "mlp"),
        butterfly_gather(query_local, "mlp"),
    )
    query_grads = [
        jnp.zeros((row_part, feature_width), jnp.float32),
        jnp.zeros((row_part, feature_width), jnp.float32),
    ]
    for step_y in (-1, 0, 1):
        for step_z in (-1, 0, 1):
            post_cols, query_cols, post_valid, pre_valid, label_cols = ([], [], [], [], [])
            for position in range(4):
                shift_x, sub_tile = column_plan[position]
                offset = shift_x * 4 * grid_depth + step_y * grid_depth + step_z
                inside = (
                    (block_x + shift_x >= 0)
                    & (block_x + shift_x < 2)
                    & (block_y + step_y >= 0)
                    & (block_y + step_y < 4)
                    & (block_z + step_z >= 0)
                    & (block_z + step_z < grid_depth)
                )
                source = jnp.clip(tile_here + offset, 0, tile_count - 1)
                tile_counts = lax.dynamic_index_in_dim(counts, source, 0, keepdims=False)[sub_tile]
                labels = lax.dynamic_index_in_dim(partner, source, 0, keepdims=False)[sub_tile]
                offset, sub_tile, inside, tile_counts, labels = (
                    offset,
                    sub_tile,
                    inside,
                    tile_counts,
                    labels,
                )
                both_sides = jnp.stack([post_whole[:, sub_tile], query_whole[:, sub_tile]], 0)
                if offset != 0:
                    both_sides = shifted(both_sides, "tile", -offset)
                post_cols.append(both_sides[0])
                query_cols.append(both_sides[1])
                post_valid.append(inside & (all_rows < tile_counts[1]))
                pre_valid.append(inside & (all_rows < tile_counts[0]))
                label_cols.append(labels)
            for pretile in (0, 1):
                chosen = range(pretile, pretile + 3)
                others = jnp.concatenate([post_cols[column_id] for column_id in chosen], 0)
                col_key = jnp.concatenate(
                    [
                        pair_code(column_id - 1 - pretile, step_y, step_z) + all_rows
                        for column_id in chosen
                    ]
                )
                col_ok = jnp.concatenate([post_valid[column_id] for column_id in chosen])
                raw_score = (
                    jnp.einsum(
                        "rf,cf->rc",
                        query_local[:, pretile],
                        others,
                        preferred_element_type=jnp.float32,
                    )
                    * score_scale
                )
                target = (own_partner[pretile][:, None] == col_key[None, :]).astype(jnp.float32)
                weight = (own_pre_ok[pretile][:, None] & col_ok[None, :]).astype(jnp.float32)
                loss_sum = loss_sum + pair_cost(raw_score, target, weight, heavy_weight)
                slope = pair_slope(raw_score, target, weight, heavy_weight, factor)
                query_grads[pretile] = query_grads[pretile] + jnp.dot(
                    slope, others, preferred_element_type=jnp.float32
                )
                senders = jnp.concatenate([query_cols[column_id] for column_id in chosen], 0)
                row_key = jnp.concatenate(
                    [
                        label_cols[column_id] - pair_code(pretile - column_id + 1, -step_y, -step_z)
                        for column_id in chosen
                    ]
                )
                row_ok = jnp.concatenate([pre_valid[column_id] for column_id in chosen])
                back_score = (
                    jnp.einsum(
                        "cf,rf->cr",
                        post_local[:, pretile],
                        senders,
                        preferred_element_type=jnp.float32,
                    )
                    * score_scale
                )
                back_target = (own_rows[:, None] == row_key[None, :]).astype(jnp.float32)
                back_weight = (own_post_ok[pretile][:, None] & row_ok[None, :]).astype(jnp.float32)
                back_slope = pair_slope(back_score, back_target, back_weight, heavy_weight, factor)
                post_grads[pretile] = post_grads[pretile] + jnp.dot(
                    back_slope, senders, preferred_element_type=jnp.float32
                )
    query_total = jnp.stack(query_grads, 1)
    query_back = query_total.astype(jnp.bfloat16)
    post_back = jnp.stack(post_grads, 1)
    bilinear_part = jnp.einsum(
        "ruf,rug->fg", pre_local, query_back, preferred_element_type=jnp.float32
    )
    pre_back = jnp.einsum("rug,fg->ruf", query_back, bilinear, preferred_element_type=jnp.float32)
    embed_grad = jnp.stack(
        [pre_back[:, 0], post_back[:, 0], pre_back[:, 1], post_back[:, 1]], 1
    ).astype(jnp.bfloat16)
    embed_whole = butterfly_gather(embed_grad, "mlp")
    active_grad = jnp.einsum("rcf,hf->rch", embed_whole, w_out, preferred_element_type=jnp.float32)
    unused, pullback = jax.vjp(jax.nn.gelu, hidden_pre)
    hidden_grad = pullback(active_grad)[0].astype(jnp.bfloat16)
    in_part = jnp.einsum("rcf,rch->fh", whole_x, hidden_grad, preferred_element_type=jnp.float32)
    out_part = jnp.einsum("rch,rcf->hf", active, embed_whole, preferred_element_type=jnp.float32)
    width = bilinear_part.shape[1]
    loss_row = jnp.broadcast_to(loss_sum, (1, width))
    shared = butterfly_sum(jnp.concatenate([bilinear_part, loss_row], 0), "mlp")
    packed = jnp.concatenate(
        [in_part.reshape(-1, width), out_part.reshape(-1, width), shared], 0
    )
    packed = butterfly_sum(packed, "tile")
    in_rows = in_part.size // width
    out_rows = out_part.size // width
    grad_in = packed[:in_rows].reshape(in_part.shape)
    grad_out = packed[in_rows : in_rows + out_rows].reshape(out_part.shape)
    grad_bilinear = packed[in_rows + out_rows : in_rows + out_rows + width]
    loss_total = packed[in_rows + out_rows + width, 0]
    pair_loss = loss_total / (2.0 * tile_count * site_rows * 27 * site_rows)
    return (pair_loss, grad_in, grad_out, grad_bilinear)


def solution(mesh):
    placed = (P("tile", "mlp", None, None, None), P(None, "mlp"), P("mlp", None), P(), P(), P())
    return jax.shard_map(
        local,
        mesh=mesh,
        in_specs=placed,
        out_specs=(P(), P(None, "mlp"), P("mlp", None), P()),
        check_vma=False,
    )
```

```python
import functools

import jax
import jax.numpy as jnp
from jax import lax
from jax.experimental import pallas as pl
from jax.experimental.pallas import tpu as pltpu
from jax.sharding import PartitionSpec as P

column_plan = ((-1, 1), (0, 0), (0, 1), (1, 0))


def shifted(array, axis, by):
    peers = lax.axis_size(axis)
    pairs = [(i, i + by) for i in range(peers) if 0 <= i + by < peers]
    return lax.ppermute(array, axis, pairs)


def butterfly_sum(x, axis):
    peers = lax.axis_size(axis)
    step = 1
    while step < peers:
        x = x + lax.ppermute(x, axis, [(i, i ^ step) for i in range(peers)])
        step *= 2
    return x


def butterfly_gather(x, axis):
    peers = lax.axis_size(axis)
    me = lax.axis_index(axis)
    step = 1
    while step < peers:
        other = lax.ppermute(x, axis, [(i, i ^ step) for i in range(peers)])
        low = (me & step) == 0
        x = jnp.where(low, jnp.concatenate([x, other], 0), jnp.concatenate([other, x], 0))
        step *= 2
    return x


def butterfly_scatter(x, axis):
    peers = lax.axis_size(axis)
    me = lax.axis_index(axis)
    step = peers // 2
    while step >= 1:
        half = x.shape[0] // 2
        upper = (me & step) != 0
        send = jnp.where(upper, x[:half], x[half:])
        keep = jnp.where(upper, x[half:], x[:half])
        x = keep + lax.ppermute(send, axis, [(i, i ^ step) for i in range(peers)])
        step //= 2
    return x


MESH = pl.DeviceIdType.MESH


def flip(index, bit):
    return index + bit - 2 * bit * ((index // bit) % 2)


def reduce_kernel(plan, x_ref, o_ref, recv, send_sem, recv_sem):
    coords = {axis: lax.axis_index(axis) for axis in ("tile", "mlp")}
    barrier = pltpu.get_barrier_semaphore()
    for axis, bit, rows in plan:
        pl.semaphore_signal(
            barrier, inc=1, device_id={axis: flip(coords[axis], bit)}, device_id_type=MESH
        )
    pl.semaphore_wait(barrier, len(plan))
    o_ref[...] = x_ref[...]
    for step, (axis, bit, rows) in enumerate(plan):
        part = pl.ds(0, rows)
        copy = pltpu.make_async_remote_copy(
            src_ref=o_ref.at[part],
            dst_ref=recv.at[step, part],
            send_sem=send_sem.at[step],
            recv_sem=recv_sem.at[step],
            device_id={axis: flip(coords[axis], bit)},
            device_id_type=MESH,
        )
        copy.start()
        copy.wait()
        o_ref[part] = o_ref[part] + recv[step, part]


def all_reduce(packed, shared_rows):
    plan = []
    for axis, rows in (("mlp", shared_rows), ("tile", packed.shape[0])):
        bit = 1
        while bit < lax.axis_size(axis):
            plan.append((axis, bit, rows))
            bit *= 2
    return pl.pallas_call(
        functools.partial(reduce_kernel, tuple(plan)),
        out_shape=jax.ShapeDtypeStruct(packed.shape, packed.dtype),
        in_specs=[pl.BlockSpec(memory_space=pltpu.VMEM)],
        out_specs=pl.BlockSpec(memory_space=pltpu.VMEM),
        scratch_shapes=[
            pltpu.VMEM((len(plan),) + packed.shape, packed.dtype),
            pltpu.SemaphoreType.DMA((len(plan),)),
            pltpu.SemaphoreType.DMA((len(plan),)),
        ],
        compiler_params=pltpu.CompilerParams(collective_id=0, has_side_effects=True),
    )(packed)


def pair_slope(raw_score, target, weight, heavy_weight, factor):
    chance = jax.nn.sigmoid(raw_score)
    signed = (1.0 - target) * chance - heavy_weight * target * (1.0 - chance)
    return (weight * signed * factor).astype(jnp.bfloat16)


def pair_cost(raw_score, target, weight, heavy_weight):
    missed = heavy_weight * target * jnp.log1p(jnp.exp(-raw_score))
    spurious = (1.0 - target) * jnp.log1p(jnp.exp(raw_score))
    return jnp.sum(weight * (missed + spurious))


def local(features, w_in, w_out, bilinear, partner, counts):
    row_part = features.shape[1]
    feature_width = features.shape[4]
    groups = lax.axis_size("mlp")
    site_rows = row_part * groups
    tile_count = lax.axis_size("tile")
    grid_depth = tile_count // 8
    tile_here = lax.axis_index("tile")
    member = lax.axis_index("mlp")
    block_x = tile_here // (4 * grid_depth)
    block_y = tile_here // grid_depth % 4
    block_z = tile_here % grid_depth
    heavy_weight = 27 * site_rows // 4
    score_scale = feature_width ** (-0.5)
    factor = score_scale / (2 * tile_count * site_rows)
    own_rows = member * row_part + jnp.arange(row_part, dtype=jnp.int32)
    all_rows = jnp.arange(site_rows, dtype=jnp.int32)
    mine_counts = lax.dynamic_index_in_dim(counts, tile_here, 0, keepdims=False)
    mine_partner = lax.dynamic_index_in_dim(partner, tile_here, 0, keepdims=False)
    own_partner = lax.dynamic_slice_in_dim(mine_partner, member * row_part, row_part, 1)
    own_pre_ok = own_rows[None, :] < mine_counts[:, 0:1]
    own_post_ok = own_rows[None, :] < mine_counts[:, 1:2]
    local_x = features.reshape(row_part, 4, feature_width)
    whole_x = butterfly_gather(local_x, "mlp")
    hidden_pre = jnp.einsum("rcf,fh->rch", whole_x, w_in, preferred_element_type=jnp.float32)
    active = jax.nn.gelu(hidden_pre).astype(jnp.bfloat16)
    mixed_rows = butterfly_scatter(
        jnp.einsum("rch,hf->rcf", active, w_out, preferred_element_type=jnp.float32), "mlp"
    )
    embedded = (local_x.astype(jnp.float32) + mixed_rows).astype(jnp.bfloat16)
    pre_local = embedded[:, 0::2]
    post_local = embedded[:, 1::2]
    query_local = jnp.einsum(
        "ruf,fg->rug", pre_local, bilinear, preferred_element_type=jnp.float32
    ).astype(jnp.bfloat16)

    def pair_code(step_x, step_y, step_z):
        return ((step_x + 1) * 9 + (step_y + 1) * 3 + step_z + 1) * site_rows

    loss_sum = jnp.zeros((), jnp.float32)
    post_grads = [
        jnp.zeros((row_part, feature_width), jnp.float32),
        jnp.zeros((row_part, feature_width), jnp.float32),
    ]
    post_whole, query_whole = (
        butterfly_gather(post_local, "mlp"),
        butterfly_gather(query_local, "mlp"),
    )
    query_grads = [
        jnp.zeros((row_part, feature_width), jnp.float32),
        jnp.zeros((row_part, feature_width), jnp.float32),
    ]
    for step_y in (-1, 0, 1):
        for step_z in (-1, 0, 1):
            post_cols, query_cols, post_valid, pre_valid, label_cols = ([], [], [], [], [])
            for position in range(4):
                shift_x, sub_tile = column_plan[position]
                offset = shift_x * 4 * grid_depth + step_y * grid_depth + step_z
                inside = (
                    (block_x + shift_x >= 0)
                    & (block_x + shift_x < 2)
                    & (block_y + step_y >= 0)
                    & (block_y + step_y < 4)
                    & (block_z + step_z >= 0)
                    & (block_z + step_z < grid_depth)
                )
                source = jnp.clip(tile_here + offset, 0, tile_count - 1)
                tile_counts = lax.dynamic_index_in_dim(counts, source, 0, keepdims=False)[sub_tile]
                labels = lax.dynamic_index_in_dim(partner, source, 0, keepdims=False)[sub_tile]
                offset, sub_tile, inside, tile_counts, labels = (
                    offset,
                    sub_tile,
                    inside,
                    tile_counts,
                    labels,
                )
                both_sides = jnp.stack([post_whole[:, sub_tile], query_whole[:, sub_tile]], 0)
                if offset != 0:
                    both_sides = shifted(both_sides, "tile", -offset)
                post_cols.append(both_sides[0])
                query_cols.append(both_sides[1])
                post_valid.append(inside & (all_rows < tile_counts[1]))
                pre_valid.append(inside & (all_rows < tile_counts[0]))
                label_cols.append(labels)
            for pretile in (0, 1):
                chosen = range(pretile, pretile + 3)
                others = jnp.concatenate([post_cols[column_id] for column_id in chosen], 0)
                col_key = jnp.concatenate(
                    [
                        pair_code(column_id - 1 - pretile, step_y, step_z) + all_rows
                        for column_id in chosen
                    ]
                )
                col_ok = jnp.concatenate([post_valid[column_id] for column_id in chosen])
                raw_score = (
                    jnp.einsum(
                        "rf,cf->rc",
                        query_local[:, pretile],
                        others,
                        preferred_element_type=jnp.float32,
                    )
                    * score_scale
                )
                target = (own_partner[pretile][:, None] == col_key[None, :]).astype(jnp.float32)
                weight = (own_pre_ok[pretile][:, None] & col_ok[None, :]).astype(jnp.float32)
                loss_sum = loss_sum + pair_cost(raw_score, target, weight, heavy_weight)
                slope = pair_slope(raw_score, target, weight, heavy_weight, factor)
                query_grads[pretile] = query_grads[pretile] + jnp.dot(
                    slope, others, preferred_element_type=jnp.float32
                )
                senders = jnp.concatenate([query_cols[column_id] for column_id in chosen], 0)
                row_key = jnp.concatenate(
                    [
                        label_cols[column_id] - pair_code(pretile - column_id + 1, -step_y, -step_z)
                        for column_id in chosen
                    ]
                )
                row_ok = jnp.concatenate([pre_valid[column_id] for column_id in chosen])
                back_score = (
                    jnp.einsum(
                        "cf,rf->cr",
                        post_local[:, pretile],
                        senders,
                        preferred_element_type=jnp.float32,
                    )
                    * score_scale
                )
                back_target = (own_rows[:, None] == row_key[None, :]).astype(jnp.float32)
                back_weight = (own_post_ok[pretile][:, None] & row_ok[None, :]).astype(jnp.float32)
                back_slope = pair_slope(back_score, back_target, back_weight, heavy_weight, factor)
                post_grads[pretile] = post_grads[pretile] + jnp.dot(
                    back_slope, senders, preferred_element_type=jnp.float32
                )
    query_total = jnp.stack(query_grads, 1)
    query_back = query_total.astype(jnp.bfloat16)
    post_back = jnp.stack(post_grads, 1)
    bilinear_part = jnp.einsum(
        "ruf,rug->fg", pre_local, query_back, preferred_element_type=jnp.float32
    )
    pre_back = jnp.einsum("rug,fg->ruf", query_back, bilinear, preferred_element_type=jnp.float32)
    embed_grad = jnp.stack(
        [pre_back[:, 0], post_back[:, 0], pre_back[:, 1], post_back[:, 1]], 1
    ).astype(jnp.bfloat16)
    embed_whole = butterfly_gather(embed_grad, "mlp")
    active_grad = jnp.einsum("rcf,hf->rch", embed_whole, w_out, preferred_element_type=jnp.float32)
    unused, pullback = jax.vjp(jax.nn.gelu, hidden_pre)
    hidden_grad = pullback(active_grad)[0].astype(jnp.bfloat16)
    in_part = jnp.einsum("rcf,rch->fh", whole_x, hidden_grad, preferred_element_type=jnp.float32)
    out_part = jnp.einsum("rch,rcf->hf", active, embed_whole, preferred_element_type=jnp.float32)
    width = bilinear_part.shape[1]
    loss_rows = jnp.zeros((8, width), jnp.float32).at[0, 0].set(loss_sum)
    in_rows = in_part.size // width
    out_rows = out_part.size // width
    packed = all_reduce(
        jnp.concatenate(
            [bilinear_part, loss_rows, in_part.reshape(-1, width), out_part.reshape(-1, width)], 0
        ),
        width + 8,
    )
    grad_bilinear = packed[:width]
    loss_total = packed[width, 0]
    grad_in = packed[width + 8 : width + 8 + in_rows].reshape(in_part.shape)
    grad_out = packed[width + 8 + in_rows : width + 8 + in_rows + out_rows].reshape(out_part.shape)
    pair_loss = loss_total / (2.0 * tile_count * site_rows * 27 * site_rows)
    return (pair_loss, grad_in, grad_out, grad_bilinear)


def solution(mesh):
    placed = (P("tile", "mlp", None, None, None), P(None, "mlp"), P("mlp", None), P(), P(), P())
    return jax.shard_map(
        local,
        mesh=mesh,
        in_specs=placed,
        out_specs=(P(), P(None, "mlp"), P("mlp", None), P()),
        check_vma=False,
    )
```

```python
import functools

import jax
import jax.numpy as jnp
from jax import lax
from jax.experimental import pallas as pl
from jax.experimental.pallas import tpu as pltpu
from jax.sharding import PartitionSpec as P

column_plan = ((-1, 1), (0, 0), (0, 1), (1, 0))


def shifted(array, axis, by):
    peers = lax.axis_size(axis)
    pairs = [(i, i + by) for i in range(peers) if 0 <= i + by < peers]
    return lax.ppermute(array, axis, pairs)


def butterfly_sum(x, axis):
    peers = lax.axis_size(axis)
    step = 1
    while step < peers:
        x = x + lax.ppermute(x, axis, [(i, i ^ step) for i in range(peers)])
        step *= 2
    return x


def butterfly_gather(x, axis):
    peers = lax.axis_size(axis)
    me = lax.axis_index(axis)
    step = 1
    while step < peers:
        other = lax.ppermute(x, axis, [(i, i ^ step) for i in range(peers)])
        low = (me & step) == 0
        x = jnp.where(low, jnp.concatenate([x, other], 0), jnp.concatenate([other, x], 0))
        step *= 2
    return x


def butterfly_scatter(x, axis):
    peers = lax.axis_size(axis)
    me = lax.axis_index(axis)
    step = peers // 2
    while step >= 1:
        half = x.shape[0] // 2
        upper = (me & step) != 0
        send = jnp.where(upper, x[:half], x[half:])
        keep = jnp.where(upper, x[half:], x[:half])
        x = keep + lax.ppermute(send, axis, [(i, i ^ step) for i in range(peers)])
        step //= 2
    return x


MESH = pl.DeviceIdType.MESH


def flip(index, bit):
    return index + bit - 2 * bit * ((index // bit) % 2)


def reduce_kernel(plan, x_ref, o_ref, recv, send_sem, recv_sem):
    coords = {axis: lax.axis_index(axis) for axis in ("tile", "mlp")}
    barrier = pltpu.get_barrier_semaphore()
    for axis, bit, rows in plan:
        pl.semaphore_signal(
            barrier, inc=1, device_id={axis: flip(coords[axis], bit)}, device_id_type=MESH
        )
    pl.semaphore_wait(barrier, len(plan))
    o_ref[...] = x_ref[...]
    for step, (axis, bit, rows) in enumerate(plan):
        part = pl.ds(0, rows)
        copy = pltpu.make_async_remote_copy(
            src_ref=o_ref.at[part],
            dst_ref=recv.at[step, part],
            send_sem=send_sem.at[step],
            recv_sem=recv_sem.at[step],
            device_id={axis: flip(coords[axis], bit)},
            device_id_type=MESH,
        )
        copy.start()
        copy.wait()
        o_ref[part] = o_ref[part] + recv[step, part]


def all_reduce(packed, shared_rows):
    plan = []
    for axis, rows in (("mlp", shared_rows), ("tile", packed.shape[0])):
        bit = 1
        while bit < lax.axis_size(axis):
            plan.append((axis, bit, rows))
            bit *= 2
    return pl.pallas_call(
        functools.partial(reduce_kernel, tuple(plan)),
        out_shape=jax.ShapeDtypeStruct(packed.shape, packed.dtype),
        in_specs=[pl.BlockSpec(memory_space=pltpu.VMEM)],
        out_specs=pl.BlockSpec(memory_space=pltpu.VMEM),
        scratch_shapes=[
            pltpu.VMEM((len(plan),) + packed.shape, packed.dtype),
            pltpu.SemaphoreType.DMA((len(plan),)),
            pltpu.SemaphoreType.DMA((len(plan),)),
        ],
        compiler_params=pltpu.CompilerParams(collective_id=0, has_side_effects=True),
    )(packed)


def pair_slope(raw_score, target, weight, heavy_weight, factor):
    chance = jax.nn.sigmoid(raw_score)
    signed = (1.0 - target) * chance - heavy_weight * target * (1.0 - chance)
    return (weight * signed * factor).astype(jnp.bfloat16)


def pair_cost(raw_score, target, weight, heavy_weight):
    missed = heavy_weight * target * jnp.log1p(jnp.exp(-raw_score))
    spurious = (1.0 - target) * jnp.log1p(jnp.exp(raw_score))
    return jnp.sum(weight * (missed + spurious))


def local(features, w_in, w_out, bilinear, partner, counts):
    row_part = features.shape[1]
    feature_width = features.shape[4]
    groups = lax.axis_size("mlp")
    site_rows = row_part * groups
    tile_count = lax.axis_size("tile")
    grid_depth = tile_count // 8
    tile_here = lax.axis_index("tile")
    member = lax.axis_index("mlp")
    block_x = tile_here // (4 * grid_depth)
    block_y = tile_here // grid_depth % 4
    block_z = tile_here % grid_depth
    heavy_weight = 27 * site_rows // 4
    score_scale = feature_width ** (-0.5)
    factor = score_scale / (2 * tile_count * site_rows)
    own_rows = member * row_part + jnp.arange(row_part, dtype=jnp.int32)
    all_rows = jnp.arange(site_rows, dtype=jnp.int32)
    mine_counts = lax.dynamic_index_in_dim(counts, tile_here, 0, keepdims=False)
    mine_partner = lax.dynamic_index_in_dim(partner, tile_here, 0, keepdims=False)
    own_partner = lax.dynamic_slice_in_dim(mine_partner, member * row_part, row_part, 1)
    own_pre_ok = own_rows[None, :] < mine_counts[:, 0:1]
    own_post_ok = own_rows[None, :] < mine_counts[:, 1:2]
    local_x = features.reshape(row_part, 4, feature_width)
    whole_x = butterfly_gather(local_x, "mlp")
    hidden_pre = jnp.einsum("rcf,fh->rch", whole_x, w_in, preferred_element_type=jnp.float32)
    active = jax.nn.gelu(hidden_pre).astype(jnp.bfloat16)
    mixed_rows = butterfly_scatter(
        jnp.einsum("rch,hf->rcf", active, w_out, preferred_element_type=jnp.float32), "mlp"
    )
    embedded = (local_x.astype(jnp.float32) + mixed_rows).astype(jnp.bfloat16)
    pre_local = embedded[:, 0::2]
    post_local = embedded[:, 1::2]
    query_local = jnp.einsum(
        "ruf,fg->rug", pre_local, bilinear, preferred_element_type=jnp.float32
    ).astype(jnp.bfloat16)

    x_stride = 4 * grid_depth
    y_stride = grid_depth
    query_all = butterfly_gather(query_local, "mlp")
    facing = jnp.where(block_x == 0, post_local[:, 1], post_local[:, 0])
    x_pairs = [(s, (s + x_stride) % tile_count) for s in range(tile_count)]
    from_x = lax.ppermute(facing, "tile", x_pairs)
    halo = jnp.stack([from_x, post_local[:, 0], post_local[:, 1]], 0)

    def position(s, stride, extent):
        return (s // stride) % extent

    def along(arr, stride, extent):
        lower = [(s, s + stride) for s in range(tile_count) if position(s, stride, extent) < extent - 1]
        upper = [(s, s - stride) for s in range(tile_count) if position(s, stride, extent) > 0]
        return jnp.stack(
            [lax.ppermute(arr, "tile", lower), arr, lax.ppermute(arr, "tile", upper)], 0
        )

    def along_back(arr, stride, extent):
        lower = [(s, s - stride) for s in range(tile_count) if position(s, stride, extent) > 0]
        upper = [(s, s + stride) for s in range(tile_count) if position(s, stride, extent) < extent - 1]
        return arr[1] + lax.ppermute(arr[0], "tile", lower) + lax.ppermute(arr[2], "tile", upper)

    halo = along(along(halo, y_stride, 4), 1, grid_depth)
    steps = jnp.arange(3, dtype=jnp.int32) - 1
    dz_grid = steps[:, None]
    dy_grid = steps[None, :]
    inside = (
        (block_y + dy_grid >= 0)
        & (block_y + dy_grid < 4)
        & (block_z + dz_grid >= 0)
        & (block_z + dz_grid < grid_depth)
    )
    near = jnp.clip(tile_here + dy_grid * y_stride + dz_grid, 0, tile_count - 1)
    far = (near + x_stride) % tile_count
    col_counts = jnp.stack(
        [counts[far, block_x, 1], counts[near, 0, 1], counts[near, 1, 1]], -1
    )
    j_ok = inside[..., None, None] & (own_rows < col_counts[..., None])
    loss_sum = jnp.zeros((), jnp.float32)
    post_grad_parts = jnp.zeros(halo.shape, jnp.float32)
    query_grads = []
    place = jnp.arange(3, dtype=jnp.int32)
    code_base = (place[None, None, :] * 9 + (dy_grid[..., None] + 1) * 3 + dz_grid[..., None] + 1) * site_rows
    col_key = (code_base[..., None] + own_rows).reshape(-1)
    for pretile, order, edge in ((0, (0, 1, 2), 0), (1, (1, 2, 0), 2)):
        edge_ok = (block_x == 1) if pretile == 0 else (block_x == 0)
        ordered = halo[:, :, order]
        others = ordered.reshape(-1, feature_width)
        x_ok = jnp.stack([edge_ok if p == edge else jnp.bool_(True) for p in range(3)])
        col_ok = (j_ok[:, :, order] & x_ok[None, None, :, None]).reshape(-1)
        queries = query_all[:, pretile]
        raw_score = (
            jnp.einsum("rf,cf->rc", queries, others, preferred_element_type=jnp.float32)
            * score_scale
        )
        row_ok = all_rows < mine_counts[pretile, 0]
        target = (mine_partner[pretile][:, None] == col_key[None, :]).astype(jnp.float32)
        weight = (row_ok[:, None] & col_ok[None, :]).astype(jnp.float32)
        loss_sum = loss_sum + pair_cost(raw_score, target, weight, heavy_weight)
        slope = pair_slope(raw_score, target, weight, heavy_weight, factor)
        query_grads.append(jnp.dot(slope, others, preferred_element_type=jnp.float32))
        back = jnp.einsum("rc,rf->cf", slope, queries, preferred_element_type=jnp.float32)
        back = back.reshape(ordered.shape)
        for p in range(3):
            post_grad_parts = post_grad_parts.at[:, :, order[p]].add(back[:, :, p])
    post_grad_parts = along_back(along_back(post_grad_parts, 1, grid_depth), y_stride, 4)
    back_x = lax.ppermute(post_grad_parts[0], "tile", x_pairs)
    post_back = jnp.stack(
        [
            post_grad_parts[1] + jnp.where(block_x == 1, back_x, 0.0),
            post_grad_parts[2] + jnp.where(block_x == 0, back_x, 0.0),
        ],
        1,
    )
    query_back = butterfly_scatter(jnp.stack(query_grads, 1), "mlp").astype(jnp.bfloat16)
    bilinear_part = jnp.einsum(
        "ruf,rug->fg", pre_local, query_back, preferred_element_type=jnp.float32
    )
    pre_back = jnp.einsum("rug,fg->ruf", query_back, bilinear, preferred_element_type=jnp.float32)
    embed_grad = jnp.stack(
        [pre_back[:, 0], post_back[:, 0], pre_back[:, 1], post_back[:, 1]], 1
    ).astype(jnp.bfloat16)
    embed_whole = butterfly_gather(embed_grad, "mlp")
    active_grad = jnp.einsum("rcf,hf->rch", embed_whole, w_out, preferred_element_type=jnp.float32)
    unused, pullback = jax.vjp(jax.nn.gelu, hidden_pre)
    hidden_grad = pullback(active_grad)[0].astype(jnp.bfloat16)
    in_part = jnp.einsum("rcf,rch->fh", whole_x, hidden_grad, preferred_element_type=jnp.float32)
    out_part = jnp.einsum("rch,rcf->hf", active, embed_whole, preferred_element_type=jnp.float32)
    width = bilinear_part.shape[1]
    loss_rows = jnp.zeros((8, width), jnp.float32).at[0, 0].set(loss_sum)
    in_rows = in_part.size // width
    out_rows = out_part.size // width
    packed = all_reduce(
        jnp.concatenate(
            [bilinear_part, loss_rows, in_part.reshape(-1, width), out_part.reshape(-1, width)], 0
        ),
        width + 8,
    )
    grad_bilinear = packed[:width]
    loss_total = packed[width, 0]
    grad_in = packed[width + 8 : width + 8 + in_rows].reshape(in_part.shape)
    grad_out = packed[width + 8 + in_rows : width + 8 + in_rows + out_rows].reshape(out_part.shape)
    pair_loss = loss_total / (2.0 * tile_count * site_rows * 27 * site_rows)
    return (pair_loss, grad_in, grad_out, grad_bilinear)


def solution(mesh):
    placed = (P("tile", "mlp", None, None, None), P(None, "mlp"), P("mlp", None), P(), P(), P())
    return jax.shard_map(
        local,
        mesh=mesh,
        in_specs=placed,
        out_specs=(P(), P(None, "mlp"), P("mlp", None), P()),
        check_vma=False,
    )
```

```python
import functools

import jax
import jax.numpy as jnp
from jax import lax
from jax.experimental import pallas as pl
from jax.experimental.pallas import tpu as pltpu
from jax.sharding import PartitionSpec as P

column_plan = ((-1, 1), (0, 0), (0, 1), (1, 0))


def shifted(array, axis, by):
    peers = lax.axis_size(axis)
    pairs = [(i, i + by) for i in range(peers) if 0 <= i + by < peers]
    return lax.ppermute(array, axis, pairs)


def butterfly_sum(x, axis):
    peers = lax.axis_size(axis)
    step = 1
    while step < peers:
        x = x + lax.ppermute(x, axis, [(i, i ^ step) for i in range(peers)])
        step *= 2
    return x


def butterfly_gather(x, axis):
    peers = lax.axis_size(axis)
    me = lax.axis_index(axis)
    step = 1
    while step < peers:
        other = lax.ppermute(x, axis, [(i, i ^ step) for i in range(peers)])
        low = (me & step) == 0
        x = jnp.where(low, jnp.concatenate([x, other], 0), jnp.concatenate([other, x], 0))
        step *= 2
    return x


def butterfly_scatter(x, axis):
    peers = lax.axis_size(axis)
    me = lax.axis_index(axis)
    step = peers // 2
    while step >= 1:
        half = x.shape[0] // 2
        upper = (me & step) != 0
        send = jnp.where(upper, x[:half], x[half:])
        keep = jnp.where(upper, x[half:], x[:half])
        x = keep + lax.ppermute(send, axis, [(i, i ^ step) for i in range(peers)])
        step //= 2
    return x


MESH = pl.DeviceIdType.MESH


def flip(index, bit):
    return index + bit - 2 * bit * ((index // bit) % 2)


def reduce_kernel(plan, x_ref, o_ref, recv, send_sem, recv_sem):
    coords = {axis: lax.axis_index(axis) for axis in ("tile", "mlp")}
    barrier = pltpu.get_barrier_semaphore()
    partners = [(axis, bit) for axis, bits, rows in plan for bit in bits]
    for axis, bit in partners:
        pl.semaphore_signal(
            barrier, inc=1, device_id={axis: flip(coords[axis], bit)}, device_id_type=MESH
        )
    pl.semaphore_wait(barrier, len(partners))
    o_ref[...] = x_ref[...]
    slot = 0

    def exchange(slot, axis, bit, src_start, length):
        copy = pltpu.make_async_remote_copy(
            src_ref=o_ref.at[pl.ds(pl.multiple_of(src_start, 8), length)],
            dst_ref=recv.at[slot, pl.ds(0, length)],
            send_sem=send_sem.at[slot],
            recv_sem=recv_sem.at[slot],
            device_id={axis: flip(coords[axis], bit)},
            device_id_type=MESH,
        )
        copy.start()
        copy.wait()
        return recv[slot, pl.ds(0, length)]

    for axis, bits, rows in plan:
        start = 0
        length = rows
        for bit in bits:
            length //= 2
            upper = (coords[axis] // bit) % 2
            keep = start + upper * length
            got = exchange(slot, axis, bit, start + (1 - upper) * length, length)
            part = pl.ds(pl.multiple_of(keep, 8), length)
            o_ref[part] = o_ref[part] + got
            start = keep
            slot += 1
        for bit in reversed(bits):
            upper = (coords[axis] // bit) % 2
            sibling = start + (1 - 2 * upper) * length
            got = exchange(slot, axis, bit, start, length)
            o_ref[pl.ds(pl.multiple_of(sibling, 8), length)] = got
            start = start - upper * length
            length *= 2
            slot += 1


def all_reduce(packed, shared_rows):
    plan = (
        ("tile", (1, 2, 16, 4, 8), packed.shape[0]),
        ("mlp", (2, 1, 4), shared_rows),
    )
    steps = sum(2 * len(bits) for axis, bits, rows in plan)
    return pl.pallas_call(
        functools.partial(reduce_kernel, plan),
        out_shape=jax.ShapeDtypeStruct(packed.shape, packed.dtype),
        in_specs=[pl.BlockSpec(memory_space=pltpu.VMEM)],
        out_specs=pl.BlockSpec(memory_space=pltpu.VMEM),
        scratch_shapes=[
            pltpu.VMEM((steps, packed.shape[0] // 2) + packed.shape[1:], packed.dtype),
            pltpu.SemaphoreType.DMA((steps,)),
            pltpu.SemaphoreType.DMA((steps,)),
        ],
        compiler_params=pltpu.CompilerParams(collective_id=0, has_side_effects=True),
    )(packed)

def pair_slope(raw_score, target, weight, heavy_weight, factor):
    chance = jax.nn.sigmoid(raw_score)
    signed = (1.0 - target) * chance - heavy_weight * target * (1.0 - chance)
    return (weight * signed * factor).astype(jnp.bfloat16)


def pair_cost(raw_score, target, weight, heavy_weight):
    missed = heavy_weight * target * jnp.log1p(jnp.exp(-raw_score))
    spurious = (1.0 - target) * jnp.log1p(jnp.exp(raw_score))
    return jnp.sum(weight * (missed + spurious))


def local(features, w_in, w_out, bilinear, partner, counts):
    row_part = features.shape[1]
    feature_width = features.shape[4]
    groups = lax.axis_size("mlp")
    site_rows = row_part * groups
    tile_count = lax.axis_size("tile")
    grid_depth = tile_count // 8
    tile_here = lax.axis_index("tile")
    member = lax.axis_index("mlp")
    block_x = tile_here // (4 * grid_depth)
    block_y = tile_here // grid_depth % 4
    block_z = tile_here % grid_depth
    heavy_weight = 27 * site_rows // 4
    score_scale = feature_width ** (-0.5)
    factor = score_scale / (2 * tile_count * site_rows)
    own_rows = member * row_part + jnp.arange(row_part, dtype=jnp.int32)
    all_rows = jnp.arange(site_rows, dtype=jnp.int32)
    mine_counts = lax.dynamic_index_in_dim(counts, tile_here, 0, keepdims=False)
    mine_partner = lax.dynamic_index_in_dim(partner, tile_here, 0, keepdims=False)
    own_partner = lax.dynamic_slice_in_dim(mine_partner, member * row_part, row_part, 1)
    own_pre_ok = own_rows[None, :] < mine_counts[:, 0:1]
    own_post_ok = own_rows[None, :] < mine_counts[:, 1:2]
    local_x = features.reshape(row_part, 4, feature_width)
    whole_x = butterfly_gather(local_x, "mlp")
    hidden_pre = jnp.einsum("rcf,fh->rch", whole_x, w_in, preferred_element_type=jnp.float32)
    active = jax.nn.gelu(hidden_pre).astype(jnp.bfloat16)
    mixed_rows = butterfly_scatter(
        jnp.einsum("rch,hf->rcf", active, w_out, preferred_element_type=jnp.float32), "mlp"
    )
    embedded = (local_x.astype(jnp.float32) + mixed_rows).astype(jnp.bfloat16)
    pre_local = embedded[:, 0::2]
    post_local = embedded[:, 1::2]
    query_local = jnp.einsum(
        "ruf,fg->rug", pre_local, bilinear, preferred_element_type=jnp.float32
    ).astype(jnp.bfloat16)

    x_stride = 4 * grid_depth
    y_stride = grid_depth
    query_all = butterfly_gather(query_local, "mlp")
    facing = jnp.where(block_x == 0, post_local[:, 1], post_local[:, 0])
    x_pairs = [(s, (s + x_stride) % tile_count) for s in range(tile_count)]
    from_x = lax.ppermute(facing, "tile", x_pairs)
    halo = jnp.stack([from_x, post_local[:, 0], post_local[:, 1]], 0)

    def position(s, stride, extent):
        return (s // stride) % extent

    def along(arr, stride, extent):
        lower = [(s, s + stride) for s in range(tile_count) if position(s, stride, extent) < extent - 1]
        upper = [(s, s - stride) for s in range(tile_count) if position(s, stride, extent) > 0]
        return jnp.stack(
            [lax.ppermute(arr, "tile", lower), arr, lax.ppermute(arr, "tile", upper)], 0
        )

    def along_back(arr, stride, extent):
        lower = [(s, s - stride) for s in range(tile_count) if position(s, stride, extent) > 0]
        upper = [(s, s + stride) for s in range(tile_count) if position(s, stride, extent) < extent - 1]
        return arr[1] + lax.ppermute(arr[0], "tile", lower) + lax.ppermute(arr[2], "tile", upper)

    halo = along(along(halo, y_stride, 4), 1, grid_depth)
    steps = jnp.arange(3, dtype=jnp.int32) - 1
    dz_grid = steps[:, None]
    dy_grid = steps[None, :]
    inside = (
        (block_y + dy_grid >= 0)
        & (block_y + dy_grid < 4)
        & (block_z + dz_grid >= 0)
        & (block_z + dz_grid < grid_depth)
    )
    near = jnp.clip(tile_here + dy_grid * y_stride + dz_grid, 0, tile_count - 1)
    far = (near + x_stride) % tile_count
    col_counts = jnp.stack(
        [counts[far, block_x, 1], counts[near, 0, 1], counts[near, 1, 1]], -1
    )
    j_ok = inside[..., None, None] & (own_rows < col_counts[..., None])
    loss_sum = jnp.zeros((), jnp.float32)
    post_grad_parts = jnp.zeros(halo.shape, jnp.float32)
    query_grads = []
    place = jnp.arange(3, dtype=jnp.int32)
    code_base = (place[None, None, :] * 9 + (dy_grid[..., None] + 1) * 3 + dz_grid[..., None] + 1) * site_rows
    col_key = (code_base[..., None] + own_rows).reshape(-1)
    for pretile, order, edge in ((0, (0, 1, 2), 0), (1, (1, 2, 0), 2)):
        edge_ok = (block_x == 1) if pretile == 0 else (block_x == 0)
        ordered = halo[:, :, order]
        others = ordered.reshape(-1, feature_width)
        x_ok = jnp.stack([edge_ok if p == edge else jnp.bool_(True) for p in range(3)])
        col_ok = (j_ok[:, :, order] & x_ok[None, None, :, None]).reshape(-1)
        queries = query_all[:, pretile]
        raw_score = (
            jnp.einsum("rf,cf->rc", queries, others, preferred_element_type=jnp.float32)
            * score_scale
        )
        row_ok = all_rows < mine_counts[pretile, 0]
        target = (mine_partner[pretile][:, None] == col_key[None, :]).astype(jnp.float32)
        weight = (row_ok[:, None] & col_ok[None, :]).astype(jnp.float32)
        loss_sum = loss_sum + pair_cost(raw_score, target, weight, heavy_weight)
        slope = pair_slope(raw_score, target, weight, heavy_weight, factor)
        query_grads.append(jnp.dot(slope, others, preferred_element_type=jnp.float32))
        back = jnp.einsum("rc,rf->cf", slope, queries, preferred_element_type=jnp.float32)
        back = back.reshape(ordered.shape)
        for p in range(3):
            post_grad_parts = post_grad_parts.at[:, :, order[p]].add(back[:, :, p])
    post_grad_parts = along_back(along_back(post_grad_parts, 1, grid_depth), y_stride, 4)
    back_x = lax.ppermute(post_grad_parts[0], "tile", x_pairs)
    post_back = jnp.stack(
        [
            post_grad_parts[1] + jnp.where(block_x == 1, back_x, 0.0),
            post_grad_parts[2] + jnp.where(block_x == 0, back_x, 0.0),
        ],
        1,
    )
    query_back = butterfly_scatter(jnp.stack(query_grads, 1), "mlp").astype(jnp.bfloat16)
    bilinear_part = jnp.einsum(
        "ruf,rug->fg", pre_local, query_back, preferred_element_type=jnp.float32
    )
    pre_back = jnp.einsum("rug,fg->ruf", query_back, bilinear, preferred_element_type=jnp.float32)
    embed_grad = jnp.stack(
        [pre_back[:, 0], post_back[:, 0], pre_back[:, 1], post_back[:, 1]], 1
    ).astype(jnp.bfloat16)
    embed_whole = butterfly_gather(embed_grad, "mlp")
    active_grad = jnp.einsum("rcf,hf->rch", embed_whole, w_out, preferred_element_type=jnp.float32)
    unused, pullback = jax.vjp(jax.nn.gelu, hidden_pre)
    hidden_grad = pullback(active_grad)[0].astype(jnp.bfloat16)
    in_part = jnp.einsum("rcf,rch->fh", whole_x, hidden_grad, preferred_element_type=jnp.float32)
    out_part = jnp.einsum("rch,rcf->hf", active, embed_whole, preferred_element_type=jnp.float32)
    width = bilinear_part.shape[1]
    in_rows = in_part.size // width
    out_rows = out_part.size // width
    shared_rows = 320
    total_rows = 768
    loss_rows = jnp.zeros((shared_rows - width, width), jnp.float32).at[0, 0].set(loss_sum)
    pad_rows = jnp.zeros((total_rows - shared_rows - in_rows - out_rows, width), jnp.float32)
    packed = all_reduce(
        jnp.concatenate(
            [bilinear_part, loss_rows, in_part.reshape(-1, width), out_part.reshape(-1, width), pad_rows], 0
        ),
        shared_rows,
    )
    grad_bilinear = packed[:width]
    loss_total = packed[width, 0]
    grad_in = packed[shared_rows : shared_rows + in_rows].reshape(in_part.shape)
    grad_out = packed[shared_rows + in_rows : shared_rows + in_rows + out_rows].reshape(out_part.shape)
    pair_loss = loss_total / (2.0 * tile_count * site_rows * 27 * site_rows)
    return (pair_loss, grad_in, grad_out, grad_bilinear)


def solution(mesh):
    placed = (P("tile", "mlp", None, None, None), P(None, "mlp"), P("mlp", None), P(), P(), P())
    return jax.shard_map(
        local,
        mesh=mesh,
        in_specs=placed,
        out_specs=(P(), P(None, "mlp"), P("mlp", None), P()),
        check_vma=False,
    )
```

```python
import functools

import jax
import jax.numpy as jnp
from jax import lax
from jax.experimental import pallas as pl
from jax.experimental.pallas import tpu as pltpu
from jax.sharding import PartitionSpec as P

column_plan = ((-1, 1), (0, 0), (0, 1), (1, 0))


def shifted(array, axis, by):
    peers = lax.axis_size(axis)
    pairs = [(i, i + by) for i in range(peers) if 0 <= i + by < peers]
    return lax.ppermute(array, axis, pairs)


def butterfly_sum(x, axis):
    peers = lax.axis_size(axis)
    step = 1
    while step < peers:
        x = x + lax.ppermute(x, axis, [(i, i ^ step) for i in range(peers)])
        step *= 2
    return x


def butterfly_gather(x, axis):
    peers = lax.axis_size(axis)
    me = lax.axis_index(axis)
    step = 1
    while step < peers:
        other = lax.ppermute(x, axis, [(i, i ^ step) for i in range(peers)])
        low = (me & step) == 0
        x = jnp.where(low, jnp.concatenate([x, other], 0), jnp.concatenate([other, x], 0))
        step *= 2
    return x


def butterfly_scatter(x, axis):
    peers = lax.axis_size(axis)
    me = lax.axis_index(axis)
    step = peers // 2
    while step >= 1:
        half = x.shape[0] // 2
        upper = (me & step) != 0
        send = jnp.where(upper, x[:half], x[half:])
        keep = jnp.where(upper, x[half:], x[:half])
        x = keep + lax.ppermute(send, axis, [(i, i ^ step) for i in range(peers)])
        step //= 2
    return x


MESH = pl.DeviceIdType.MESH


def flip(index, bit):
    return index + bit - 2 * bit * ((index // bit) % 2)


def reduce_kernel(plan, x_ref, o_ref, recv, send_sem, recv_sem):
    coords = {axis: lax.axis_index(axis) for axis in ("tile", "mlp")}
    barrier = pltpu.get_barrier_semaphore()
    partners = [(axis, bit) for axis, bits, rows in plan for bit in bits]
    for axis, bit in partners:
        pl.semaphore_signal(
            barrier, inc=1, device_id={axis: flip(coords[axis], bit)}, device_id_type=MESH
        )
    pl.semaphore_wait(barrier, len(partners))
    o_ref[...] = x_ref[...]
    slot = 0

    def exchange(slot, axis, bit, src_start, length):
        copy = pltpu.make_async_remote_copy(
            src_ref=o_ref.at[pl.ds(pl.multiple_of(src_start, 8), length)],
            dst_ref=recv.at[slot, pl.ds(0, length)],
            send_sem=send_sem.at[slot],
            recv_sem=recv_sem.at[slot],
            device_id={axis: flip(coords[axis], bit)},
            device_id_type=MESH,
        )
        copy.start()
        copy.wait()
        return recv[slot, pl.ds(0, length)]

    for axis, bits, rows in plan:
        start = 0
        length = rows
        for bit in bits:
            length //= 2
            upper = (coords[axis] // bit) % 2
            keep = start + upper * length
            got = exchange(slot, axis, bit, start + (1 - upper) * length, length)
            part = pl.ds(pl.multiple_of(keep, 8), length)
            o_ref[part] = o_ref[part] + got
            start = keep
            slot += 1
        for bit in reversed(bits):
            upper = (coords[axis] // bit) % 2
            sibling = start + (1 - 2 * upper) * length
            got = exchange(slot, axis, bit, start, length)
            o_ref[pl.ds(pl.multiple_of(sibling, 8), length)] = got
            start = start - upper * length
            length *= 2
            slot += 1


def all_reduce(packed, shared_rows):
    plan = (
        ("tile", (1, 2, 16, 4, 8), packed.shape[0]),
        ("mlp", (2, 1, 4), shared_rows),
    )
    steps = sum(2 * len(bits) for axis, bits, rows in plan)
    return pl.pallas_call(
        functools.partial(reduce_kernel, plan),
        out_shape=jax.ShapeDtypeStruct(packed.shape, packed.dtype),
        in_specs=[pl.BlockSpec(memory_space=pltpu.VMEM)],
        out_specs=pl.BlockSpec(memory_space=pltpu.VMEM),
        scratch_shapes=[
            pltpu.VMEM((steps, packed.shape[0] // 2) + packed.shape[1:], packed.dtype),
            pltpu.SemaphoreType.DMA((steps,)),
            pltpu.SemaphoreType.DMA((steps,)),
        ],
        compiler_params=pltpu.CompilerParams(collective_id=0, has_side_effects=True),
    )(packed)

def pair_slope(raw_score, target, weight, heavy_weight, factor):
    chance = jax.nn.sigmoid(raw_score)
    signed = (1.0 - target) * chance - heavy_weight * target * (1.0 - chance)
    return (weight * signed * factor).astype(jnp.bfloat16)


def pair_cost(raw_score, target, weight, heavy_weight):
    missed = heavy_weight * target * jnp.log1p(jnp.exp(-raw_score))
    spurious = (1.0 - target) * jnp.log1p(jnp.exp(raw_score))
    return jnp.sum(weight * (missed + spurious))


def local(features, w_in, w_out, bilinear, partner, counts):
    row_part = features.shape[1]
    feature_width = features.shape[4]
    groups = lax.axis_size("mlp")
    site_rows = row_part * groups
    tile_count = lax.axis_size("tile")
    grid_depth = tile_count // 8
    tile_here = lax.axis_index("tile")
    member = lax.axis_index("mlp")
    block_x = tile_here // (4 * grid_depth)
    block_y = tile_here // grid_depth % 4
    block_z = tile_here % grid_depth
    heavy_weight = 27 * site_rows // 4
    score_scale = feature_width ** (-0.5)
    factor = score_scale / (2 * tile_count * site_rows)
    own_rows = member * row_part + jnp.arange(row_part, dtype=jnp.int32)
    all_rows = jnp.arange(site_rows, dtype=jnp.int32)
    mine_counts = lax.dynamic_index_in_dim(counts, tile_here, 0, keepdims=False)
    mine_partner = lax.dynamic_index_in_dim(partner, tile_here, 0, keepdims=False)
    own_partner = lax.dynamic_slice_in_dim(mine_partner, member * row_part, row_part, 1)
    own_pre_ok = own_rows[None, :] < mine_counts[:, 0:1]
    own_post_ok = own_rows[None, :] < mine_counts[:, 1:2]
    local_x = features.reshape(row_part, 4, feature_width)
    weights = butterfly_gather(jnp.stack([w_in.T, w_out], 1), "mlp")
    own_hidden = jnp.einsum("rcf,hf->rch", local_x, weights[:, 0], preferred_element_type=jnp.float32)
    own_active = jax.nn.gelu(own_hidden).astype(jnp.bfloat16)
    mixed_rows = jnp.einsum("rch,hf->rcf", own_active, weights[:, 1], preferred_element_type=jnp.float32)
    embedded = (local_x.astype(jnp.float32) + mixed_rows).astype(jnp.bfloat16)
    pre_local = embedded[:, 0::2]
    post_local = embedded[:, 1::2]
    query_local = jnp.einsum(
        "ruf,fg->rug", pre_local, bilinear, preferred_element_type=jnp.float32
    ).astype(jnp.bfloat16)

    x_stride = 4 * grid_depth
    y_stride = grid_depth
    query_all = butterfly_gather(query_local, "mlp")
    facing = jnp.where(block_x == 0, post_local[:, 1], post_local[:, 0])
    x_pairs = [(s, (s + x_stride) % tile_count) for s in range(tile_count)]
    from_x = lax.ppermute(facing, "tile", x_pairs)
    halo = jnp.stack([from_x, post_local[:, 0], post_local[:, 1]], 0)

    def position(s, stride, extent):
        return (s // stride) % extent

    def along(arr, stride, extent):
        lower = [(s, s + stride) for s in range(tile_count) if position(s, stride, extent) < extent - 1]
        upper = [(s, s - stride) for s in range(tile_count) if position(s, stride, extent) > 0]
        return jnp.stack(
            [lax.ppermute(arr, "tile", lower), arr, lax.ppermute(arr, "tile", upper)], 0
        )

    def along_back(arr, stride, extent):
        lower = [(s, s - stride) for s in range(tile_count) if position(s, stride, extent) > 0]
        upper = [(s, s + stride) for s in range(tile_count) if position(s, stride, extent) < extent - 1]
        return arr[1] + lax.ppermute(arr[0], "tile", lower) + lax.ppermute(arr[2], "tile", upper)

    halo = along(along(halo, y_stride, 4), 1, grid_depth)
    steps = jnp.arange(3, dtype=jnp.int32) - 1
    dz_grid = steps[:, None]
    dy_grid = steps[None, :]
    inside = (
        (block_y + dy_grid >= 0)
        & (block_y + dy_grid < 4)
        & (block_z + dz_grid >= 0)
        & (block_z + dz_grid < grid_depth)
    )
    near = jnp.clip(tile_here + dy_grid * y_stride + dz_grid, 0, tile_count - 1)
    far = (near + x_stride) % tile_count
    col_counts = jnp.stack(
        [counts[far, block_x, 1], counts[near, 0, 1], counts[near, 1, 1]], -1
    )
    j_ok = inside[..., None, None] & (own_rows < col_counts[..., None])
    loss_sum = jnp.zeros((), jnp.float32)
    post_grad_parts = jnp.zeros(halo.shape, jnp.float32)
    query_grads = []
    place = jnp.arange(3, dtype=jnp.int32)
    code_base = (place[None, None, :] * 9 + (dy_grid[..., None] + 1) * 3 + dz_grid[..., None] + 1) * site_rows
    col_key = (code_base[..., None] + own_rows).reshape(-1)
    for pretile, order, edge in ((0, (0, 1, 2), 0), (1, (1, 2, 0), 2)):
        edge_ok = (block_x == 1) if pretile == 0 else (block_x == 0)
        ordered = halo[:, :, order]
        others = ordered.reshape(-1, feature_width)
        x_ok = jnp.stack([edge_ok if p == edge else jnp.bool_(True) for p in range(3)])
        col_ok = (j_ok[:, :, order] & x_ok[None, None, :, None]).reshape(-1)
        queries = query_all[:, pretile]
        raw_score = (
            jnp.einsum("rf,cf->rc", queries, others, preferred_element_type=jnp.float32)
            * score_scale
        )
        row_ok = all_rows < mine_counts[pretile, 0]
        target = (mine_partner[pretile][:, None] == col_key[None, :]).astype(jnp.float32)
        weight = (row_ok[:, None] & col_ok[None, :]).astype(jnp.float32)
        loss_sum = loss_sum + pair_cost(raw_score, target, weight, heavy_weight)
        slope = pair_slope(raw_score, target, weight, heavy_weight, factor)
        query_grads.append(jnp.dot(slope, others, preferred_element_type=jnp.float32))
        back = jnp.einsum("rc,rf->cf", slope, queries, preferred_element_type=jnp.float32)
        back = back.reshape(ordered.shape)
        for p in range(3):
            post_grad_parts = post_grad_parts.at[:, :, order[p]].add(back[:, :, p])
    post_grad_parts = along_back(along_back(post_grad_parts, 1, grid_depth), y_stride, 4)
    back_x = lax.ppermute(post_grad_parts[0], "tile", x_pairs)
    post_back = jnp.stack(
        [
            post_grad_parts[1] + jnp.where(block_x == 1, back_x, 0.0),
            post_grad_parts[2] + jnp.where(block_x == 0, back_x, 0.0),
        ],
        1,
    )
    query_back = butterfly_scatter(jnp.stack(query_grads, 1), "mlp").astype(jnp.bfloat16)
    bilinear_part = jnp.einsum(
        "ruf,rug->fg", pre_local, query_back, preferred_element_type=jnp.float32
    )
    pre_back = jnp.einsum("rug,fg->ruf", query_back, bilinear, preferred_element_type=jnp.float32)
    embed_grad = jnp.stack(
        [pre_back[:, 0], post_back[:, 0], pre_back[:, 1], post_back[:, 1]], 1
    ).astype(jnp.bfloat16)
    whole_x = butterfly_gather(local_x, "mlp")
    hidden_pre = jnp.einsum("rcf,fh->rch", whole_x, w_in, preferred_element_type=jnp.float32)
    active = jax.nn.gelu(hidden_pre).astype(jnp.bfloat16)
    embed_whole = butterfly_gather(embed_grad, "mlp")
    active_grad = jnp.einsum("rcf,hf->rch", embed_whole, w_out, preferred_element_type=jnp.float32)
    unused, pullback = jax.vjp(jax.nn.gelu, hidden_pre)
    hidden_grad = pullback(active_grad)[0].astype(jnp.bfloat16)
    in_part = jnp.einsum("rcf,rch->fh", whole_x, hidden_grad, preferred_element_type=jnp.float32)
    out_part = jnp.einsum("rch,rcf->hf", active, embed_whole, preferred_element_type=jnp.float32)
    width = bilinear_part.shape[1]
    in_rows = in_part.size // width
    out_rows = out_part.size // width
    shared_rows = 320
    total_rows = 768
    loss_rows = jnp.zeros((shared_rows - width, width), jnp.float32).at[0, 0].set(loss_sum)
    pad_rows = jnp.zeros((total_rows - shared_rows - in_rows - out_rows, width), jnp.float32)
    packed = all_reduce(
        jnp.concatenate(
            [bilinear_part, loss_rows, in_part.reshape(-1, width), out_part.reshape(-1, width), pad_rows], 0
        ),
        shared_rows,
    )
    grad_bilinear = packed[:width]
    loss_total = packed[width, 0]
    grad_in = packed[shared_rows : shared_rows + in_rows].reshape(in_part.shape)
    grad_out = packed[shared_rows + in_rows : shared_rows + in_rows + out_rows].reshape(out_part.shape)
    pair_loss = loss_total / (2.0 * tile_count * site_rows * 27 * site_rows)
    return (pair_loss, grad_in, grad_out, grad_bilinear)


def solution(mesh):
    placed = (P("tile", "mlp", None, None, None), P(None, "mlp"), P("mlp", None), P(), P(), P())
    return jax.shard_map(
        local,
        mesh=mesh,
        in_specs=placed,
        out_specs=(P(), P(None, "mlp"), P("mlp", None), P()),
        check_vma=False,
    )
```

```python
import functools

import jax
import jax.numpy as jnp
from jax import lax
from jax.experimental import pallas as pl
from jax.experimental.pallas import tpu as pltpu
from jax.sharding import PartitionSpec as P

column_plan = ((-1, 1), (0, 0), (0, 1), (1, 0))


def shifted(array, axis, by):
    peers = lax.axis_size(axis)
    pairs = [(i, i + by) for i in range(peers) if 0 <= i + by < peers]
    return lax.ppermute(array, axis, pairs)


def butterfly_sum(x, axis):
    peers = lax.axis_size(axis)
    step = 1
    while step < peers:
        x = x + lax.ppermute(x, axis, [(i, i ^ step) for i in range(peers)])
        step *= 2
    return x


def butterfly_gather(x, axis):
    peers = lax.axis_size(axis)
    me = lax.axis_index(axis)
    step = 1
    while step < peers:
        other = lax.ppermute(x, axis, [(i, i ^ step) for i in range(peers)])
        low = (me & step) == 0
        x = jnp.where(low, jnp.concatenate([x, other], 0), jnp.concatenate([other, x], 0))
        step *= 2
    return x


def butterfly_scatter(x, axis):
    peers = lax.axis_size(axis)
    me = lax.axis_index(axis)
    step = peers // 2
    while step >= 1:
        half = x.shape[0] // 2
        upper = (me & step) != 0
        send = jnp.where(upper, x[:half], x[half:])
        keep = jnp.where(upper, x[half:], x[:half])
        x = keep + lax.ppermute(send, axis, [(i, i ^ step) for i in range(peers)])
        step //= 2
    return x


MESH = pl.DeviceIdType.MESH


def flip(index, bit):
    return index + bit - 2 * bit * ((index // bit) % 2)


def reduce_kernel(plan, x_ref, o_ref, recv, send_sem, recv_sem):
    coords = {axis: lax.axis_index(axis) for axis in ("tile", "mlp")}

    def partner(axis, bits, distance):
        index = coords[axis]
        for place, bit in enumerate(bits):
            if (distance >> place) & 1:
                index = flip(index, bit)
        return index

    def rank(axis, bits, distance=0):
        total = 0
        for place, bit in enumerate(bits):
            own = (coords[axis] // bit) % 2
            if (distance >> place) & 1:
                own = 1 - own
            total = total + own * (1 << place)
        return total

    barrier = pltpu.get_barrier_semaphore()
    greeted = 0
    for axis, groups, rows in plan:
        for bits in groups:
            for distance in range(1, 1 << len(bits)):
                pl.semaphore_signal(
                    barrier, inc=1, device_id={axis: partner(axis, bits, distance)}, device_id_type=MESH
                )
                greeted += 1
    pl.semaphore_wait(barrier, greeted)
    o_ref[...] = x_ref[...]
    slot = 0

    def send_all(axis, bits, slot, sources, length):
        copies = []
        for distance in range(1, 1 << len(bits)):
            copy = pltpu.make_async_remote_copy(
                src_ref=o_ref.at[pl.ds(pl.multiple_of(sources(distance), 8), length)],
                dst_ref=recv.at[slot + distance - 1, pl.ds(0, length)],
                send_sem=send_sem.at[slot + distance - 1],
                recv_sem=recv_sem.at[slot + distance - 1],
                device_id={axis: partner(axis, bits, distance)},
                device_id_type=MESH,
            )
            copy.start()
            copies.append(copy)
        for copy in copies:
            copy.wait()

    for axis, groups, rows in plan:
        start = 0
        length = rows
        for bits in groups:
            fan = 1 << len(bits)
            length //= fan
            send_all(axis, bits, slot, lambda d: start + rank(axis, bits, d) * length, length)
            start = start + rank(axis, bits) * length
            mine = pl.ds(pl.multiple_of(start, 8), length)
            total = o_ref[mine]
            for distance in range(1, fan):
                total = total + recv[slot + distance - 1, pl.ds(0, length)]
            o_ref[mine] = total
            slot += fan - 1
        for bits in reversed(groups):
            fan = 1 << len(bits)
            send_all(axis, bits, slot, lambda d: start, length)
            base = start - rank(axis, bits) * length
            for distance in range(1, fan):
                spot = base + rank(axis, bits, distance) * length
                o_ref[pl.ds(pl.multiple_of(spot, 8), length)] = recv[slot + distance - 1, pl.ds(0, length)]
            start = base
            length *= fan
            slot += fan - 1


def all_reduce(packed, shared_rows):
    plan = (
        ("tile", ((1,), (2,), (16, 4, 8)), packed.shape[0]),
        ("mlp", ((2, 1, 4),), shared_rows),
    )
    steps = sum(2 * ((1 << len(bits)) - 1) for axis, groups, rows in plan for bits in groups)
    return pl.pallas_call(
        functools.partial(reduce_kernel, plan),
        out_shape=jax.ShapeDtypeStruct(packed.shape, packed.dtype),
        in_specs=[pl.BlockSpec(memory_space=pltpu.VMEM)],
        out_specs=pl.BlockSpec(memory_space=pltpu.VMEM),
        scratch_shapes=[
            pltpu.VMEM((steps, packed.shape[0] // 2) + packed.shape[1:], packed.dtype),
            pltpu.SemaphoreType.DMA((steps,)),
            pltpu.SemaphoreType.DMA((steps,)),
        ],
        compiler_params=pltpu.CompilerParams(collective_id=0, has_side_effects=True),
    )(packed)

def pair_slope(raw_score, target, weight, heavy_weight, factor):
    chance = jax.nn.sigmoid(raw_score)
    signed = (1.0 - target) * chance - heavy_weight * target * (1.0 - chance)
    return (weight * signed * factor).astype(jnp.bfloat16)


def pair_cost(raw_score, target, weight, heavy_weight):
    missed = heavy_weight * target * jnp.log1p(jnp.exp(-raw_score))
    spurious = (1.0 - target) * jnp.log1p(jnp.exp(raw_score))
    return jnp.sum(weight * (missed + spurious))


def local(features, w_in, w_out, bilinear, partner, counts):
    row_part = features.shape[1]
    feature_width = features.shape[4]
    groups = lax.axis_size("mlp")
    site_rows = row_part * groups
    tile_count = lax.axis_size("tile")
    grid_depth = tile_count // 8
    tile_here = lax.axis_index("tile")
    member = lax.axis_index("mlp")
    block_x = tile_here // (4 * grid_depth)
    block_y = tile_here // grid_depth % 4
    block_z = tile_here % grid_depth
    heavy_weight = 27 * site_rows // 4
    score_scale = feature_width ** (-0.5)
    factor = score_scale / (2 * tile_count * site_rows)
    own_rows = member * row_part + jnp.arange(row_part, dtype=jnp.int32)
    all_rows = jnp.arange(site_rows, dtype=jnp.int32)
    mine_counts = lax.dynamic_index_in_dim(counts, tile_here, 0, keepdims=False)
    mine_partner = lax.dynamic_index_in_dim(partner, tile_here, 0, keepdims=False)
    own_partner = lax.dynamic_slice_in_dim(mine_partner, member * row_part, row_part, 1)
    own_pre_ok = own_rows[None, :] < mine_counts[:, 0:1]
    own_post_ok = own_rows[None, :] < mine_counts[:, 1:2]
    local_x = features.reshape(row_part, 4, feature_width)
    weights = butterfly_gather(jnp.stack([w_in.T, w_out], 1), "mlp")
    own_hidden = jnp.einsum("rcf,hf->rch", local_x, weights[:, 0], preferred_element_type=jnp.float32)
    own_active = jax.nn.gelu(own_hidden).astype(jnp.bfloat16)
    mixed_rows = jnp.einsum("rch,hf->rcf", own_active, weights[:, 1], preferred_element_type=jnp.float32)
    embedded = (local_x.astype(jnp.float32) + mixed_rows).astype(jnp.bfloat16)
    pre_local = embedded[:, 0::2]
    post_local = embedded[:, 1::2]
    query_local = jnp.einsum(
        "ruf,fg->rug", pre_local, bilinear, preferred_element_type=jnp.float32
    ).astype(jnp.bfloat16)

    x_stride = 4 * grid_depth
    y_stride = grid_depth
    query_all = butterfly_gather(query_local, "mlp")
    facing = jnp.where(block_x == 0, post_local[:, 1], post_local[:, 0])
    x_pairs = [(s, (s + x_stride) % tile_count) for s in range(tile_count)]
    from_x = lax.ppermute(facing, "tile", x_pairs)
    halo = jnp.stack([from_x, post_local[:, 0], post_local[:, 1]], 0)

    def position(s, stride, extent):
        return (s // stride) % extent

    def along(arr, stride, extent):
        lower = [(s, s + stride) for s in range(tile_count) if position(s, stride, extent) < extent - 1]
        upper = [(s, s - stride) for s in range(tile_count) if position(s, stride, extent) > 0]
        return jnp.stack(
            [lax.ppermute(arr, "tile", lower), arr, lax.ppermute(arr, "tile", upper)], 0
        )

    def along_back(arr, stride, extent):
        lower = [(s, s - stride) for s in range(tile_count) if position(s, stride, extent) > 0]
        upper = [(s, s + stride) for s in range(tile_count) if position(s, stride, extent) < extent - 1]
        return arr[1] + lax.ppermute(arr[0], "tile", lower) + lax.ppermute(arr[2], "tile", upper)

    halo = along(along(halo, y_stride, 4), 1, grid_depth)
    steps = jnp.arange(3, dtype=jnp.int32) - 1
    dz_grid = steps[:, None]
    dy_grid = steps[None, :]
    inside = (
        (block_y + dy_grid >= 0)
        & (block_y + dy_grid < 4)
        & (block_z + dz_grid >= 0)
        & (block_z + dz_grid < grid_depth)
    )
    near = jnp.clip(tile_here + dy_grid * y_stride + dz_grid, 0, tile_count - 1)
    far = (near + x_stride) % tile_count
    col_counts = jnp.stack(
        [counts[far, block_x, 1], counts[near, 0, 1], counts[near, 1, 1]], -1
    )
    j_ok = inside[..., None, None] & (own_rows < col_counts[..., None])
    loss_sum = jnp.zeros((), jnp.float32)
    post_grad_parts = jnp.zeros(halo.shape, jnp.float32)
    query_grads = []
    place = jnp.arange(3, dtype=jnp.int32)
    code_base = (place[None, None, :] * 9 + (dy_grid[..., None] + 1) * 3 + dz_grid[..., None] + 1) * site_rows
    col_key = (code_base[..., None] + own_rows).reshape(-1)
    for pretile, order, edge in ((0, (0, 1, 2), 0), (1, (1, 2, 0), 2)):
        edge_ok = (block_x == 1) if pretile == 0 else (block_x == 0)
        ordered = halo[:, :, order]
        others = ordered.reshape(-1, feature_width)
        x_ok = jnp.stack([edge_ok if p == edge else jnp.bool_(True) for p in range(3)])
        col_ok = (j_ok[:, :, order] & x_ok[None, None, :, None]).reshape(-1)
        queries = query_all[:, pretile]
        raw_score = (
            jnp.einsum("rf,cf->rc", queries, others, preferred_element_type=jnp.float32)
            * score_scale
        )
        row_ok = all_rows < mine_counts[pretile, 0]
        target = (mine_partner[pretile][:, None] == col_key[None, :]).astype(jnp.float32)
        weight = (row_ok[:, None] & col_ok[None, :]).astype(jnp.float32)
        loss_sum = loss_sum + pair_cost(raw_score, target, weight, heavy_weight)
        slope = pair_slope(raw_score, target, weight, heavy_weight, factor)
        query_grads.append(jnp.dot(slope, others, preferred_element_type=jnp.float32))
        back = jnp.einsum("rc,rf->cf", slope, queries, preferred_element_type=jnp.float32)
        back = back.reshape(ordered.shape)
        for p in range(3):
            post_grad_parts = post_grad_parts.at[:, :, order[p]].add(back[:, :, p])
    post_grad_parts = along_back(along_back(post_grad_parts, 1, grid_depth), y_stride, 4)
    back_x = lax.ppermute(post_grad_parts[0], "tile", x_pairs)
    post_back = jnp.stack(
        [
            post_grad_parts[1] + jnp.where(block_x == 1, back_x, 0.0),
            post_grad_parts[2] + jnp.where(block_x == 0, back_x, 0.0),
        ],
        1,
    )
    query_back = butterfly_scatter(jnp.stack(query_grads, 1), "mlp").astype(jnp.bfloat16)
    bilinear_part = jnp.einsum(
        "ruf,rug->fg", pre_local, query_back, preferred_element_type=jnp.float32
    )
    pre_back = jnp.einsum("rug,fg->ruf", query_back, bilinear, preferred_element_type=jnp.float32)
    embed_grad = jnp.stack(
        [pre_back[:, 0], post_back[:, 0], pre_back[:, 1], post_back[:, 1]], 1
    ).astype(jnp.bfloat16)
    whole_x = butterfly_gather(local_x, "mlp")
    hidden_pre = jnp.einsum("rcf,fh->rch", whole_x, w_in, preferred_element_type=jnp.float32)
    active = jax.nn.gelu(hidden_pre).astype(jnp.bfloat16)
    embed_whole = butterfly_gather(embed_grad, "mlp")
    active_grad = jnp.einsum("rcf,hf->rch", embed_whole, w_out, preferred_element_type=jnp.float32)
    unused, pullback = jax.vjp(jax.nn.gelu, hidden_pre)
    hidden_grad = pullback(active_grad)[0].astype(jnp.bfloat16)
    in_part = jnp.einsum("rcf,rch->fh", whole_x, hidden_grad, preferred_element_type=jnp.float32)
    out_part = jnp.einsum("rch,rcf->hf", active, embed_whole, preferred_element_type=jnp.float32)
    width = bilinear_part.shape[1]
    in_rows = in_part.size // width
    out_rows = out_part.size // width
    shared_rows = 320
    total_rows = 768
    loss_rows = jnp.zeros((shared_rows - width, width), jnp.float32).at[0, 0].set(loss_sum)
    pad_rows = jnp.zeros((total_rows - shared_rows - in_rows - out_rows, width), jnp.float32)
    packed = all_reduce(
        jnp.concatenate(
            [bilinear_part, loss_rows, in_part.reshape(-1, width), out_part.reshape(-1, width), pad_rows], 0
        ),
        shared_rows,
    )
    grad_bilinear = packed[:width]
    loss_total = packed[width, 0]
    grad_in = packed[shared_rows : shared_rows + in_rows].reshape(in_part.shape)
    grad_out = packed[shared_rows + in_rows : shared_rows + in_rows + out_rows].reshape(out_part.shape)
    pair_loss = loss_total / (2.0 * tile_count * site_rows * 27 * site_rows)
    return (pair_loss, grad_in, grad_out, grad_bilinear)


def solution(mesh):
    placed = (P("tile", "mlp", None, None, None), P(None, "mlp"), P("mlp", None), P(), P(), P())
    return jax.shard_map(
        local,
        mesh=mesh,
        in_specs=placed,
        out_specs=(P(), P(None, "mlp"), P("mlp", None), P()),
        check_vma=False,
    )
```

```python
import functools

import jax
import jax.numpy as jnp
from jax import lax
from jax.experimental import pallas as pl
from jax.experimental.pallas import tpu as pltpu
from jax.sharding import PartitionSpec as P

column_plan = ((-1, 1), (0, 0), (0, 1), (1, 0))


def shifted(array, axis, by):
    peers = lax.axis_size(axis)
    pairs = [(i, i + by) for i in range(peers) if 0 <= i + by < peers]
    return lax.ppermute(array, axis, pairs)


def butterfly_sum(x, axis):
    peers = lax.axis_size(axis)
    step = 1
    while step < peers:
        x = x + lax.ppermute(x, axis, [(i, i ^ step) for i in range(peers)])
        step *= 2
    return x


def butterfly_gather(x, axis):
    peers = lax.axis_size(axis)
    me = lax.axis_index(axis)
    step = 1
    while step < peers:
        other = lax.ppermute(x, axis, [(i, i ^ step) for i in range(peers)])
        low = (me & step) == 0
        x = jnp.where(low, jnp.concatenate([x, other], 0), jnp.concatenate([other, x], 0))
        step *= 2
    return x


def butterfly_scatter(x, axis):
    peers = lax.axis_size(axis)
    me = lax.axis_index(axis)
    step = peers // 2
    while step >= 1:
        half = x.shape[0] // 2
        upper = (me & step) != 0
        send = jnp.where(upper, x[:half], x[half:])
        keep = jnp.where(upper, x[half:], x[:half])
        x = keep + lax.ppermute(send, axis, [(i, i ^ step) for i in range(peers)])
        step //= 2
    return x


MESH = pl.DeviceIdType.MESH


def flip(index, bit):
    return index + bit - 2 * bit * ((index // bit) % 2)


def reduce_kernel(plan, x_ref, o_ref, recv, send_sem, recv_sem):
    coords = {axis: lax.axis_index(axis) for axis in ("tile", "mlp")}

    def partner(axis, bits, distance):
        index = coords[axis]
        for place, bit in enumerate(bits):
            if (distance >> place) & 1:
                index = flip(index, bit)
        return index

    def rank(axis, bits, distance=0):
        total = 0
        for place, bit in enumerate(bits):
            own = (coords[axis] // bit) % 2
            if (distance >> place) & 1:
                own = 1 - own
            total = total + own * (1 << place)
        return total

    barrier = pltpu.get_barrier_semaphore()
    greeted = 0
    for axis, groups, rows in plan:
        for bits in groups:
            for distance in range(1, 1 << len(bits)):
                pl.semaphore_signal(
                    barrier, inc=1, device_id={axis: partner(axis, bits, distance)}, device_id_type=MESH
                )
                greeted += 1
    pl.semaphore_wait(barrier, greeted)
    o_ref[...] = x_ref[...]
    slot = 0

    def send_all(axis, bits, slot, sources, length):
        copies = []
        for distance in range(1, 1 << len(bits)):
            copy = pltpu.make_async_remote_copy(
                src_ref=o_ref.at[pl.ds(pl.multiple_of(sources(distance), 8), length)],
                dst_ref=recv.at[slot + distance - 1, pl.ds(0, length)],
                send_sem=send_sem.at[slot + distance - 1],
                recv_sem=recv_sem.at[slot + distance - 1],
                device_id={axis: partner(axis, bits, distance)},
                device_id_type=MESH,
            )
            copy.start()
            copies.append(copy)
        for copy in copies:
            copy.wait()

    for axis, groups, rows in plan:
        start = 0
        length = rows
        for bits in groups:
            fan = 1 << len(bits)
            length //= fan
            send_all(axis, bits, slot, lambda d: start + rank(axis, bits, d) * length, length)
            start = start + rank(axis, bits) * length
            mine = pl.ds(pl.multiple_of(start, 8), length)
            total = o_ref[mine]
            for distance in range(1, fan):
                total = total + recv[slot + distance - 1, pl.ds(0, length)]
            o_ref[mine] = total
            slot += fan - 1
        for bits in reversed(groups):
            fan = 1 << len(bits)
            send_all(axis, bits, slot, lambda d: start, length)
            base = start - rank(axis, bits) * length
            for distance in range(1, fan):
                spot = base + rank(axis, bits, distance) * length
                o_ref[pl.ds(pl.multiple_of(spot, 8), length)] = recv[slot + distance - 1, pl.ds(0, length)]
            start = base
            length *= fan
            slot += fan - 1


def all_reduce(packed, shared_rows):
    plan = (
        ("tile", ((1,), (2,), (16, 4, 8)), packed.shape[0]),
        ("mlp", ((2, 1, 4),), shared_rows),
    )
    steps = sum(2 * ((1 << len(bits)) - 1) for axis, groups, rows in plan for bits in groups)
    return pl.pallas_call(
        functools.partial(reduce_kernel, plan),
        out_shape=jax.ShapeDtypeStruct(packed.shape, packed.dtype),
        in_specs=[pl.BlockSpec(memory_space=pltpu.VMEM)],
        out_specs=pl.BlockSpec(memory_space=pltpu.VMEM),
        scratch_shapes=[
            pltpu.VMEM((steps, packed.shape[0] // 2) + packed.shape[1:], packed.dtype),
            pltpu.SemaphoreType.DMA((steps,)),
            pltpu.SemaphoreType.DMA((steps,)),
        ],
        compiler_params=pltpu.CompilerParams(collective_id=0, has_side_effects=True),
    )(packed)

def gather_kernel(x_ref, o_ref, send_sem, recv_sem):
    me = lax.axis_index("mlp")
    rows = x_ref.shape[0]
    bits = (1, 2, 4)

    def partner(distance):
        index = me
        for place, bit in enumerate(bits):
            if (distance >> place) & 1:
                index = flip(index, bit)
        return index

    barrier = pltpu.get_barrier_semaphore()
    for distance in range(1, 8):
        pl.semaphore_signal(barrier, inc=1, device_id={"mlp": partner(distance)}, device_id_type=MESH)
    pl.semaphore_wait(barrier, 7)
    copies = []
    for distance in range(1, 8):
        copy = pltpu.make_async_remote_copy(
            src_ref=x_ref,
            dst_ref=o_ref.at[pl.ds(pl.multiple_of(me * rows, rows), rows)],
            send_sem=send_sem.at[distance - 1],
            recv_sem=recv_sem.at[distance - 1],
            device_id={"mlp": partner(distance)},
            device_id_type=MESH,
        )
        copy.start()
        copies.append(copy)
    o_ref[pl.ds(pl.multiple_of(me * rows, rows), rows)] = x_ref[...]
    for copy in copies:
        copy.wait()


def mlp_gather(x, kernel_id):
    return pl.pallas_call(
        gather_kernel,
        out_shape=jax.ShapeDtypeStruct((x.shape[0] * 8,) + x.shape[1:], x.dtype),
        in_specs=[pl.BlockSpec(memory_space=pltpu.VMEM)],
        out_specs=pl.BlockSpec(memory_space=pltpu.VMEM),
        scratch_shapes=[pltpu.SemaphoreType.DMA((7,)), pltpu.SemaphoreType.DMA((7,))],
        compiler_params=pltpu.CompilerParams(collective_id=kernel_id, has_side_effects=True),
    )(x)


def pair_slope(raw_score, target, weight, heavy_weight, factor):
    chance = jax.nn.sigmoid(raw_score)
    signed = (1.0 - target) * chance - heavy_weight * target * (1.0 - chance)
    return (weight * signed * factor).astype(jnp.bfloat16)


def pair_cost(raw_score, target, weight, heavy_weight):
    missed = heavy_weight * target * jnp.log1p(jnp.exp(-raw_score))
    spurious = (1.0 - target) * jnp.log1p(jnp.exp(raw_score))
    return jnp.sum(weight * (missed + spurious))


def local(features, w_in, w_out, bilinear, partner, counts):
    row_part = features.shape[1]
    feature_width = features.shape[4]
    groups = lax.axis_size("mlp")
    site_rows = row_part * groups
    tile_count = lax.axis_size("tile")
    grid_depth = tile_count // 8
    tile_here = lax.axis_index("tile")
    member = lax.axis_index("mlp")
    block_x = tile_here // (4 * grid_depth)
    block_y = tile_here // grid_depth % 4
    block_z = tile_here % grid_depth
    heavy_weight = 27 * site_rows // 4
    score_scale = feature_width ** (-0.5)
    factor = score_scale / (2 * tile_count * site_rows)
    own_rows = member * row_part + jnp.arange(row_part, dtype=jnp.int32)
    all_rows = jnp.arange(site_rows, dtype=jnp.int32)
    mine_counts = lax.dynamic_index_in_dim(counts, tile_here, 0, keepdims=False)
    mine_partner = lax.dynamic_index_in_dim(partner, tile_here, 0, keepdims=False)
    own_partner = lax.dynamic_slice_in_dim(mine_partner, member * row_part, row_part, 1)
    own_pre_ok = own_rows[None, :] < mine_counts[:, 0:1]
    own_post_ok = own_rows[None, :] < mine_counts[:, 1:2]
    local_x = features.reshape(row_part, 4, feature_width)
    weights = mlp_gather(jnp.stack([w_in.T, w_out], 1), 1)
    own_hidden = jnp.einsum("rcf,hf->rch", local_x, weights[:, 0], preferred_element_type=jnp.float32)
    own_active = jax.nn.gelu(own_hidden).astype(jnp.bfloat16)
    mixed_rows = jnp.einsum("rch,hf->rcf", own_active, weights[:, 1], preferred_element_type=jnp.float32)
    embedded = (local_x.astype(jnp.float32) + mixed_rows).astype(jnp.bfloat16)
    pre_local = embedded[:, 0::2]
    post_local = embedded[:, 1::2]
    query_local = jnp.einsum(
        "ruf,fg->rug", pre_local, bilinear, preferred_element_type=jnp.float32
    ).astype(jnp.bfloat16)

    x_stride = 4 * grid_depth
    y_stride = grid_depth
    query_all = mlp_gather(query_local, 2)
    facing = jnp.where(block_x == 0, post_local[:, 1], post_local[:, 0])
    x_pairs = [(s, (s + x_stride) % tile_count) for s in range(tile_count)]
    from_x = lax.ppermute(facing, "tile", x_pairs)
    halo = jnp.stack([from_x, post_local[:, 0], post_local[:, 1]], 0)

    def position(s, stride, extent):
        return (s // stride) % extent

    def along(arr, stride, extent):
        lower = [(s, s + stride) for s in range(tile_count) if position(s, stride, extent) < extent - 1]
        upper = [(s, s - stride) for s in range(tile_count) if position(s, stride, extent) > 0]
        return jnp.stack(
            [lax.ppermute(arr, "tile", lower), arr, lax.ppermute(arr, "tile", upper)], 0
        )

    def along_back(arr, stride, extent):
        lower = [(s, s - stride) for s in range(tile_count) if position(s, stride, extent) > 0]
        upper = [(s, s + stride) for s in range(tile_count) if position(s, stride, extent) < extent - 1]
        return arr[1] + lax.ppermute(arr[0], "tile", lower) + lax.ppermute(arr[2], "tile", upper)

    halo = along(along(halo, y_stride, 4), 1, grid_depth)
    steps = jnp.arange(3, dtype=jnp.int32) - 1
    dz_grid = steps[:, None]
    dy_grid = steps[None, :]
    inside = (
        (block_y + dy_grid >= 0)
        & (block_y + dy_grid < 4)
        & (block_z + dz_grid >= 0)
        & (block_z + dz_grid < grid_depth)
    )
    near = jnp.clip(tile_here + dy_grid * y_stride + dz_grid, 0, tile_count - 1)
    far = (near + x_stride) % tile_count
    col_counts = jnp.stack(
        [counts[far, block_x, 1], counts[near, 0, 1], counts[near, 1, 1]], -1
    )
    j_ok = inside[..., None, None] & (own_rows < col_counts[..., None])
    loss_sum = jnp.zeros((), jnp.float32)
    post_grad_parts = jnp.zeros(halo.shape, jnp.float32)
    query_grads = []
    place = jnp.arange(3, dtype=jnp.int32)
    code_base = (place[None, None, :] * 9 + (dy_grid[..., None] + 1) * 3 + dz_grid[..., None] + 1) * site_rows
    col_key = (code_base[..., None] + own_rows).reshape(-1)
    for pretile, order, edge in ((0, (0, 1, 2), 0), (1, (1, 2, 0), 2)):
        edge_ok = (block_x == 1) if pretile == 0 else (block_x == 0)
        ordered = halo[:, :, order]
        others = ordered.reshape(-1, feature_width)
        x_ok = jnp.stack([edge_ok if p == edge else jnp.bool_(True) for p in range(3)])
        col_ok = (j_ok[:, :, order] & x_ok[None, None, :, None]).reshape(-1)
        queries = query_all[:, pretile]
        raw_score = (
            jnp.einsum("rf,cf->rc", queries, others, preferred_element_type=jnp.float32)
            * score_scale
        )
        row_ok = all_rows < mine_counts[pretile, 0]
        target = (mine_partner[pretile][:, None] == col_key[None, :]).astype(jnp.float32)
        weight = (row_ok[:, None] & col_ok[None, :]).astype(jnp.float32)
        loss_sum = loss_sum + pair_cost(raw_score, target, weight, heavy_weight)
        slope = pair_slope(raw_score, target, weight, heavy_weight, factor)
        query_grads.append(jnp.dot(slope, others, preferred_element_type=jnp.float32))
        back = jnp.einsum("rc,rf->cf", slope, queries, preferred_element_type=jnp.float32)
        back = back.reshape(ordered.shape)
        for p in range(3):
            post_grad_parts = post_grad_parts.at[:, :, order[p]].add(back[:, :, p])
    post_grad_parts = along_back(along_back(post_grad_parts, 1, grid_depth), y_stride, 4)
    back_x = lax.ppermute(post_grad_parts[0], "tile", x_pairs)
    post_back = jnp.stack(
        [
            post_grad_parts[1] + jnp.where(block_x == 1, back_x, 0.0),
            post_grad_parts[2] + jnp.where(block_x == 0, back_x, 0.0),
        ],
        1,
    )
    query_back = butterfly_scatter(jnp.stack(query_grads, 1), "mlp").astype(jnp.bfloat16)
    bilinear_part = jnp.einsum(
        "ruf,rug->fg", pre_local, query_back, preferred_element_type=jnp.float32
    )
    pre_back = jnp.einsum("rug,fg->ruf", query_back, bilinear, preferred_element_type=jnp.float32)
    embed_grad = jnp.stack(
        [pre_back[:, 0], post_back[:, 0], pre_back[:, 1], post_back[:, 1]], 1
    ).astype(jnp.bfloat16)
    whole_x = mlp_gather(local_x, 3)
    hidden_pre = jnp.einsum("rcf,fh->rch", whole_x, w_in, preferred_element_type=jnp.float32)
    active = jax.nn.gelu(hidden_pre).astype(jnp.bfloat16)
    embed_whole = mlp_gather(embed_grad, 4)
    active_grad = jnp.einsum("rcf,hf->rch", embed_whole, w_out, preferred_element_type=jnp.float32)
    unused, pullback = jax.vjp(jax.nn.gelu, hidden_pre)
    hidden_grad = pullback(active_grad)[0].astype(jnp.bfloat16)
    in_part = jnp.einsum("rcf,rch->fh", whole_x, hidden_grad, preferred_element_type=jnp.float32)
    out_part = jnp.einsum("rch,rcf->hf", active, embed_whole, preferred_element_type=jnp.float32)
    width = bilinear_part.shape[1]
    in_rows = in_part.size // width
    out_rows = out_part.size // width
    shared_rows = 320
    total_rows = 768
    loss_rows = jnp.zeros((shared_rows - width, width), jnp.float32).at[0, 0].set(loss_sum)
    pad_rows = jnp.zeros((total_rows - shared_rows - in_rows - out_rows, width), jnp.float32)
    packed = all_reduce(
        jnp.concatenate(
            [bilinear_part, loss_rows, in_part.reshape(-1, width), out_part.reshape(-1, width), pad_rows], 0
        ),
        shared_rows,
    )
    grad_bilinear = packed[:width]
    loss_total = packed[width, 0]
    grad_in = packed[shared_rows : shared_rows + in_rows].reshape(in_part.shape)
    grad_out = packed[shared_rows + in_rows : shared_rows + in_rows + out_rows].reshape(out_part.shape)
    pair_loss = loss_total / (2.0 * tile_count * site_rows * 27 * site_rows)
    return (pair_loss, grad_in, grad_out, grad_bilinear)


def solution(mesh):
    placed = (P("tile", "mlp", None, None, None), P(None, "mlp"), P("mlp", None), P(), P(), P())
    return jax.shard_map(
        local,
        mesh=mesh,
        in_specs=placed,
        out_specs=(P(), P(None, "mlp"), P("mlp", None), P()),
        check_vma=False,
    )
```

```python
import functools

import jax
import jax.numpy as jnp
from jax import lax
from jax.experimental import pallas as pl
from jax.experimental.pallas import tpu as pltpu
from jax.sharding import PartitionSpec as P

column_plan = ((-1, 1), (0, 0), (0, 1), (1, 0))


def shifted(array, axis, by):
    peers = lax.axis_size(axis)
    pairs = [(i, i + by) for i in range(peers) if 0 <= i + by < peers]
    return lax.ppermute(array, axis, pairs)


def butterfly_sum(x, axis):
    peers = lax.axis_size(axis)
    step = 1
    while step < peers:
        x = x + lax.ppermute(x, axis, [(i, i ^ step) for i in range(peers)])
        step *= 2
    return x


def butterfly_gather(x, axis):
    peers = lax.axis_size(axis)
    me = lax.axis_index(axis)
    step = 1
    while step < peers:
        other = lax.ppermute(x, axis, [(i, i ^ step) for i in range(peers)])
        low = (me & step) == 0
        x = jnp.where(low, jnp.concatenate([x, other], 0), jnp.concatenate([other, x], 0))
        step *= 2
    return x


def butterfly_scatter(x, axis):
    peers = lax.axis_size(axis)
    me = lax.axis_index(axis)
    step = peers // 2
    while step >= 1:
        half = x.shape[0] // 2
        upper = (me & step) != 0
        send = jnp.where(upper, x[:half], x[half:])
        keep = jnp.where(upper, x[half:], x[:half])
        x = keep + lax.ppermute(send, axis, [(i, i ^ step) for i in range(peers)])
        step //= 2
    return x


MESH = pl.DeviceIdType.MESH


def flip(index, bit):
    return index + bit - 2 * bit * ((index // bit) % 2)


def reduce_kernel(x_ref, l_ref, o_ref, lo_ref, recv, lrecv, lbuf, send_sem, recv_sem, lsend_sem, lrecv_sem):
    coords = {axis: lax.axis_index(axis) for axis in ("tile", "mlp")}
    tile_groups = ((1,), (2,), (16, 4, 8))
    mlp_bits = (2, 1, 4)

    def partner(axis, bits, distance):
        index = coords[axis]
        for place, bit in enumerate(bits):
            if (distance >> place) & 1:
                index = flip(index, bit)
        return index

    def rank(axis, bits, distance=0):
        total = 0
        for place, bit in enumerate(bits):
            own = (coords[axis] // bit) % 2
            if (distance >> place) & 1:
                own = 1 - own
            total = total + own * (1 << place)
        return total

    def ordered_sum(blocks, axis, bits):
        fan = 1 << len(bits)
        if fan == 2:
            return blocks[0] + blocks[1]
        total = None
        for q in range(fan):
            pick = None
            for distance in range(fan):
                term = jnp.where(rank(axis, bits, distance) == q, blocks[distance], 0.0)
                pick = term if pick is None else pick + term
            total = pick if total is None else total + pick
        return total

    steps = [("tile", bits) for bits in tile_groups] + [("mlp", mlp_bits)]
    barrier = pltpu.get_barrier_semaphore()
    greeted = 0
    for axis, bits in steps:
        for distance in range(1, 1 << len(bits)):
            pl.semaphore_signal(
                barrier, inc=1, device_id={axis: partner(axis, bits, distance)}, device_id_type=MESH
            )
            greeted += 1
    pl.semaphore_wait(barrier, greeted)
    o_ref[...] = x_ref[...]

    def send_all(axis, bits, slot, sources, length, loss_slot=None):
        copies = []
        for distance in range(1, 1 << len(bits)):
            target = {axis: partner(axis, bits, distance)}
            copy = pltpu.make_async_remote_copy(
                src_ref=o_ref.at[pl.ds(pl.multiple_of(sources(distance), 8), length)],
                dst_ref=recv.at[slot + distance - 1, pl.ds(0, length)],
                send_sem=send_sem.at[slot + distance - 1],
                recv_sem=recv_sem.at[slot + distance - 1],
                device_id=target,
                device_id_type=MESH,
            )
            copy.start()
            copies.append(copy)
            if loss_slot is not None:
                copy = pltpu.make_async_remote_copy(
                    src_ref=lbuf.at[loss_slot[0]],
                    dst_ref=lrecv.at[loss_slot[1] + distance - 1],
                    send_sem=lsend_sem.at[loss_slot[1] + distance - 1],
                    recv_sem=lrecv_sem.at[loss_slot[1] + distance - 1],
                    device_id=target,
                    device_id_type=MESH,
                )
                copy.start()
                copies.append(copy)
        for copy in copies:
            copy.wait()

    loss = l_ref[...]
    slot = 0
    lslot = 0
    start = 0
    length = o_ref.shape[0]
    for stage, (axis, bits) in enumerate(steps):
        fan = 1 << len(bits)
        lbuf[stage] = loss
        if axis == "tile":
            length //= fan
            send_all(axis, bits, slot, lambda d: start + rank(axis, bits, d) * length, length, (stage, lslot))
            start = start + rank(axis, bits) * length
            mine = pl.ds(pl.multiple_of(start, 8), length)
            total = o_ref[mine]
            for distance in range(1, fan):
                total = total + recv[slot + distance - 1, pl.ds(0, length)]
            o_ref[mine] = total
        else:
            send_all(axis, bits, slot, lambda d: start, length, (stage, lslot))
            mine = pl.ds(pl.multiple_of(start, 8), length)
            own = o_ref[mine]
            blocks = [own] + [recv[slot + distance - 1, pl.ds(0, length)] for distance in range(1, fan)]
            o_ref[mine] = jnp.where(start < x_ref.shape[1], ordered_sum(blocks, axis, bits), own)
        loss = ordered_sum([loss] + [lrecv[lslot + distance - 1] for distance in range(1, fan)], axis, bits)
        slot += fan - 1
        lslot += fan - 1
    lo_ref[...] = loss
    for bits in reversed(tile_groups):
        fan = 1 << len(bits)
        send_all("tile", bits, slot, lambda d: start, length)
        base = start - rank("tile", bits) * length
        for distance in range(1, fan):
            spot = base + rank("tile", bits, distance) * length
            o_ref[pl.ds(pl.multiple_of(spot, 8), length)] = recv[slot + distance - 1, pl.ds(0, length)]
        start = base
        length *= fan
        slot += fan - 1


def all_reduce(packed, loss_block):
    slots = 2 * (1 + 1 + 7) + 7
    loss_slots = 1 + 1 + 7 + 7
    return pl.pallas_call(
        reduce_kernel,
        out_shape=(
            jax.ShapeDtypeStruct(packed.shape, packed.dtype),
            jax.ShapeDtypeStruct(loss_block.shape, loss_block.dtype),
        ),
        in_specs=[pl.BlockSpec(memory_space=pltpu.VMEM)] * 2,
        out_specs=(pl.BlockSpec(memory_space=pltpu.VMEM), pl.BlockSpec(memory_space=pltpu.VMEM)),
        scratch_shapes=[
            pltpu.VMEM((slots, packed.shape[0] // 2) + packed.shape[1:], packed.dtype),
            pltpu.VMEM((loss_slots,) + loss_block.shape, loss_block.dtype),
            pltpu.VMEM((4,) + loss_block.shape, loss_block.dtype),
            pltpu.SemaphoreType.DMA((slots,)),
            pltpu.SemaphoreType.DMA((slots,)),
            pltpu.SemaphoreType.DMA((loss_slots,)),
            pltpu.SemaphoreType.DMA((loss_slots,)),
        ],
        compiler_params=pltpu.CompilerParams(collective_id=0, has_side_effects=True),
    )(packed, loss_block)

def pair_slope(raw_score, target, weight, heavy_weight, factor):
    chance = jax.nn.sigmoid(raw_score)
    signed = (1.0 - target) * chance - heavy_weight * target * (1.0 - chance)
    return (weight * signed * factor).astype(jnp.bfloat16)


def pair_cost(raw_score, target, weight, heavy_weight):
    missed = heavy_weight * target * jnp.log1p(jnp.exp(-raw_score))
    spurious = (1.0 - target) * jnp.log1p(jnp.exp(raw_score))
    return jnp.sum(weight * (missed + spurious))


def local(features, w_in, w_out, bilinear, partner, counts):
    row_part = features.shape[1]
    feature_width = features.shape[4]
    groups = lax.axis_size("mlp")
    site_rows = row_part * groups
    tile_count = lax.axis_size("tile")
    grid_depth = tile_count // 8
    tile_here = lax.axis_index("tile")
    member = lax.axis_index("mlp")
    block_x = tile_here // (4 * grid_depth)
    block_y = tile_here // grid_depth % 4
    block_z = tile_here % grid_depth
    heavy_weight = 27 * site_rows // 4
    score_scale = feature_width ** (-0.5)
    factor = score_scale / (2 * tile_count * site_rows)
    own_rows = member * row_part + jnp.arange(row_part, dtype=jnp.int32)
    all_rows = jnp.arange(site_rows, dtype=jnp.int32)
    mine_counts = lax.dynamic_index_in_dim(counts, tile_here, 0, keepdims=False)
    mine_partner = lax.dynamic_index_in_dim(partner, tile_here, 0, keepdims=False)
    own_partner = lax.dynamic_slice_in_dim(mine_partner, member * row_part, row_part, 1)
    own_pre_ok = own_rows[None, :] < mine_counts[:, 0:1]
    own_post_ok = own_rows[None, :] < mine_counts[:, 1:2]
    local_x = features.reshape(row_part, 4, feature_width)
    weights = butterfly_gather(jnp.stack([w_in.T, w_out], 1), "mlp")
    own_hidden = jnp.einsum("rcf,hf->rch", local_x, weights[:, 0], preferred_element_type=jnp.float32)
    own_active = jax.nn.gelu(own_hidden).astype(jnp.bfloat16)
    mixed_rows = jnp.einsum("rch,hf->rcf", own_active, weights[:, 1], preferred_element_type=jnp.float32)
    embedded = (local_x.astype(jnp.float32) + mixed_rows).astype(jnp.bfloat16)
    pre_local = embedded[:, 0::2]
    post_local = embedded[:, 1::2]
    query_local = jnp.einsum(
        "ruf,fg->rug", pre_local, bilinear, preferred_element_type=jnp.float32
    ).astype(jnp.bfloat16)

    x_stride = 4 * grid_depth
    y_stride = grid_depth
    query_all = butterfly_gather(query_local, "mlp")
    facing = jnp.where(block_x == 0, post_local[:, 1], post_local[:, 0])
    x_pairs = [(s, (s + x_stride) % tile_count) for s in range(tile_count)]
    from_x = lax.ppermute(facing, "tile", x_pairs)
    halo = jnp.stack([from_x, post_local[:, 0], post_local[:, 1]], 0)

    def position(s, stride, extent):
        return (s // stride) % extent

    def along(arr, stride, extent):
        lower = [(s, s + stride) for s in range(tile_count) if position(s, stride, extent) < extent - 1]
        upper = [(s, s - stride) for s in range(tile_count) if position(s, stride, extent) > 0]
        return jnp.stack(
            [lax.ppermute(arr, "tile", lower), arr, lax.ppermute(arr, "tile", upper)], 0
        )

    def along_back(arr, stride, extent):
        lower = [(s, s - stride) for s in range(tile_count) if position(s, stride, extent) > 0]
        upper = [(s, s + stride) for s in range(tile_count) if position(s, stride, extent) < extent - 1]
        return arr[1] + lax.ppermute(arr[0], "tile", lower) + lax.ppermute(arr[2], "tile", upper)

    halo = along(along(halo, y_stride, 4), 1, grid_depth)
    steps = jnp.arange(3, dtype=jnp.int32) - 1
    dz_grid = steps[:, None]
    dy_grid = steps[None, :]
    inside = (
        (block_y + dy_grid >= 0)
        & (block_y + dy_grid < 4)
        & (block_z + dz_grid >= 0)
        & (block_z + dz_grid < grid_depth)
    )
    near = jnp.clip(tile_here + dy_grid * y_stride + dz_grid, 0, tile_count - 1)
    far = (near + x_stride) % tile_count
    col_counts = jnp.stack(
        [counts[far, block_x, 1], counts[near, 0, 1], counts[near, 1, 1]], -1
    )
    j_ok = inside[..., None, None] & (own_rows < col_counts[..., None])
    loss_sum = jnp.zeros((), jnp.float32)
    post_grad_parts = jnp.zeros(halo.shape, jnp.float32)
    query_grads = []
    place = jnp.arange(3, dtype=jnp.int32)
    code_base = (place[None, None, :] * 9 + (dy_grid[..., None] + 1) * 3 + dz_grid[..., None] + 1) * site_rows
    col_key = (code_base[..., None] + own_rows).reshape(-1)
    for pretile, order, edge in ((0, (0, 1, 2), 0), (1, (1, 2, 0), 2)):
        edge_ok = (block_x == 1) if pretile == 0 else (block_x == 0)
        ordered = halo[:, :, order]
        others = ordered.reshape(-1, feature_width)
        x_ok = jnp.stack([edge_ok if p == edge else jnp.bool_(True) for p in range(3)])
        col_ok = (j_ok[:, :, order] & x_ok[None, None, :, None]).reshape(-1)
        queries = query_all[:, pretile]
        raw_score = (
            jnp.einsum("rf,cf->rc", queries, others, preferred_element_type=jnp.float32)
            * score_scale
        )
        row_ok = all_rows < mine_counts[pretile, 0]
        target = (mine_partner[pretile][:, None] == col_key[None, :]).astype(jnp.float32)
        weight = (row_ok[:, None] & col_ok[None, :]).astype(jnp.float32)
        loss_sum = loss_sum + pair_cost(raw_score, target, weight, heavy_weight)
        slope = pair_slope(raw_score, target, weight, heavy_weight, factor)
        query_grads.append(jnp.dot(slope, others, preferred_element_type=jnp.float32))
        back = jnp.einsum("rc,rf->cf", slope, queries, preferred_element_type=jnp.float32)
        back = back.reshape(ordered.shape)
        for p in range(3):
            post_grad_parts = post_grad_parts.at[:, :, order[p]].add(back[:, :, p])
    post_grad_parts = along_back(along_back(post_grad_parts, 1, grid_depth), y_stride, 4)
    back_x = lax.ppermute(post_grad_parts[0], "tile", x_pairs)
    post_back = jnp.stack(
        [
            post_grad_parts[1] + jnp.where(block_x == 1, back_x, 0.0),
            post_grad_parts[2] + jnp.where(block_x == 0, back_x, 0.0),
        ],
        1,
    )
    query_back = butterfly_scatter(jnp.stack(query_grads, 1), "mlp").astype(jnp.bfloat16)
    bilinear_part = jnp.einsum(
        "ruf,rug->fg", pre_local, query_back, preferred_element_type=jnp.float32
    )
    pre_back = jnp.einsum("rug,fg->ruf", query_back, bilinear, preferred_element_type=jnp.float32)
    embed_grad = jnp.stack(
        [pre_back[:, 0], post_back[:, 0], pre_back[:, 1], post_back[:, 1]], 1
    ).astype(jnp.bfloat16)
    whole_x = butterfly_gather(local_x, "mlp")
    hidden_pre = jnp.einsum("rcf,fh->rch", whole_x, w_in, preferred_element_type=jnp.float32)
    active = jax.nn.gelu(hidden_pre).astype(jnp.bfloat16)
    embed_whole = butterfly_gather(embed_grad, "mlp")
    active_grad = jnp.einsum("rcf,hf->rch", embed_whole, w_out, preferred_element_type=jnp.float32)
    unused, pullback = jax.vjp(jax.nn.gelu, hidden_pre)
    hidden_grad = pullback(active_grad)[0].astype(jnp.bfloat16)
    in_part = jnp.einsum("rcf,rch->fh", whole_x, hidden_grad, preferred_element_type=jnp.float32)
    out_part = jnp.einsum("rch,rcf->hf", active, embed_whole, preferred_element_type=jnp.float32)
    width = bilinear_part.shape[1]
    in_rows = in_part.size // width
    out_rows = out_part.size // width
    packed, loss_block = all_reduce(
        jnp.concatenate([bilinear_part, in_part.reshape(-1, width), out_part.reshape(-1, width)], 0),
        jnp.broadcast_to(loss_sum, (8, 128)),
    )
    grad_bilinear = packed[:width]
    loss_total = loss_block[0, 0]
    grad_in = packed[width : width + in_rows].reshape(in_part.shape)
    grad_out = packed[width + in_rows : width + in_rows + out_rows].reshape(out_part.shape)
    pair_loss = loss_total / (2.0 * tile_count * site_rows * 27 * site_rows)
    return (pair_loss, grad_in, grad_out, grad_bilinear)


def solution(mesh):
    placed = (P("tile", "mlp", None, None, None), P(None, "mlp"), P("mlp", None), P(), P(), P())
    return jax.shard_map(
        local,
        mesh=mesh,
        in_specs=placed,
        out_specs=(P(), P(None, "mlp"), P("mlp", None), P()),
        check_vma=False,
    )
```

```python
import functools

import jax
import jax.numpy as jnp
from jax import lax
from jax.experimental import pallas as pl
from jax.experimental.pallas import tpu as pltpu
from jax.sharding import PartitionSpec as P

column_plan = ((-1, 1), (0, 0), (0, 1), (1, 0))


def shifted(array, axis, by):
    peers = lax.axis_size(axis)
    pairs = [(i, i + by) for i in range(peers) if 0 <= i + by < peers]
    return lax.ppermute(array, axis, pairs)


def butterfly_sum(x, axis):
    peers = lax.axis_size(axis)
    step = 1
    while step < peers:
        x = x + lax.ppermute(x, axis, [(i, i ^ step) for i in range(peers)])
        step *= 2
    return x


def butterfly_gather(x, axis):
    peers = lax.axis_size(axis)
    me = lax.axis_index(axis)
    step = 1
    while step < peers:
        other = lax.ppermute(x, axis, [(i, i ^ step) for i in range(peers)])
        low = (me & step) == 0
        x = jnp.where(low, jnp.concatenate([x, other], 0), jnp.concatenate([other, x], 0))
        step *= 2
    return x


def butterfly_scatter(x, axis):
    peers = lax.axis_size(axis)
    me = lax.axis_index(axis)
    step = peers // 2
    while step >= 1:
        half = x.shape[0] // 2
        upper = (me & step) != 0
        send = jnp.where(upper, x[:half], x[half:])
        keep = jnp.where(upper, x[half:], x[:half])
        x = keep + lax.ppermute(send, axis, [(i, i ^ step) for i in range(peers)])
        step //= 2
    return x


MESH = pl.DeviceIdType.MESH


def flip(index, bit):
    return index + bit - 2 * bit * ((index // bit) % 2)


def reduce_kernel(x_ref, l_ref, o_ref, lo_ref, recv, lrecv, lbuf, send_sem, recv_sem, lsend_sem, lrecv_sem):
    coords = {axis: lax.axis_index(axis) for axis in ("tile", "mlp")}
    tile_groups = ((1,), (2,), (16, 4, 8))
    mlp_bits = (2, 1, 4)

    def partner(axis, bits, distance):
        index = coords[axis]
        for place, bit in enumerate(bits):
            if (distance >> place) & 1:
                index = flip(index, bit)
        return index

    def rank(axis, bits, distance=0):
        total = 0
        for place, bit in enumerate(bits):
            own = (coords[axis] // bit) % 2
            if (distance >> place) & 1:
                own = 1 - own
            total = total + own * (1 << place)
        return total

    def ordered_sum(blocks, axis, bits):
        fan = 1 << len(bits)
        if fan == 2:
            return blocks[0] + blocks[1]
        total = None
        for q in range(fan):
            pick = None
            for distance in range(fan):
                term = jnp.where(rank(axis, bits, distance) == q, blocks[distance], 0.0)
                pick = term if pick is None else pick + term
            total = pick if total is None else total + pick
        return total

    steps = [("tile", bits) for bits in tile_groups] + [("mlp", mlp_bits)]
    barrier = pltpu.get_barrier_semaphore()
    greeted = 0
    for axis, bits in steps:
        for distance in range(1, 1 << len(bits)):
            pl.semaphore_signal(
                barrier, inc=1, device_id={axis: partner(axis, bits, distance)}, device_id_type=MESH
            )
            greeted += 1
    pl.semaphore_wait(barrier, greeted)
    o_ref[...] = x_ref[...]

    def send_all(axis, bits, slot, sources, length, loss_slot=None):
        copies = []
        for distance in range(1, 1 << len(bits)):
            target = {axis: partner(axis, bits, distance)}
            copy = pltpu.make_async_remote_copy(
                src_ref=o_ref.at[pl.ds(pl.multiple_of(sources(distance), 8), length)],
                dst_ref=recv.at[slot + distance - 1, pl.ds(0, length)],
                send_sem=send_sem.at[slot + distance - 1],
                recv_sem=recv_sem.at[slot + distance - 1],
                device_id=target,
                device_id_type=MESH,
            )
            copy.start()
            copies.append(copy)
            if loss_slot is not None:
                copy = pltpu.make_async_remote_copy(
                    src_ref=lbuf.at[loss_slot[0]],
                    dst_ref=lrecv.at[loss_slot[1] + distance - 1],
                    send_sem=lsend_sem.at[loss_slot[1] + distance - 1],
                    recv_sem=lrecv_sem.at[loss_slot[1] + distance - 1],
                    device_id=target,
                    device_id_type=MESH,
                )
                copy.start()
                copies.append(copy)
        for copy in copies:
            copy.wait()

    loss = l_ref[...]
    slot = 0
    lslot = 0
    start = 0
    length = o_ref.shape[0]
    for stage, (axis, bits) in enumerate(steps):
        fan = 1 << len(bits)
        lbuf[stage] = loss
        if axis == "tile":
            length //= fan
            send_all(axis, bits, slot, lambda d: start + rank(axis, bits, d) * length, length, (stage, lslot))
            start = start + rank(axis, bits) * length
            mine = pl.ds(pl.multiple_of(start, 8), length)
            total = o_ref[mine]
            for distance in range(1, fan):
                total = total + recv[slot + distance - 1, pl.ds(0, length)]
            o_ref[mine] = total
        else:
            send_all(axis, bits, slot, lambda d: start, length, (stage, lslot))
            mine = pl.ds(pl.multiple_of(start, 8), length)
            own = o_ref[mine]
            blocks = [own] + [recv[slot + distance - 1, pl.ds(0, length)] for distance in range(1, fan)]
            o_ref[mine] = jnp.where(start < x_ref.shape[1], ordered_sum(blocks, axis, bits), own)
        loss = ordered_sum([loss] + [lrecv[lslot + distance - 1] for distance in range(1, fan)], axis, bits)
        slot += fan - 1
        lslot += fan - 1
    lo_ref[...] = loss
    for bits in reversed(tile_groups):
        fan = 1 << len(bits)
        send_all("tile", bits, slot, lambda d: start, length)
        base = start - rank("tile", bits) * length
        for distance in range(1, fan):
            spot = base + rank("tile", bits, distance) * length
            o_ref[pl.ds(pl.multiple_of(spot, 8), length)] = recv[slot + distance - 1, pl.ds(0, length)]
        start = base
        length *= fan
        slot += fan - 1


def all_reduce(packed, loss_block):
    slots = 2 * (1 + 1 + 7) + 7
    loss_slots = 1 + 1 + 7 + 7
    return pl.pallas_call(
        reduce_kernel,
        out_shape=(
            jax.ShapeDtypeStruct(packed.shape, packed.dtype),
            jax.ShapeDtypeStruct(loss_block.shape, loss_block.dtype),
        ),
        in_specs=[pl.BlockSpec(memory_space=pltpu.VMEM)] * 2,
        out_specs=(pl.BlockSpec(memory_space=pltpu.VMEM), pl.BlockSpec(memory_space=pltpu.VMEM)),
        scratch_shapes=[
            pltpu.VMEM((slots, packed.shape[0] // 2) + packed.shape[1:], packed.dtype),
            pltpu.VMEM((loss_slots,) + loss_block.shape, loss_block.dtype),
            pltpu.VMEM((4,) + loss_block.shape, loss_block.dtype),
            pltpu.SemaphoreType.DMA((slots,)),
            pltpu.SemaphoreType.DMA((slots,)),
            pltpu.SemaphoreType.DMA((loss_slots,)),
            pltpu.SemaphoreType.DMA((loss_slots,)),
        ],
        compiler_params=pltpu.CompilerParams(collective_id=0, has_side_effects=True),
    )(packed, loss_block)

def pair_slope(raw_score, target, weight, heavy_weight, factor):
    chance = jax.nn.sigmoid(raw_score)
    signed = (1.0 - target) * chance - heavy_weight * target * (1.0 - chance)
    return (weight * signed * factor).astype(jnp.bfloat16)


def pair_cost(raw_score, target, weight, heavy_weight):
    missed = heavy_weight * target * jnp.log1p(jnp.exp(-raw_score))
    spurious = (1.0 - target) * jnp.log1p(jnp.exp(raw_score))
    return jnp.sum(weight * (missed + spurious))


def local(features, w_in, w_out, bilinear, partner, counts):
    row_part = features.shape[1]
    feature_width = features.shape[4]
    groups = lax.axis_size("mlp")
    site_rows = row_part * groups
    tile_count = lax.axis_size("tile")
    grid_depth = tile_count // 8
    tile_here = lax.axis_index("tile")
    member = lax.axis_index("mlp")
    block_x = tile_here // (4 * grid_depth)
    block_y = tile_here // grid_depth % 4
    block_z = tile_here % grid_depth
    heavy_weight = 27 * site_rows // 4
    score_scale = feature_width ** (-0.5)
    factor = score_scale / (2 * tile_count * site_rows)
    own_rows = member * row_part + jnp.arange(row_part, dtype=jnp.int32)
    all_rows = jnp.arange(site_rows, dtype=jnp.int32)
    mine_counts = lax.dynamic_index_in_dim(counts, tile_here, 0, keepdims=False)
    mine_partner = lax.dynamic_index_in_dim(partner, tile_here, 0, keepdims=False)
    own_partner = lax.dynamic_slice_in_dim(mine_partner, member * row_part, row_part, 1)
    own_pre_ok = own_rows[None, :] < mine_counts[:, 0:1]
    own_post_ok = own_rows[None, :] < mine_counts[:, 1:2]
    local_x = features.reshape(row_part, 4, feature_width)
    weight_rows = jnp.stack([w_in.T, w_out], 1).reshape(-1, feature_width)
    mixed_gather = butterfly_gather(
        jnp.concatenate([weight_rows, local_x.reshape(-1, feature_width)], 0)[None], "mlp"
    )
    weights = mixed_gather[:, : weight_rows.shape[0]].reshape(-1, 2, feature_width)
    whole_x = mixed_gather[:, weight_rows.shape[0] :].reshape(-1, 4, feature_width)
    own_hidden = jnp.einsum("rcf,hf->rch", local_x, weights[:, 0], preferred_element_type=jnp.float32)
    own_active = jax.nn.gelu(own_hidden).astype(jnp.bfloat16)
    mixed_rows = jnp.einsum("rch,hf->rcf", own_active, weights[:, 1], preferred_element_type=jnp.float32)
    embedded = (local_x.astype(jnp.float32) + mixed_rows).astype(jnp.bfloat16)
    pre_local = embedded[:, 0::2]
    post_local = embedded[:, 1::2]
    query_local = jnp.einsum(
        "ruf,fg->rug", pre_local, bilinear, preferred_element_type=jnp.float32
    ).astype(jnp.bfloat16)

    x_stride = 4 * grid_depth
    y_stride = grid_depth
    query_all = butterfly_gather(query_local, "mlp")
    facing = jnp.where(block_x == 0, post_local[:, 1], post_local[:, 0])
    x_pairs = [(s, (s + x_stride) % tile_count) for s in range(tile_count)]
    from_x = lax.ppermute(facing, "tile", x_pairs)
    halo = jnp.stack([from_x, post_local[:, 0], post_local[:, 1]], 0)

    def position(s, stride, extent):
        return (s // stride) % extent

    def along(arr, stride, extent):
        lower = [(s, s + stride) for s in range(tile_count) if position(s, stride, extent) < extent - 1]
        upper = [(s, s - stride) for s in range(tile_count) if position(s, stride, extent) > 0]
        return jnp.stack(
            [lax.ppermute(arr, "tile", lower), arr, lax.ppermute(arr, "tile", upper)], 0
        )

    def along_back(arr, stride, extent):
        lower = [(s, s - stride) for s in range(tile_count) if position(s, stride, extent) > 0]
        upper = [(s, s + stride) for s in range(tile_count) if position(s, stride, extent) < extent - 1]
        return arr[1] + lax.ppermute(arr[0], "tile", lower) + lax.ppermute(arr[2], "tile", upper)

    halo = along(along(halo, y_stride, 4), 1, grid_depth)
    steps = jnp.arange(3, dtype=jnp.int32) - 1
    dz_grid = steps[:, None]
    dy_grid = steps[None, :]
    inside = (
        (block_y + dy_grid >= 0)
        & (block_y + dy_grid < 4)
        & (block_z + dz_grid >= 0)
        & (block_z + dz_grid < grid_depth)
    )
    near = jnp.clip(tile_here + dy_grid * y_stride + dz_grid, 0, tile_count - 1)
    far = (near + x_stride) % tile_count
    col_counts = jnp.stack(
        [counts[far, block_x, 1], counts[near, 0, 1], counts[near, 1, 1]], -1
    )
    j_ok = inside[..., None, None] & (own_rows < col_counts[..., None])
    loss_sum = jnp.zeros((), jnp.float32)
    post_grad_parts = jnp.zeros(halo.shape, jnp.float32)
    query_grads = []
    place = jnp.arange(3, dtype=jnp.int32)
    code_base = (place[None, None, :] * 9 + (dy_grid[..., None] + 1) * 3 + dz_grid[..., None] + 1) * site_rows
    col_key = (code_base[..., None] + own_rows).reshape(-1)
    for pretile, order, edge in ((0, (0, 1, 2), 0), (1, (1, 2, 0), 2)):
        edge_ok = (block_x == 1) if pretile == 0 else (block_x == 0)
        ordered = halo[:, :, order]
        others = ordered.reshape(-1, feature_width)
        x_ok = jnp.stack([edge_ok if p == edge else jnp.bool_(True) for p in range(3)])
        col_ok = (j_ok[:, :, order] & x_ok[None, None, :, None]).reshape(-1)
        queries = query_all[:, pretile]
        raw_score = (
            jnp.einsum("rf,cf->rc", queries, others, preferred_element_type=jnp.float32)
            * score_scale
        )
        row_ok = all_rows < mine_counts[pretile, 0]
        target = (mine_partner[pretile][:, None] == col_key[None, :]).astype(jnp.float32)
        weight = (row_ok[:, None] & col_ok[None, :]).astype(jnp.float32)
        loss_sum = loss_sum + pair_cost(raw_score, target, weight, heavy_weight)
        slope = pair_slope(raw_score, target, weight, heavy_weight, factor)
        query_grads.append(jnp.dot(slope, others, preferred_element_type=jnp.float32))
        back = jnp.einsum("rc,rf->cf", slope, queries, preferred_element_type=jnp.float32)
        back = back.reshape(ordered.shape)
        for p in range(3):
            post_grad_parts = post_grad_parts.at[:, :, order[p]].add(back[:, :, p])
    post_grad_parts = along_back(along_back(post_grad_parts, 1, grid_depth), y_stride, 4)
    back_x = lax.ppermute(post_grad_parts[0], "tile", x_pairs)
    post_back = jnp.stack(
        [
            post_grad_parts[1] + jnp.where(block_x == 1, back_x, 0.0),
            post_grad_parts[2] + jnp.where(block_x == 0, back_x, 0.0),
        ],
        1,
    )
    query_back = butterfly_scatter(jnp.stack(query_grads, 1), "mlp").astype(jnp.bfloat16)
    bilinear_part = jnp.einsum(
        "ruf,rug->fg", pre_local, query_back, preferred_element_type=jnp.float32
    )
    pre_back = jnp.einsum("rug,fg->ruf", query_back, bilinear, preferred_element_type=jnp.float32)
    embed_grad = jnp.stack(
        [pre_back[:, 0], post_back[:, 0], pre_back[:, 1], post_back[:, 1]], 1
    ).astype(jnp.bfloat16)
    hidden_pre = jnp.einsum("rcf,fh->rch", whole_x, w_in, preferred_element_type=jnp.float32)
    active = jax.nn.gelu(hidden_pre).astype(jnp.bfloat16)
    embed_whole = butterfly_gather(embed_grad, "mlp")
    active_grad = jnp.einsum("rcf,hf->rch", embed_whole, w_out, preferred_element_type=jnp.float32)
    unused, pullback = jax.vjp(jax.nn.gelu, hidden_pre)
    hidden_grad = pullback(active_grad)[0].astype(jnp.bfloat16)
    in_part = jnp.einsum("rcf,rch->fh", whole_x, hidden_grad, preferred_element_type=jnp.float32)
    out_part = jnp.einsum("rch,rcf->hf", active, embed_whole, preferred_element_type=jnp.float32)
    width = bilinear_part.shape[1]
    in_rows = in_part.size // width
    out_rows = out_part.size // width
    packed, loss_block = all_reduce(
        jnp.concatenate([bilinear_part, in_part.reshape(-1, width), out_part.reshape(-1, width)], 0),
        jnp.broadcast_to(loss_sum, (8, 128)),
    )
    grad_bilinear = packed[:width]
    loss_total = loss_block[0, 0]
    grad_in = packed[width : width + in_rows].reshape(in_part.shape)
    grad_out = packed[width + in_rows : width + in_rows + out_rows].reshape(out_part.shape)
    pair_loss = loss_total / (2.0 * tile_count * site_rows * 27 * site_rows)
    return (pair_loss, grad_in, grad_out, grad_bilinear)


def solution(mesh):
    placed = (P("tile", "mlp", None, None, None), P(None, "mlp"), P("mlp", None), P(), P(), P())
    return jax.shard_map(
        local,
        mesh=mesh,
        in_specs=placed,
        out_specs=(P(), P(None, "mlp"), P("mlp", None), P()),
        check_vma=False,
    )
```

```python
import functools

import jax
import jax.numpy as jnp
from jax import lax
from jax.experimental import pallas as pl
from jax.experimental.pallas import tpu as pltpu
from jax.sharding import PartitionSpec as P

column_plan = ((-1, 1), (0, 0), (0, 1), (1, 0))


def shifted(array, axis, by):
    peers = lax.axis_size(axis)
    pairs = [(i, i + by) for i in range(peers) if 0 <= i + by < peers]
    return lax.ppermute(array, axis, pairs)


def butterfly_sum(x, axis):
    peers = lax.axis_size(axis)
    step = 1
    while step < peers:
        x = x + lax.ppermute(x, axis, [(i, i ^ step) for i in range(peers)])
        step *= 2
    return x


def butterfly_gather(x, axis):
    peers = lax.axis_size(axis)
    me = lax.axis_index(axis)
    step = 1
    while step < peers:
        other = lax.ppermute(x, axis, [(i, i ^ step) for i in range(peers)])
        low = (me & step) == 0
        x = jnp.where(low, jnp.concatenate([x, other], 0), jnp.concatenate([other, x], 0))
        step *= 2
    return x


def butterfly_scatter(x, axis):
    peers = lax.axis_size(axis)
    me = lax.axis_index(axis)
    step = peers // 2
    while step >= 1:
        half = x.shape[0] // 2
        upper = (me & step) != 0
        send = jnp.where(upper, x[:half], x[half:])
        keep = jnp.where(upper, x[half:], x[:half])
        x = keep + lax.ppermute(send, axis, [(i, i ^ step) for i in range(peers)])
        step //= 2
    return x


MESH = pl.DeviceIdType.MESH


def flip(index, bit):
    return index + bit - 2 * bit * ((index // bit) % 2)


def reduce_kernel(x_ref, l_ref, o_ref, lo_ref, recv, lrecv, lbuf, send_sem, recv_sem, lsend_sem, lrecv_sem):
    coords = {axis: lax.axis_index(axis) for axis in ("tile", "mlp")}
    tile_groups = ((1,), (2,), (16, 4, 8))
    mlp_bits = (2, 1, 4)

    def partner(axis, bits, distance):
        index = coords[axis]
        for place, bit in enumerate(bits):
            if (distance >> place) & 1:
                index = flip(index, bit)
        return index

    def rank(axis, bits, distance=0):
        total = 0
        for place, bit in enumerate(bits):
            own = (coords[axis] // bit) % 2
            if (distance >> place) & 1:
                own = 1 - own
            total = total + own * (1 << place)
        return total

    def ordered_sum(blocks, axis, bits):
        fan = 1 << len(bits)
        if fan == 2:
            return blocks[0] + blocks[1]
        total = None
        for q in range(fan):
            pick = None
            for distance in range(fan):
                term = jnp.where(rank(axis, bits, distance) == q, blocks[distance], 0.0)
                pick = term if pick is None else pick + term
            total = pick if total is None else total + pick
        return total

    steps = [("tile", bits) for bits in tile_groups] + [("mlp", mlp_bits)]
    barrier = pltpu.get_barrier_semaphore()
    greeted = 0
    for axis, bits in steps:
        for distance in range(1, 1 << len(bits)):
            pl.semaphore_signal(
                barrier, inc=1, device_id={axis: partner(axis, bits, distance)}, device_id_type=MESH
            )
            greeted += 1
    pl.semaphore_wait(barrier, greeted)
    o_ref[...] = x_ref[...]

    def send_all(axis, bits, slot, sources, length, loss_slot=None):
        copies = []
        for distance in range(1, 1 << len(bits)):
            target = {axis: partner(axis, bits, distance)}
            copy = pltpu.make_async_remote_copy(
                src_ref=o_ref.at[pl.ds(pl.multiple_of(sources(distance), 8), length)],
                dst_ref=recv.at[slot + distance - 1, pl.ds(0, length)],
                send_sem=send_sem.at[slot + distance - 1],
                recv_sem=recv_sem.at[slot + distance - 1],
                device_id=target,
                device_id_type=MESH,
            )
            copy.start()
            copies.append(copy)
            if loss_slot is not None:
                copy = pltpu.make_async_remote_copy(
                    src_ref=lbuf.at[loss_slot[0]],
                    dst_ref=lrecv.at[loss_slot[1] + distance - 1],
                    send_sem=lsend_sem.at[loss_slot[1] + distance - 1],
                    recv_sem=lrecv_sem.at[loss_slot[1] + distance - 1],
                    device_id=target,
                    device_id_type=MESH,
                )
                copy.start()
                copies.append(copy)
        for copy in copies:
            copy.wait()

    loss = l_ref[...]
    slot = 0
    lslot = 0
    start = 0
    length = o_ref.shape[0]
    for stage, (axis, bits) in enumerate(steps):
        fan = 1 << len(bits)
        lbuf[stage] = loss
        if axis == "tile":
            length //= fan
            send_all(axis, bits, slot, lambda d: start + rank(axis, bits, d) * length, length, (stage, lslot))
            start = start + rank(axis, bits) * length
            mine = pl.ds(pl.multiple_of(start, 8), length)
            total = o_ref[mine]
            for distance in range(1, fan):
                total = total + recv[slot + distance - 1, pl.ds(0, length)]
            o_ref[mine] = total
        else:
            send_all(axis, bits, slot, lambda d: start, length, (stage, lslot))
            mine = pl.ds(pl.multiple_of(start, 8), length)
            own = o_ref[mine]
            blocks = [own] + [recv[slot + distance - 1, pl.ds(0, length)] for distance in range(1, fan)]
            o_ref[mine] = jnp.where(start < x_ref.shape[1], ordered_sum(blocks, axis, bits), own)
        loss = ordered_sum([loss] + [lrecv[lslot + distance - 1] for distance in range(1, fan)], axis, bits)
        slot += fan - 1
        lslot += fan - 1
    lo_ref[...] = loss
    for bits in reversed(tile_groups):
        fan = 1 << len(bits)
        send_all("tile", bits, slot, lambda d: start, length)
        base = start - rank("tile", bits) * length
        for distance in range(1, fan):
            spot = base + rank("tile", bits, distance) * length
            o_ref[pl.ds(pl.multiple_of(spot, 8), length)] = recv[slot + distance - 1, pl.ds(0, length)]
        start = base
        length *= fan
        slot += fan - 1


def all_reduce(packed, loss_block):
    slots = 2 * (1 + 1 + 7) + 7
    loss_slots = 1 + 1 + 7 + 7
    return pl.pallas_call(
        reduce_kernel,
        out_shape=(
            jax.ShapeDtypeStruct(packed.shape, packed.dtype),
            jax.ShapeDtypeStruct(loss_block.shape, loss_block.dtype),
        ),
        in_specs=[pl.BlockSpec(memory_space=pltpu.VMEM)] * 2,
        out_specs=(pl.BlockSpec(memory_space=pltpu.VMEM), pl.BlockSpec(memory_space=pltpu.VMEM)),
        scratch_shapes=[
            pltpu.VMEM((slots, packed.shape[0] // 2) + packed.shape[1:], packed.dtype),
            pltpu.VMEM((loss_slots,) + loss_block.shape, loss_block.dtype),
            pltpu.VMEM((4,) + loss_block.shape, loss_block.dtype),
            pltpu.SemaphoreType.DMA((slots,)),
            pltpu.SemaphoreType.DMA((slots,)),
            pltpu.SemaphoreType.DMA((loss_slots,)),
            pltpu.SemaphoreType.DMA((loss_slots,)),
        ],
        compiler_params=pltpu.CompilerParams(collective_id=0, has_side_effects=True),
    )(packed, loss_block)

def halo_kernel(x_ref, o_ref, send_sem, recv_sem, local_sem):
    tile_count = lax.axis_size("tile")
    depth = tile_count // 8
    here = lax.axis_index("tile")
    block_x = here // (4 * depth)
    block_y = here // depth % 4
    block_z = here % depth
    zeros = jnp.zeros(o_ref.shape[2:], o_ref.dtype)
    for dz in range(3):
        for dy in range(3):
            if dz != 1 or dy != 1:
                o_ref[dz, dy] = zeros
    locals_ = [
        pltpu.make_async_copy(x_ref.at[u], o_ref.at[1, 1, 1 + u], local_sem.at[u]) for u in range(2)
    ]
    for copy in locals_:
        copy.start()
    sides = (
        (block_y > 0, here - depth),
        (block_y < 3, here + depth),
        (block_z > 0, here - 1),
        (block_z < depth - 1, here + 1),
    )
    barrier = pltpu.get_barrier_semaphore()
    x_partner = (here + 4 * depth) % tile_count
    pl.semaphore_signal(barrier, inc=1, device_id={"tile": x_partner}, device_id_type=MESH)
    for exists, target in sides:
        @pl.when(exists)
        def _():
            pl.semaphore_signal(barrier, inc=1, device_id={"tile": target}, device_id_type=MESH)
    count = 1
    for exists, target in sides:
        count = count + exists.astype(jnp.int32)
    pl.semaphore_wait(barrier, count)
    copy_x = pltpu.make_async_remote_copy(
        src_ref=x_ref.at[1 - block_x],
        dst_ref=o_ref.at[1, 1, 0],
        send_sem=send_sem.at[0],
        recv_sem=recv_sem.at[0],
        device_id={"tile": x_partner},
        device_id_type=MESH,
    )
    copy_x.start()
    for copy in locals_:
        copy.wait()
    copy_x.wait()

    def stage(src, lower_dst, upper_dst, lower, upper, first):
        to_lower = pltpu.make_async_remote_copy(
            src_ref=src,
            dst_ref=upper_dst,
            send_sem=send_sem.at[first],
            recv_sem=recv_sem.at[first + 1],
            device_id={"tile": lower[1]},
            device_id_type=MESH,
        )
        to_upper = pltpu.make_async_remote_copy(
            src_ref=src,
            dst_ref=lower_dst,
            send_sem=send_sem.at[first + 1],
            recv_sem=recv_sem.at[first],
            device_id={"tile": upper[1]},
            device_id_type=MESH,
        )

        @pl.when(lower[0])
        def _():
            to_lower.start()

        @pl.when(upper[0])
        def _():
            to_upper.start()

        @pl.when(lower[0])
        def _():
            to_lower.wait_send()
            to_upper.wait_recv()

        @pl.when(upper[0])
        def _():
            to_upper.wait_send()
            to_lower.wait_recv()

    stage(o_ref.at[1, 1], o_ref.at[1, 0], o_ref.at[1, 2], sides[0], sides[1], 1)
    stage(o_ref.at[1], o_ref.at[0], o_ref.at[2], sides[2], sides[3], 3)


def halo_gather(tiles):
    return pl.pallas_call(
        halo_kernel,
        out_shape=jax.ShapeDtypeStruct((3, 3, 3) + tiles.shape[1:], tiles.dtype),
        in_specs=[pl.BlockSpec(memory_space=pltpu.VMEM)],
        out_specs=pl.BlockSpec(memory_space=pltpu.VMEM),
        scratch_shapes=[
            pltpu.SemaphoreType.DMA((5,)),
            pltpu.SemaphoreType.DMA((5,)),
            pltpu.SemaphoreType.DMA((2,)),
        ],
        compiler_params=pltpu.CompilerParams(collective_id=1, has_side_effects=True),
    )(tiles)


def pair_slope(raw_score, target, weight, heavy_weight, factor):
    chance = jax.nn.sigmoid(raw_score)
    signed = (1.0 - target) * chance - heavy_weight * target * (1.0 - chance)
    return (weight * signed * factor).astype(jnp.bfloat16)


def pair_cost(raw_score, target, weight, heavy_weight):
    missed = heavy_weight * target * jnp.log1p(jnp.exp(-raw_score))
    spurious = (1.0 - target) * jnp.log1p(jnp.exp(raw_score))
    return jnp.sum(weight * (missed + spurious))


def local(features, w_in, w_out, bilinear, partner, counts):
    row_part = features.shape[1]
    feature_width = features.shape[4]
    groups = lax.axis_size("mlp")
    site_rows = row_part * groups
    tile_count = lax.axis_size("tile")
    grid_depth = tile_count // 8
    tile_here = lax.axis_index("tile")
    member = lax.axis_index("mlp")
    block_x = tile_here // (4 * grid_depth)
    block_y = tile_here // grid_depth % 4
    block_z = tile_here % grid_depth
    heavy_weight = 27 * site_rows // 4
    score_scale = feature_width ** (-0.5)
    factor = score_scale / (2 * tile_count * site_rows)
    own_rows = member * row_part + jnp.arange(row_part, dtype=jnp.int32)
    all_rows = jnp.arange(site_rows, dtype=jnp.int32)
    mine_counts = lax.dynamic_index_in_dim(counts, tile_here, 0, keepdims=False)
    mine_partner = lax.dynamic_index_in_dim(partner, tile_here, 0, keepdims=False)
    own_partner = lax.dynamic_slice_in_dim(mine_partner, member * row_part, row_part, 1)
    own_pre_ok = own_rows[None, :] < mine_counts[:, 0:1]
    own_post_ok = own_rows[None, :] < mine_counts[:, 1:2]
    local_x = features.reshape(row_part, 4, feature_width)
    weights = butterfly_gather(jnp.stack([w_in.T, w_out], 1), "mlp")
    own_hidden = jnp.einsum("rcf,hf->rch", local_x, weights[:, 0], preferred_element_type=jnp.float32)
    own_active = jax.nn.gelu(own_hidden).astype(jnp.bfloat16)
    mixed_rows = jnp.einsum("rch,hf->rcf", own_active, weights[:, 1], preferred_element_type=jnp.float32)
    embedded = (local_x.astype(jnp.float32) + mixed_rows).astype(jnp.bfloat16)
    pre_local = embedded[:, 0::2]
    post_local = embedded[:, 1::2]
    query_local = jnp.einsum(
        "ruf,fg->rug", pre_local, bilinear, preferred_element_type=jnp.float32
    ).astype(jnp.bfloat16)

    x_stride = 4 * grid_depth
    y_stride = grid_depth
    query_all = butterfly_gather(query_local, "mlp")
    x_pairs = [(s, (s + x_stride) % tile_count) for s in range(tile_count)]

    def position(s, stride, extent):
        return (s // stride) % extent

    def along_back(arr, stride, extent):
        lower = [(s, s - stride) for s in range(tile_count) if position(s, stride, extent) > 0]
        upper = [(s, s + stride) for s in range(tile_count) if position(s, stride, extent) < extent - 1]
        return arr[1] + lax.ppermute(arr[0], "tile", lower) + lax.ppermute(arr[2], "tile", upper)

    halo = halo_gather(jnp.moveaxis(post_local, 1, 0))
    steps = jnp.arange(3, dtype=jnp.int32) - 1
    dz_grid = steps[:, None]
    dy_grid = steps[None, :]
    inside = (
        (block_y + dy_grid >= 0)
        & (block_y + dy_grid < 4)
        & (block_z + dz_grid >= 0)
        & (block_z + dz_grid < grid_depth)
    )
    near = jnp.clip(tile_here + dy_grid * y_stride + dz_grid, 0, tile_count - 1)
    far = (near + x_stride) % tile_count
    col_counts = jnp.stack(
        [counts[far, block_x, 1], counts[near, 0, 1], counts[near, 1, 1]], -1
    )
    j_ok = inside[..., None, None] & (own_rows < col_counts[..., None])
    loss_sum = jnp.zeros((), jnp.float32)
    post_grad_parts = jnp.zeros(halo.shape, jnp.float32)
    query_grads = []
    place = jnp.arange(3, dtype=jnp.int32)
    code_base = (place[None, None, :] * 9 + (dy_grid[..., None] + 1) * 3 + dz_grid[..., None] + 1) * site_rows
    col_key = (code_base[..., None] + own_rows).reshape(-1)
    for pretile, order, edge in ((0, (0, 1, 2), 0), (1, (1, 2, 0), 2)):
        edge_ok = (block_x == 1) if pretile == 0 else (block_x == 0)
        ordered = halo[:, :, order]
        others = ordered.reshape(-1, feature_width)
        x_ok = jnp.stack([edge_ok if p == edge else jnp.bool_(True) for p in range(3)])
        col_ok = (j_ok[:, :, order] & x_ok[None, None, :, None]).reshape(-1)
        queries = query_all[:, pretile]
        raw_score = (
            jnp.einsum("rf,cf->rc", queries, others, preferred_element_type=jnp.float32)
            * score_scale
        )
        row_ok = all_rows < mine_counts[pretile, 0]
        target = (mine_partner[pretile][:, None] == col_key[None, :]).astype(jnp.float32)
        weight = (row_ok[:, None] & col_ok[None, :]).astype(jnp.float32)
        loss_sum = loss_sum + pair_cost(raw_score, target, weight, heavy_weight)
        slope = pair_slope(raw_score, target, weight, heavy_weight, factor)
        query_grads.append(jnp.dot(slope, others, preferred_element_type=jnp.float32))
        back = jnp.einsum("rc,rf->cf", slope, queries, preferred_element_type=jnp.float32)
        back = back.reshape(ordered.shape)
        for p in range(3):
            post_grad_parts = post_grad_parts.at[:, :, order[p]].add(back[:, :, p])
    post_grad_parts = along_back(along_back(post_grad_parts, 1, grid_depth), y_stride, 4)
    back_x = lax.ppermute(post_grad_parts[0], "tile", x_pairs)
    post_back = jnp.stack(
        [
            post_grad_parts[1] + jnp.where(block_x == 1, back_x, 0.0),
            post_grad_parts[2] + jnp.where(block_x == 0, back_x, 0.0),
        ],
        1,
    )
    query_back = butterfly_scatter(jnp.stack(query_grads, 1), "mlp").astype(jnp.bfloat16)
    bilinear_part = jnp.einsum(
        "ruf,rug->fg", pre_local, query_back, preferred_element_type=jnp.float32
    )
    pre_back = jnp.einsum("rug,fg->ruf", query_back, bilinear, preferred_element_type=jnp.float32)
    embed_grad = jnp.stack(
        [pre_back[:, 0], post_back[:, 0], pre_back[:, 1], post_back[:, 1]], 1
    ).astype(jnp.bfloat16)
    whole_x = butterfly_gather(local_x, "mlp")
    hidden_pre = jnp.einsum("rcf,fh->rch", whole_x, w_in, preferred_element_type=jnp.float32)
    active = jax.nn.gelu(hidden_pre).astype(jnp.bfloat16)
    embed_whole = butterfly_gather(embed_grad, "mlp")
    active_grad = jnp.einsum("rcf,hf->rch", embed_whole, w_out, preferred_element_type=jnp.float32)
    unused, pullback = jax.vjp(jax.nn.gelu, hidden_pre)
    hidden_grad = pullback(active_grad)[0].astype(jnp.bfloat16)
    in_part = jnp.einsum("rcf,rch->fh", whole_x, hidden_grad, preferred_element_type=jnp.float32)
    out_part = jnp.einsum("rch,rcf->hf", active, embed_whole, preferred_element_type=jnp.float32)
    width = bilinear_part.shape[1]
    in_rows = in_part.size // width
    out_rows = out_part.size // width
    packed, loss_block = all_reduce(
        jnp.concatenate([bilinear_part, in_part.reshape(-1, width), out_part.reshape(-1, width)], 0),
        jnp.broadcast_to(loss_sum, (8, 128)),
    )
    grad_bilinear = packed[:width]
    loss_total = loss_block[0, 0]
    grad_in = packed[width : width + in_rows].reshape(in_part.shape)
    grad_out = packed[width + in_rows : width + in_rows + out_rows].reshape(out_part.shape)
    pair_loss = loss_total / (2.0 * tile_count * site_rows * 27 * site_rows)
    return (pair_loss, grad_in, grad_out, grad_bilinear)


def solution(mesh):
    placed = (P("tile", "mlp", None, None, None), P(None, "mlp"), P("mlp", None), P(), P(), P())
    return jax.shard_map(
        local,
        mesh=mesh,
        in_specs=placed,
        out_specs=(P(), P(None, "mlp"), P("mlp", None), P()),
        check_vma=False,
    )
```

```python
import functools

import jax
import jax.numpy as jnp
from jax import lax
from jax.experimental import pallas as pl
from jax.experimental.pallas import tpu as pltpu
from jax.sharding import PartitionSpec as P

column_plan = ((-1, 1), (0, 0), (0, 1), (1, 0))


def shifted(array, axis, by):
    peers = lax.axis_size(axis)
    pairs = [(i, i + by) for i in range(peers) if 0 <= i + by < peers]
    return lax.ppermute(array, axis, pairs)


def butterfly_sum(x, axis):
    peers = lax.axis_size(axis)
    step = 1
    while step < peers:
        x = x + lax.ppermute(x, axis, [(i, i ^ step) for i in range(peers)])
        step *= 2
    return x


def butterfly_gather(x, axis):
    peers = lax.axis_size(axis)
    me = lax.axis_index(axis)
    step = 1
    while step < peers:
        other = lax.ppermute(x, axis, [(i, i ^ step) for i in range(peers)])
        low = (me & step) == 0
        x = jnp.where(low, jnp.concatenate([x, other], 0), jnp.concatenate([other, x], 0))
        step *= 2
    return x


def butterfly_scatter(x, axis):
    peers = lax.axis_size(axis)
    me = lax.axis_index(axis)
    step = peers // 2
    while step >= 1:
        half = x.shape[0] // 2
        upper = (me & step) != 0
        send = jnp.where(upper, x[:half], x[half:])
        keep = jnp.where(upper, x[half:], x[:half])
        x = keep + lax.ppermute(send, axis, [(i, i ^ step) for i in range(peers)])
        step //= 2
    return x


MESH = pl.DeviceIdType.MESH


def flip(index, bit):
    return index + bit - 2 * bit * ((index // bit) % 2)


def reduce_kernel(x_ref, l_ref, o_ref, lo_ref, recv, lrecv, lbuf, send_sem, recv_sem, lsend_sem, lrecv_sem):
    coords = {axis: lax.axis_index(axis) for axis in ("tile", "mlp")}
    tile_groups = ((1,), (2,), (16, 4, 8))
    mlp_bits = (2, 1, 4)

    def partner(axis, bits, distance):
        index = coords[axis]
        for place, bit in enumerate(bits):
            if (distance >> place) & 1:
                index = flip(index, bit)
        return index

    def rank(axis, bits, distance=0):
        total = 0
        for place, bit in enumerate(bits):
            own = (coords[axis] // bit) % 2
            if (distance >> place) & 1:
                own = 1 - own
            total = total + own * (1 << place)
        return total

    def ordered_sum(blocks, axis, bits):
        fan = 1 << len(bits)
        if fan == 2:
            return blocks[0] + blocks[1]
        total = None
        for q in range(fan):
            pick = None
            for distance in range(fan):
                term = jnp.where(rank(axis, bits, distance) == q, blocks[distance], 0.0)
                pick = term if pick is None else pick + term
            total = pick if total is None else total + pick
        return total

    steps = [("tile", bits) for bits in tile_groups] + [("mlp", mlp_bits)]
    barrier = pltpu.get_barrier_semaphore()
    greeted = 0
    for axis, bits in steps:
        for distance in range(1, 1 << len(bits)):
            pl.semaphore_signal(
                barrier, inc=1, device_id={axis: partner(axis, bits, distance)}, device_id_type=MESH
            )
            greeted += 1
    pl.semaphore_wait(barrier, greeted)
    o_ref[...] = x_ref[...]

    def send_all(axis, bits, slot, sources, length, loss_slot=None):
        copies = []
        for distance in range(1, 1 << len(bits)):
            target = {axis: partner(axis, bits, distance)}
            copy = pltpu.make_async_remote_copy(
                src_ref=o_ref.at[pl.ds(pl.multiple_of(sources(distance), 8), length)],
                dst_ref=recv.at[slot + distance - 1, pl.ds(0, length)],
                send_sem=send_sem.at[slot + distance - 1],
                recv_sem=recv_sem.at[slot + distance - 1],
                device_id=target,
                device_id_type=MESH,
            )
            copy.start()
            copies.append(copy)
            if loss_slot is not None:
                copy = pltpu.make_async_remote_copy(
                    src_ref=lbuf.at[loss_slot[0]],
                    dst_ref=lrecv.at[loss_slot[1] + distance - 1],
                    send_sem=lsend_sem.at[loss_slot[1] + distance - 1],
                    recv_sem=lrecv_sem.at[loss_slot[1] + distance - 1],
                    device_id=target,
                    device_id_type=MESH,
                )
                copy.start()
                copies.append(copy)
        for copy in copies:
            copy.wait()

    loss = l_ref[...]
    slot = 0
    lslot = 0
    start = 0
    length = o_ref.shape[0]
    for stage, (axis, bits) in enumerate(steps):
        fan = 1 << len(bits)
        lbuf[stage] = loss
        if axis == "tile":
            length //= fan
            send_all(axis, bits, slot, lambda d: start + rank(axis, bits, d) * length, length, (stage, lslot))
            start = start + rank(axis, bits) * length
            mine = pl.ds(pl.multiple_of(start, 8), length)
            total = o_ref[mine]
            for distance in range(1, fan):
                total = total + recv[slot + distance - 1, pl.ds(0, length)]
            o_ref[mine] = total
        else:
            send_all(axis, bits, slot, lambda d: start, length, (stage, lslot))
            mine = pl.ds(pl.multiple_of(start, 8), length)
            own = o_ref[mine]
            blocks = [own] + [recv[slot + distance - 1, pl.ds(0, length)] for distance in range(1, fan)]
            o_ref[mine] = jnp.where(start < x_ref.shape[1], ordered_sum(blocks, axis, bits), own)
        loss = ordered_sum([loss] + [lrecv[lslot + distance - 1] for distance in range(1, fan)], axis, bits)
        slot += fan - 1
        lslot += fan - 1
    lo_ref[...] = loss
    for bits in reversed(tile_groups):
        fan = 1 << len(bits)
        send_all("tile", bits, slot, lambda d: start, length)
        base = start - rank("tile", bits) * length
        for distance in range(1, fan):
            spot = base + rank("tile", bits, distance) * length
            o_ref[pl.ds(pl.multiple_of(spot, 8), length)] = recv[slot + distance - 1, pl.ds(0, length)]
        start = base
        length *= fan
        slot += fan - 1


def all_reduce(packed, loss_block):
    slots = 2 * (1 + 1 + 7) + 7
    loss_slots = 1 + 1 + 7 + 7
    return pl.pallas_call(
        reduce_kernel,
        out_shape=(
            jax.ShapeDtypeStruct(packed.shape, packed.dtype),
            jax.ShapeDtypeStruct(loss_block.shape, loss_block.dtype),
        ),
        in_specs=[pl.BlockSpec(memory_space=pltpu.VMEM)] * 2,
        out_specs=(pl.BlockSpec(memory_space=pltpu.VMEM), pl.BlockSpec(memory_space=pltpu.VMEM)),
        scratch_shapes=[
            pltpu.VMEM((slots, packed.shape[0] // 2) + packed.shape[1:], packed.dtype),
            pltpu.VMEM((loss_slots,) + loss_block.shape, loss_block.dtype),
            pltpu.VMEM((4,) + loss_block.shape, loss_block.dtype),
            pltpu.SemaphoreType.DMA((slots,)),
            pltpu.SemaphoreType.DMA((slots,)),
            pltpu.SemaphoreType.DMA((loss_slots,)),
            pltpu.SemaphoreType.DMA((loss_slots,)),
        ],
        compiler_params=pltpu.CompilerParams(collective_id=0, has_side_effects=True),
    )(packed, loss_block)

def pair_slope(raw_score, target, weight, heavy_weight, factor):
    chance = jax.nn.sigmoid(raw_score)
    signed = (1.0 - target) * chance - heavy_weight * target * (1.0 - chance)
    return (weight * signed * factor).astype(jnp.bfloat16)


def pair_cost(raw_score, target, weight, heavy_weight):
    missed = heavy_weight * target * jnp.log1p(jnp.exp(-raw_score))
    spurious = (1.0 - target) * jnp.log1p(jnp.exp(raw_score))
    return jnp.sum(weight * (missed + spurious))


def local(features, w_in, w_out, bilinear, partner, counts):
    row_part = features.shape[1]
    feature_width = features.shape[4]
    groups = lax.axis_size("mlp")
    site_rows = row_part * groups
    tile_count = lax.axis_size("tile")
    grid_depth = tile_count // 8
    tile_here = lax.axis_index("tile")
    member = lax.axis_index("mlp")
    block_x = tile_here // (4 * grid_depth)
    block_y = tile_here // grid_depth % 4
    block_z = tile_here % grid_depth
    heavy_weight = 27 * site_rows // 4
    score_scale = feature_width ** (-0.5)
    factor = score_scale / (2 * tile_count * site_rows)
    own_rows = member * row_part + jnp.arange(row_part, dtype=jnp.int32)
    all_rows = jnp.arange(site_rows, dtype=jnp.int32)
    mine_counts = lax.dynamic_index_in_dim(counts, tile_here, 0, keepdims=False)
    mine_partner = lax.dynamic_index_in_dim(partner, tile_here, 0, keepdims=False)
    own_partner = lax.dynamic_slice_in_dim(mine_partner, member * row_part, row_part, 1)
    own_pre_ok = own_rows[None, :] < mine_counts[:, 0:1]
    own_post_ok = own_rows[None, :] < mine_counts[:, 1:2]
    local_x = features.reshape(row_part, 4, feature_width)
    weights = butterfly_gather(jnp.stack([w_in.T, w_out], 1), "mlp")
    own_hidden = jnp.einsum("rcf,hf->rch", local_x, weights[:, 0], preferred_element_type=jnp.float32)
    own_active = jax.nn.gelu(own_hidden).astype(jnp.bfloat16)
    mixed_rows = jnp.einsum("rch,hf->rcf", own_active, weights[:, 1], preferred_element_type=jnp.float32)
    embedded = (local_x.astype(jnp.float32) + mixed_rows).astype(jnp.bfloat16)
    pre_local = embedded[:, 0::2]
    post_local = embedded[:, 1::2]
    query_local = jnp.einsum(
        "ruf,fg->rug", pre_local, bilinear, preferred_element_type=jnp.float32
    ).astype(jnp.bfloat16)

    x_stride = 4 * grid_depth
    y_stride = grid_depth
    query_all = butterfly_gather(query_local, "mlp")
    facing = jnp.where(block_x == 0, post_local[:, 1], post_local[:, 0])
    x_pairs = [(s, (s + x_stride) % tile_count) for s in range(tile_count)]
    from_x = lax.ppermute(facing, "tile", x_pairs)
    halo = jnp.stack([from_x, post_local[:, 0], post_local[:, 1]], 0)

    def position(s, stride, extent):
        return (s // stride) % extent

    def along(arr, stride, extent):
        lower = [(s, s + stride) for s in range(tile_count) if position(s, stride, extent) < extent - 1]
        upper = [(s, s - stride) for s in range(tile_count) if position(s, stride, extent) > 0]
        return jnp.stack(
            [lax.ppermute(arr, "tile", lower), arr, lax.ppermute(arr, "tile", upper)], 0
        )

    def along_back(arr, stride, extent):
        lower = [(s, s - stride) for s in range(tile_count) if position(s, stride, extent) > 0]
        upper = [(s, s + stride) for s in range(tile_count) if position(s, stride, extent) < extent - 1]
        return arr[1] + lax.ppermute(arr[0], "tile", lower) + lax.ppermute(arr[2], "tile", upper)

    halo = along(along(halo, y_stride, 4), 1, grid_depth)
    steps = jnp.arange(3, dtype=jnp.int32) - 1
    dz_grid = steps[:, None]
    dy_grid = steps[None, :]
    inside = (
        (block_y + dy_grid >= 0)
        & (block_y + dy_grid < 4)
        & (block_z + dz_grid >= 0)
        & (block_z + dz_grid < grid_depth)
    )
    near = jnp.clip(tile_here + dy_grid * y_stride + dz_grid, 0, tile_count - 1)
    far = (near + x_stride) % tile_count
    col_counts = jnp.stack(
        [counts[far, block_x, 1], counts[near, 0, 1], counts[near, 1, 1]], -1
    )
    j_ok = inside[..., None, None] & (own_rows < col_counts[..., None])
    loss_sum = jnp.zeros((), jnp.float32)
    post_grad_parts = jnp.zeros(halo.shape, jnp.float32)
    query_grads = []
    place = jnp.arange(3, dtype=jnp.int32)
    code_base = (place[None, None, :] * 9 + (dy_grid[..., None] + 1) * 3 + dz_grid[..., None] + 1) * site_rows
    col_key = (code_base[..., None] + own_rows).reshape(-1)
    for pretile, order, edge in ((0, (0, 1, 2), 0), (1, (1, 2, 0), 2)):
        edge_ok = (block_x == 1) if pretile == 0 else (block_x == 0)
        ordered = halo[:, :, order]
        others = ordered.reshape(-1, feature_width)
        x_ok = jnp.stack([edge_ok if p == edge else jnp.bool_(True) for p in range(3)])
        col_ok = (j_ok[:, :, order] & x_ok[None, None, :, None]).reshape(-1)
        queries = query_all[:, pretile]
        raw_score = (
            jnp.einsum("rf,cf->rc", queries, others, preferred_element_type=jnp.float32)
            * score_scale
        )
        row_ok = all_rows < mine_counts[pretile, 0]
        target = (mine_partner[pretile][:, None] == col_key[None, :]).astype(jnp.float32)
        weight = (row_ok[:, None] & col_ok[None, :]).astype(jnp.float32)
        decay = jnp.exp(-jnp.abs(raw_score))
        soft = jnp.log1p(decay)
        inverse = 1.0 / (1.0 + decay)
        ahead = raw_score >= 0
        missed = heavy_weight * target * (jnp.maximum(-raw_score, 0.0) + soft)
        spurious = (1.0 - target) * (jnp.maximum(raw_score, 0.0) + soft)
        loss_sum = loss_sum + jnp.sum(weight * (missed + spurious))
        chance = jnp.where(ahead, inverse, decay * inverse)
        doubt = jnp.where(ahead, decay * inverse, inverse)
        signed = (1.0 - target) * chance - heavy_weight * target * doubt
        slope = (weight * signed * factor).astype(jnp.bfloat16)
        query_grads.append(jnp.dot(slope, others, preferred_element_type=jnp.float32))
        back = jnp.einsum("rc,rf->cf", slope, queries, preferred_element_type=jnp.float32)
        back = back.reshape(ordered.shape)
        for p in range(3):
            post_grad_parts = post_grad_parts.at[:, :, order[p]].add(back[:, :, p])
    post_grad_parts = along_back(along_back(post_grad_parts, 1, grid_depth), y_stride, 4)
    back_x = lax.ppermute(post_grad_parts[0], "tile", x_pairs)
    post_back = jnp.stack(
        [
            post_grad_parts[1] + jnp.where(block_x == 1, back_x, 0.0),
            post_grad_parts[2] + jnp.where(block_x == 0, back_x, 0.0),
        ],
        1,
    )
    query_back = butterfly_scatter(jnp.stack(query_grads, 1), "mlp").astype(jnp.bfloat16)
    bilinear_part = jnp.einsum(
        "ruf,rug->fg", pre_local, query_back, preferred_element_type=jnp.float32
    )
    pre_back = jnp.einsum("rug,fg->ruf", query_back, bilinear, preferred_element_type=jnp.float32)
    embed_grad = jnp.stack(
        [pre_back[:, 0], post_back[:, 0], pre_back[:, 1], post_back[:, 1]], 1
    ).astype(jnp.bfloat16)
    whole_x = butterfly_gather(local_x, "mlp")
    hidden_pre = jnp.einsum("rcf,fh->rch", whole_x, w_in, preferred_element_type=jnp.float32)
    active = jax.nn.gelu(hidden_pre).astype(jnp.bfloat16)
    embed_whole = butterfly_gather(embed_grad, "mlp")
    active_grad = jnp.einsum("rcf,hf->rch", embed_whole, w_out, preferred_element_type=jnp.float32)
    unused, pullback = jax.vjp(jax.nn.gelu, hidden_pre)
    hidden_grad = pullback(active_grad)[0].astype(jnp.bfloat16)
    in_part = jnp.einsum("rcf,rch->fh", whole_x, hidden_grad, preferred_element_type=jnp.float32)
    out_part = jnp.einsum("rch,rcf->hf", active, embed_whole, preferred_element_type=jnp.float32)
    width = bilinear_part.shape[1]
    in_rows = in_part.size // width
    out_rows = out_part.size // width
    packed, loss_block = all_reduce(
        jnp.concatenate([bilinear_part, in_part.reshape(-1, width), out_part.reshape(-1, width)], 0),
        jnp.broadcast_to(loss_sum, (8, 128)),
    )
    grad_bilinear = packed[:width]
    loss_total = loss_block[0, 0]
    grad_in = packed[width : width + in_rows].reshape(in_part.shape)
    grad_out = packed[width + in_rows : width + in_rows + out_rows].reshape(out_part.shape)
    pair_loss = loss_total / (2.0 * tile_count * site_rows * 27 * site_rows)
    return (pair_loss, grad_in, grad_out, grad_bilinear)


def solution(mesh):
    placed = (P("tile", "mlp", None, None, None), P(None, "mlp"), P("mlp", None), P(), P(), P())
    return jax.shard_map(
        local,
        mesh=mesh,
        in_specs=placed,
        out_specs=(P(), P(None, "mlp"), P("mlp", None), P()),
        check_vma=False,
    )
```

```python
import functools

import jax
import jax.numpy as jnp
from jax import lax
from jax.experimental import pallas as pl
from jax.experimental.pallas import tpu as pltpu
from jax.sharding import PartitionSpec as P

column_plan = ((-1, 1), (0, 0), (0, 1), (1, 0))


def shifted(array, axis, by):
    peers = lax.axis_size(axis)
    pairs = [(i, i + by) for i in range(peers) if 0 <= i + by < peers]
    return lax.ppermute(array, axis, pairs)


def butterfly_sum(x, axis):
    peers = lax.axis_size(axis)
    step = 1
    while step < peers:
        x = x + lax.ppermute(x, axis, [(i, i ^ step) for i in range(peers)])
        step *= 2
    return x


def butterfly_gather(x, axis, order=(4, 1, 2)):
    peers = lax.axis_size(axis)
    me = lax.axis_index(axis)
    done = []
    for bit in order:
        other = lax.ppermute(x, axis, [(i, i ^ bit) for i in range(peers)])
        low = (me // bit) % 2 == 0
        x = jnp.where(low, jnp.stack([x, other], 0), jnp.stack([other, x], 0))
        done.insert(0, bit)
    count = len(done)
    axes = sorted(range(count), key=lambda place: -done[place])
    x = x.transpose(axes + list(range(count, x.ndim)))
    return x.reshape((-1,) + x.shape[count + 1 :])


def butterfly_scatter(x, axis, order=(2, 1, 4)):
    peers = lax.axis_size(axis)
    me = lax.axis_index(axis)
    bits = sorted(order, reverse=True)
    x = x.reshape((2,) * len(bits) + (x.shape[0] // peers,) + x.shape[1:])
    for bit in order:
        place = bits.index(bit)
        upper = (me // bit) % 2 == 1
        lower_half = lax.index_in_dim(x, 0, place, keepdims=False)
        upper_half = lax.index_in_dim(x, 1, place, keepdims=False)
        send = jnp.where(upper, lower_half, upper_half)
        keep = jnp.where(upper, upper_half, lower_half)
        x = keep + lax.ppermute(send, axis, [(i, i ^ bit) for i in range(peers)])
        bits.remove(bit)
    return x

MESH = pl.DeviceIdType.MESH


def flip(index, bit):
    return index + bit - 2 * bit * ((index // bit) % 2)


def reduce_kernel(x_ref, l_ref, o_ref, lo_ref, recv, lrecv, lbuf, send_sem, recv_sem, lsend_sem, lrecv_sem):
    coords = {axis: lax.axis_index(axis) for axis in ("tile", "mlp")}
    tile_groups = ((1,), (2,), (16, 4, 8))
    mlp_bits = (2, 1, 4)

    def partner(axis, bits, distance):
        index = coords[axis]
        for place, bit in enumerate(bits):
            if (distance >> place) & 1:
                index = flip(index, bit)
        return index

    def rank(axis, bits, distance=0):
        total = 0
        for place, bit in enumerate(bits):
            own = (coords[axis] // bit) % 2
            if (distance >> place) & 1:
                own = 1 - own
            total = total + own * (1 << place)
        return total

    def ordered_sum(blocks, axis, bits):
        fan = 1 << len(bits)
        if fan == 2:
            return blocks[0] + blocks[1]
        total = None
        for q in range(fan):
            pick = None
            for distance in range(fan):
                term = jnp.where(rank(axis, bits, distance) == q, blocks[distance], 0.0)
                pick = term if pick is None else pick + term
            total = pick if total is None else total + pick
        return total

    steps = [("tile", bits) for bits in tile_groups] + [("mlp", mlp_bits)]
    barrier = pltpu.get_barrier_semaphore()
    greeted = 0
    for axis, bits in steps:
        for distance in range(1, 1 << len(bits)):
            pl.semaphore_signal(
                barrier, inc=1, device_id={axis: partner(axis, bits, distance)}, device_id_type=MESH
            )
            greeted += 1
    pl.semaphore_wait(barrier, greeted)
    o_ref[...] = x_ref[...]

    def send_all(axis, bits, slot, sources, length, loss_slot=None):
        copies = []
        for distance in range(1, 1 << len(bits)):
            target = {axis: partner(axis, bits, distance)}
            copy = pltpu.make_async_remote_copy(
                src_ref=o_ref.at[pl.ds(pl.multiple_of(sources(distance), 8), length)],
                dst_ref=recv.at[slot + distance - 1, pl.ds(0, length)],
                send_sem=send_sem.at[slot + distance - 1],
                recv_sem=recv_sem.at[slot + distance - 1],
                device_id=target,
                device_id_type=MESH,
            )
            copy.start()
            copies.append(copy)
            if loss_slot is not None:
                copy = pltpu.make_async_remote_copy(
                    src_ref=lbuf.at[loss_slot[0]],
                    dst_ref=lrecv.at[loss_slot[1] + distance - 1],
                    send_sem=lsend_sem.at[loss_slot[1] + distance - 1],
                    recv_sem=lrecv_sem.at[loss_slot[1] + distance - 1],
                    device_id=target,
                    device_id_type=MESH,
                )
                copy.start()
                copies.append(copy)
        for copy in copies:
            copy.wait()

    loss = l_ref[...]
    slot = 0
    lslot = 0
    start = 0
    length = o_ref.shape[0]
    for stage, (axis, bits) in enumerate(steps):
        fan = 1 << len(bits)
        lbuf[stage] = loss
        if axis == "tile":
            length //= fan
            send_all(axis, bits, slot, lambda d: start + rank(axis, bits, d) * length, length, (stage, lslot))
            start = start + rank(axis, bits) * length
            mine = pl.ds(pl.multiple_of(start, 8), length)
            total = o_ref[mine]
            for distance in range(1, fan):
                total = total + recv[slot + distance - 1, pl.ds(0, length)]
            o_ref[mine] = total
        else:
            send_all(axis, bits, slot, lambda d: start, length, (stage, lslot))
            mine = pl.ds(pl.multiple_of(start, 8), length)
            own = o_ref[mine]
            blocks = [own] + [recv[slot + distance - 1, pl.ds(0, length)] for distance in range(1, fan)]
            o_ref[mine] = jnp.where(start < x_ref.shape[1], ordered_sum(blocks, axis, bits), own)
        loss = ordered_sum([loss] + [lrecv[lslot + distance - 1] for distance in range(1, fan)], axis, bits)
        slot += fan - 1
        lslot += fan - 1
    lo_ref[...] = loss
    for bits in reversed(tile_groups):
        fan = 1 << len(bits)
        send_all("tile", bits, slot, lambda d: start, length)
        base = start - rank("tile", bits) * length
        for distance in range(1, fan):
            spot = base + rank("tile", bits, distance) * length
            o_ref[pl.ds(pl.multiple_of(spot, 8), length)] = recv[slot + distance - 1, pl.ds(0, length)]
        start = base
        length *= fan
        slot += fan - 1


def all_reduce(packed, loss_block):
    slots = 2 * (1 + 1 + 7) + 7
    loss_slots = 1 + 1 + 7 + 7
    return pl.pallas_call(
        reduce_kernel,
        out_shape=(
            jax.ShapeDtypeStruct(packed.shape, packed.dtype),
            jax.ShapeDtypeStruct(loss_block.shape, loss_block.dtype),
        ),
        in_specs=[pl.BlockSpec(memory_space=pltpu.VMEM)] * 2,
        out_specs=(pl.BlockSpec(memory_space=pltpu.VMEM), pl.BlockSpec(memory_space=pltpu.VMEM)),
        scratch_shapes=[
            pltpu.VMEM((slots, packed.shape[0] // 2) + packed.shape[1:], packed.dtype),
            pltpu.VMEM((loss_slots,) + loss_block.shape, loss_block.dtype),
            pltpu.VMEM((4,) + loss_block.shape, loss_block.dtype),
            pltpu.SemaphoreType.DMA((slots,)),
            pltpu.SemaphoreType.DMA((slots,)),
            pltpu.SemaphoreType.DMA((loss_slots,)),
            pltpu.SemaphoreType.DMA((loss_slots,)),
        ],
        compiler_params=pltpu.CompilerParams(collective_id=0, has_side_effects=True),
    )(packed, loss_block)

def pair_slope(raw_score, target, weight, heavy_weight, factor):
    chance = jax.nn.sigmoid(raw_score)
    signed = (1.0 - target) * chance - heavy_weight * target * (1.0 - chance)
    return (weight * signed * factor).astype(jnp.bfloat16)


def pair_cost(raw_score, target, weight, heavy_weight):
    missed = heavy_weight * target * jnp.log1p(jnp.exp(-raw_score))
    spurious = (1.0 - target) * jnp.log1p(jnp.exp(raw_score))
    return jnp.sum(weight * (missed + spurious))


def local(features, w_in, w_out, bilinear, partner, counts):
    row_part = features.shape[1]
    feature_width = features.shape[4]
    groups = lax.axis_size("mlp")
    site_rows = row_part * groups
    tile_count = lax.axis_size("tile")
    grid_depth = tile_count // 8
    tile_here = lax.axis_index("tile")
    member = lax.axis_index("mlp")
    block_x = tile_here // (4 * grid_depth)
    block_y = tile_here // grid_depth % 4
    block_z = tile_here % grid_depth
    heavy_weight = 27 * site_rows // 4
    score_scale = feature_width ** (-0.5)
    factor = score_scale / (2 * tile_count * site_rows)
    own_rows = member * row_part + jnp.arange(row_part, dtype=jnp.int32)
    all_rows = jnp.arange(site_rows, dtype=jnp.int32)
    mine_counts = lax.dynamic_index_in_dim(counts, tile_here, 0, keepdims=False)
    mine_partner = lax.dynamic_index_in_dim(partner, tile_here, 0, keepdims=False)
    own_partner = lax.dynamic_slice_in_dim(mine_partner, member * row_part, row_part, 1)
    own_pre_ok = own_rows[None, :] < mine_counts[:, 0:1]
    own_post_ok = own_rows[None, :] < mine_counts[:, 1:2]
    local_x = features.reshape(row_part, 4, feature_width)
    weights = butterfly_gather(jnp.stack([w_in.T, w_out], 1), "mlp")
    own_hidden = jnp.einsum("rcf,hf->rch", local_x, weights[:, 0], preferred_element_type=jnp.float32)
    own_active = jax.nn.gelu(own_hidden).astype(jnp.bfloat16)
    mixed_rows = jnp.einsum("rch,hf->rcf", own_active, weights[:, 1], preferred_element_type=jnp.float32)
    embedded = (local_x.astype(jnp.float32) + mixed_rows).astype(jnp.bfloat16)
    pre_local = embedded[:, 0::2]
    post_local = embedded[:, 1::2]
    query_local = jnp.einsum(
        "ruf,fg->rug", pre_local, bilinear, preferred_element_type=jnp.float32
    ).astype(jnp.bfloat16)

    x_stride = 4 * grid_depth
    y_stride = grid_depth
    query_all = butterfly_gather(query_local, "mlp")
    facing = jnp.where(block_x == 0, post_local[:, 1], post_local[:, 0])
    x_pairs = [(s, (s + x_stride) % tile_count) for s in range(tile_count)]
    from_x = lax.ppermute(facing, "tile", x_pairs)
    halo = jnp.stack([from_x, post_local[:, 0], post_local[:, 1]], 0)

    def position(s, stride, extent):
        return (s // stride) % extent

    def along(arr, stride, extent):
        lower = [(s, s + stride) for s in range(tile_count) if position(s, stride, extent) < extent - 1]
        upper = [(s, s - stride) for s in range(tile_count) if position(s, stride, extent) > 0]
        return jnp.stack(
            [lax.ppermute(arr, "tile", lower), arr, lax.ppermute(arr, "tile", upper)], 0
        )

    def along_back(arr, stride, extent):
        lower = [(s, s - stride) for s in range(tile_count) if position(s, stride, extent) > 0]
        upper = [(s, s + stride) for s in range(tile_count) if position(s, stride, extent) < extent - 1]
        return arr[1] + lax.ppermute(arr[0], "tile", lower) + lax.ppermute(arr[2], "tile", upper)

    halo = along(along(halo, y_stride, 4), 1, grid_depth)
    steps = jnp.arange(3, dtype=jnp.int32) - 1
    dz_grid = steps[:, None]
    dy_grid = steps[None, :]
    inside = (
        (block_y + dy_grid >= 0)
        & (block_y + dy_grid < 4)
        & (block_z + dz_grid >= 0)
        & (block_z + dz_grid < grid_depth)
    )
    near = jnp.clip(tile_here + dy_grid * y_stride + dz_grid, 0, tile_count - 1)
    far = (near + x_stride) % tile_count
    col_counts = jnp.stack(
        [counts[far, block_x, 1], counts[near, 0, 1], counts[near, 1, 1]], -1
    )
    j_ok = inside[..., None, None] & (own_rows < col_counts[..., None])
    loss_sum = jnp.zeros((), jnp.float32)
    post_grad_parts = jnp.zeros(halo.shape, jnp.float32)
    query_grads = []
    place = jnp.arange(3, dtype=jnp.int32)
    code_base = (place[None, None, :] * 9 + (dy_grid[..., None] + 1) * 3 + dz_grid[..., None] + 1) * site_rows
    col_key = (code_base[..., None] + own_rows).reshape(-1)
    for pretile, order, edge in ((0, (0, 1, 2), 0), (1, (1, 2, 0), 2)):
        edge_ok = (block_x == 1) if pretile == 0 else (block_x == 0)
        ordered = halo[:, :, order]
        others = ordered.reshape(-1, feature_width)
        x_ok = jnp.stack([edge_ok if p == edge else jnp.bool_(True) for p in range(3)])
        col_ok = (j_ok[:, :, order] & x_ok[None, None, :, None]).reshape(-1)
        queries = query_all[:, pretile]
        raw_score = (
            jnp.einsum("rf,cf->rc", queries, others, preferred_element_type=jnp.float32)
            * score_scale
        )
        row_ok = all_rows < mine_counts[pretile, 0]
        target = (mine_partner[pretile][:, None] == col_key[None, :]).astype(jnp.float32)
        weight = (row_ok[:, None] & col_ok[None, :]).astype(jnp.float32)
        loss_sum = loss_sum + pair_cost(raw_score, target, weight, heavy_weight)
        slope = pair_slope(raw_score, target, weight, heavy_weight, factor)
        query_grads.append(jnp.dot(slope, others, preferred_element_type=jnp.float32))
        back = jnp.einsum("rc,rf->cf", slope, queries, preferred_element_type=jnp.float32)
        back = back.reshape(ordered.shape)
        for p in range(3):
            post_grad_parts = post_grad_parts.at[:, :, order[p]].add(back[:, :, p])
    post_grad_parts = along_back(along_back(post_grad_parts, 1, grid_depth), y_stride, 4)
    back_x = lax.ppermute(post_grad_parts[0], "tile", x_pairs)
    post_back = jnp.stack(
        [
            post_grad_parts[1] + jnp.where(block_x == 1, back_x, 0.0),
            post_grad_parts[2] + jnp.where(block_x == 0, back_x, 0.0),
        ],
        1,
    )
    query_back = butterfly_scatter(jnp.stack(query_grads, 1), "mlp").astype(jnp.bfloat16)
    bilinear_part = jnp.einsum(
        "ruf,rug->fg", pre_local, query_back, preferred_element_type=jnp.float32
    )
    pre_back = jnp.einsum("rug,fg->ruf", query_back, bilinear, preferred_element_type=jnp.float32)
    embed_grad = jnp.stack(
        [pre_back[:, 0], post_back[:, 0], pre_back[:, 1], post_back[:, 1]], 1
    ).astype(jnp.bfloat16)
    whole_x = butterfly_gather(local_x, "mlp")
    hidden_pre = jnp.einsum("rcf,fh->rch", whole_x, w_in, preferred_element_type=jnp.float32)
    active = jax.nn.gelu(hidden_pre).astype(jnp.bfloat16)
    embed_whole = butterfly_gather(embed_grad, "mlp")
    active_grad = jnp.einsum("rcf,hf->rch", embed_whole, w_out, preferred_element_type=jnp.float32)
    unused, pullback = jax.vjp(jax.nn.gelu, hidden_pre)
    hidden_grad = pullback(active_grad)[0].astype(jnp.bfloat16)
    in_part = jnp.einsum("rcf,rch->fh", whole_x, hidden_grad, preferred_element_type=jnp.float32)
    out_part = jnp.einsum("rch,rcf->hf", active, embed_whole, preferred_element_type=jnp.float32)
    width = bilinear_part.shape[1]
    in_rows = in_part.size // width
    out_rows = out_part.size // width
    packed, loss_block = all_reduce(
        jnp.concatenate([bilinear_part, in_part.reshape(-1, width), out_part.reshape(-1, width)], 0),
        jnp.broadcast_to(loss_sum, (8, 128)),
    )
    grad_bilinear = packed[:width]
    loss_total = loss_block[0, 0]
    grad_in = packed[width : width + in_rows].reshape(in_part.shape)
    grad_out = packed[width + in_rows : width + in_rows + out_rows].reshape(out_part.shape)
    pair_loss = loss_total / (2.0 * tile_count * site_rows * 27 * site_rows)
    return (pair_loss, grad_in, grad_out, grad_bilinear)


def solution(mesh):
    placed = (P("tile", "mlp", None, None, None), P(None, "mlp"), P("mlp", None), P(), P(), P())
    return jax.shard_map(
        local,
        mesh=mesh,
        in_specs=placed,
        out_specs=(P(), P(None, "mlp"), P("mlp", None), P()),
        check_vma=False,
    )
```

```python
import functools

import jax
import jax.numpy as jnp
from jax import lax
from jax.experimental import pallas as pl
from jax.experimental.pallas import tpu as pltpu
from jax.sharding import PartitionSpec as P

column_plan = ((-1, 1), (0, 0), (0, 1), (1, 0))


def shifted(array, axis, by):
    peers = lax.axis_size(axis)
    pairs = [(i, i + by) for i in range(peers) if 0 <= i + by < peers]
    return lax.ppermute(array, axis, pairs)


def butterfly_sum(x, axis):
    peers = lax.axis_size(axis)
    step = 1
    while step < peers:
        x = x + lax.ppermute(x, axis, [(i, i ^ step) for i in range(peers)])
        step *= 2
    return x


def butterfly_gather(x, axis):
    peers = lax.axis_size(axis)
    me = lax.axis_index(axis)
    step = 1
    while step < peers:
        other = lax.ppermute(x, axis, [(i, i ^ step) for i in range(peers)])
        low = (me & step) == 0
        x = jnp.where(low, jnp.concatenate([x, other], 0), jnp.concatenate([other, x], 0))
        step *= 2
    return x


def butterfly_scatter(x, axis, order=(2, 1, 4)):
    peers = lax.axis_size(axis)
    me = lax.axis_index(axis)
    bits = sorted(order, reverse=True)
    x = x.reshape((2,) * len(bits) + (x.shape[0] // peers,) + x.shape[1:])
    for bit in order:
        place = bits.index(bit)
        upper = (me // bit) % 2 == 1
        lower_half = lax.index_in_dim(x, 0, place, keepdims=False)
        upper_half = lax.index_in_dim(x, 1, place, keepdims=False)
        send = jnp.where(upper, lower_half, upper_half)
        keep = jnp.where(upper, upper_half, lower_half)
        x = keep + lax.ppermute(send, axis, [(i, i ^ bit) for i in range(peers)])
        bits.remove(bit)
    return x

MESH = pl.DeviceIdType.MESH


def flip(index, bit):
    return index + bit - 2 * bit * ((index // bit) % 2)


def reduce_kernel(x_ref, l_ref, o_ref, lo_ref, recv, lrecv, lbuf, send_sem, recv_sem, lsend_sem, lrecv_sem):
    coords = {axis: lax.axis_index(axis) for axis in ("tile", "mlp")}
    tile_groups = ((1,), (2,), (16, 4, 8))
    mlp_bits = (2, 1, 4)

    def partner(axis, bits, distance):
        index = coords[axis]
        for place, bit in enumerate(bits):
            if (distance >> place) & 1:
                index = flip(index, bit)
        return index

    def rank(axis, bits, distance=0):
        total = 0
        for place, bit in enumerate(bits):
            own = (coords[axis] // bit) % 2
            if (distance >> place) & 1:
                own = 1 - own
            total = total + own * (1 << place)
        return total

    def ordered_sum(blocks, axis, bits):
        fan = 1 << len(bits)
        if fan == 2:
            return blocks[0] + blocks[1]
        total = None
        for q in range(fan):
            pick = None
            for distance in range(fan):
                term = jnp.where(rank(axis, bits, distance) == q, blocks[distance], 0.0)
                pick = term if pick is None else pick + term
            total = pick if total is None else total + pick
        return total

    steps = [("tile", bits) for bits in tile_groups] + [("mlp", mlp_bits)]
    barrier = pltpu.get_barrier_semaphore()
    greeted = 0
    for axis, bits in steps:
        for distance in range(1, 1 << len(bits)):
            pl.semaphore_signal(
                barrier, inc=1, device_id={axis: partner(axis, bits, distance)}, device_id_type=MESH
            )
            greeted += 1
    pl.semaphore_wait(barrier, greeted)
    o_ref[...] = x_ref[...]

    def send_all(axis, bits, slot, sources, length, loss_slot=None):
        copies = []
        for distance in range(1, 1 << len(bits)):
            target = {axis: partner(axis, bits, distance)}
            copy = pltpu.make_async_remote_copy(
                src_ref=o_ref.at[pl.ds(pl.multiple_of(sources(distance), 8), length)],
                dst_ref=recv.at[slot + distance - 1, pl.ds(0, length)],
                send_sem=send_sem.at[slot + distance - 1],
                recv_sem=recv_sem.at[slot + distance - 1],
                device_id=target,
                device_id_type=MESH,
            )
            copy.start()
            copies.append(copy)
            if loss_slot is not None:
                copy = pltpu.make_async_remote_copy(
                    src_ref=lbuf.at[loss_slot[0]],
                    dst_ref=lrecv.at[loss_slot[1] + distance - 1],
                    send_sem=lsend_sem.at[loss_slot[1] + distance - 1],
                    recv_sem=lrecv_sem.at[loss_slot[1] + distance - 1],
                    device_id=target,
                    device_id_type=MESH,
                )
                copy.start()
                copies.append(copy)
        for copy in copies:
            copy.wait()

    loss = l_ref[...]
    slot = 0
    lslot = 0
    start = 0
    length = o_ref.shape[0]
    for stage, (axis, bits) in enumerate(steps):
        fan = 1 << len(bits)
        lbuf[stage] = loss
        if axis == "tile":
            length //= fan
            send_all(axis, bits, slot, lambda d: start + rank(axis, bits, d) * length, length, (stage, lslot))
            start = start + rank(axis, bits) * length
            mine = pl.ds(pl.multiple_of(start, 8), length)
            total = o_ref[mine]
            for distance in range(1, fan):
                total = total + recv[slot + distance - 1, pl.ds(0, length)]
            o_ref[mine] = total
        else:
            send_all(axis, bits, slot, lambda d: start, length, (stage, lslot))
            mine = pl.ds(pl.multiple_of(start, 8), length)
            own = o_ref[mine]
            blocks = [own] + [recv[slot + distance - 1, pl.ds(0, length)] for distance in range(1, fan)]
            o_ref[mine] = jnp.where(start < x_ref.shape[1], ordered_sum(blocks, axis, bits), own)
        loss = ordered_sum([loss] + [lrecv[lslot + distance - 1] for distance in range(1, fan)], axis, bits)
        slot += fan - 1
        lslot += fan - 1
    lo_ref[...] = loss
    for bits in reversed(tile_groups):
        fan = 1 << len(bits)
        send_all("tile", bits, slot, lambda d: start, length)
        base = start - rank("tile", bits) * length
        for distance in range(1, fan):
            spot = base + rank("tile", bits, distance) * length
            o_ref[pl.ds(pl.multiple_of(spot, 8), length)] = recv[slot + distance - 1, pl.ds(0, length)]
        start = base
        length *= fan
        slot += fan - 1


def all_reduce(packed, loss_block):
    slots = 2 * (1 + 1 + 7) + 7
    loss_slots = 1 + 1 + 7 + 7
    return pl.pallas_call(
        reduce_kernel,
        out_shape=(
            jax.ShapeDtypeStruct(packed.shape, packed.dtype),
            jax.ShapeDtypeStruct(loss_block.shape, loss_block.dtype),
        ),
        in_specs=[pl.BlockSpec(memory_space=pltpu.VMEM)] * 2,
        out_specs=(pl.BlockSpec(memory_space=pltpu.VMEM), pl.BlockSpec(memory_space=pltpu.VMEM)),
        scratch_shapes=[
            pltpu.VMEM((slots, packed.shape[0] // 2) + packed.shape[1:], packed.dtype),
            pltpu.VMEM((loss_slots,) + loss_block.shape, loss_block.dtype),
            pltpu.VMEM((4,) + loss_block.shape, loss_block.dtype),
            pltpu.SemaphoreType.DMA((slots,)),
            pltpu.SemaphoreType.DMA((slots,)),
            pltpu.SemaphoreType.DMA((loss_slots,)),
            pltpu.SemaphoreType.DMA((loss_slots,)),
        ],
        compiler_params=pltpu.CompilerParams(collective_id=0, has_side_effects=True),
    )(packed, loss_block)

def pair_slope(raw_score, target, weight, heavy_weight, factor):
    chance = jax.nn.sigmoid(raw_score)
    signed = (1.0 - target) * chance - heavy_weight * target * (1.0 - chance)
    return (weight * signed * factor).astype(jnp.bfloat16)


def pair_cost(raw_score, target, weight, heavy_weight):
    missed = heavy_weight * target * jnp.log1p(jnp.exp(-raw_score))
    spurious = (1.0 - target) * jnp.log1p(jnp.exp(raw_score))
    return jnp.sum(weight * (missed + spurious))


def local(features, w_in, w_out, bilinear, partner, counts):
    row_part = features.shape[1]
    feature_width = features.shape[4]
    groups = lax.axis_size("mlp")
    site_rows = row_part * groups
    tile_count = lax.axis_size("tile")
    grid_depth = tile_count // 8
    tile_here = lax.axis_index("tile")
    member = lax.axis_index("mlp")
    block_x = tile_here // (4 * grid_depth)
    block_y = tile_here // grid_depth % 4
    block_z = tile_here % grid_depth
    heavy_weight = 27 * site_rows // 4
    score_scale = feature_width ** (-0.5)
    factor = score_scale / (2 * tile_count * site_rows)
    own_rows = member * row_part + jnp.arange(row_part, dtype=jnp.int32)
    all_rows = jnp.arange(site_rows, dtype=jnp.int32)
    mine_counts = lax.dynamic_index_in_dim(counts, tile_here, 0, keepdims=False)
    mine_partner = lax.dynamic_index_in_dim(partner, tile_here, 0, keepdims=False)
    own_partner = lax.dynamic_slice_in_dim(mine_partner, member * row_part, row_part, 1)
    own_pre_ok = own_rows[None, :] < mine_counts[:, 0:1]
    own_post_ok = own_rows[None, :] < mine_counts[:, 1:2]
    local_x = features.reshape(row_part, 4, feature_width)
    weights = butterfly_gather(jnp.stack([w_in.T, w_out], 1), "mlp")
    own_hidden = jnp.einsum("rcf,hf->rch", local_x, weights[:, 0], preferred_element_type=jnp.float32)
    own_active = jax.nn.gelu(own_hidden).astype(jnp.bfloat16)
    mixed_rows = jnp.einsum("rch,hf->rcf", own_active, weights[:, 1], preferred_element_type=jnp.float32)
    embedded = (local_x.astype(jnp.float32) + mixed_rows).astype(jnp.bfloat16)
    pre_local = embedded[:, 0::2]
    post_local = embedded[:, 1::2]
    query_local = jnp.einsum(
        "ruf,fg->rug", pre_local, bilinear, preferred_element_type=jnp.float32
    ).astype(jnp.bfloat16)

    x_stride = 4 * grid_depth
    y_stride = grid_depth
    query_all = butterfly_gather(query_local, "mlp")
    facing = jnp.where(block_x == 0, post_local[:, 1], post_local[:, 0])
    x_pairs = [(s, (s + x_stride) % tile_count) for s in range(tile_count)]
    from_x = lax.ppermute(facing, "tile", x_pairs)
    halo = jnp.stack([from_x, post_local[:, 0], post_local[:, 1]], 0)

    def position(s, stride, extent):
        return (s // stride) % extent

    def along(arr, stride, extent):
        lower = [(s, s + stride) for s in range(tile_count) if position(s, stride, extent) < extent - 1]
        upper = [(s, s - stride) for s in range(tile_count) if position(s, stride, extent) > 0]
        return jnp.stack(
            [lax.ppermute(arr, "tile", lower), arr, lax.ppermute(arr, "tile", upper)], 0
        )

    def along_back(arr, stride, extent):
        lower = [(s, s - stride) for s in range(tile_count) if position(s, stride, extent) > 0]
        upper = [(s, s + stride) for s in range(tile_count) if position(s, stride, extent) < extent - 1]
        return arr[1] + lax.ppermute(arr[0], "tile", lower) + lax.ppermute(arr[2], "tile", upper)

    halo = along(along(halo, y_stride, 4), 1, grid_depth)
    steps = jnp.arange(3, dtype=jnp.int32) - 1
    dz_grid = steps[:, None]
    dy_grid = steps[None, :]
    inside = (
        (block_y + dy_grid >= 0)
        & (block_y + dy_grid < 4)
        & (block_z + dz_grid >= 0)
        & (block_z + dz_grid < grid_depth)
    )
    near = jnp.clip(tile_here + dy_grid * y_stride + dz_grid, 0, tile_count - 1)
    far = (near + x_stride) % tile_count
    col_counts = jnp.stack(
        [counts[far, block_x, 1], counts[near, 0, 1], counts[near, 1, 1]], -1
    )
    j_ok = inside[..., None, None] & (own_rows < col_counts[..., None])
    loss_sum = jnp.zeros((), jnp.float32)
    post_grad_parts = jnp.zeros(halo.shape, jnp.float32)
    query_grads = []
    place = jnp.arange(3, dtype=jnp.int32)
    code_base = (place[None, None, :] * 9 + (dy_grid[..., None] + 1) * 3 + dz_grid[..., None] + 1) * site_rows
    col_key = (code_base[..., None] + own_rows).reshape(-1)
    for pretile, order, edge in ((0, (0, 1, 2), 0), (1, (1, 2, 0), 2)):
        edge_ok = (block_x == 1) if pretile == 0 else (block_x == 0)
        ordered = halo[:, :, order]
        others = ordered.reshape(-1, feature_width)
        x_ok = jnp.stack([edge_ok if p == edge else jnp.bool_(True) for p in range(3)])
        col_ok = (j_ok[:, :, order] & x_ok[None, None, :, None]).reshape(-1)
        queries = query_all[:, pretile]
        raw_score = (
            jnp.einsum("rf,cf->rc", queries, others, preferred_element_type=jnp.float32)
            * score_scale
        )
        row_ok = all_rows < mine_counts[pretile, 0]
        target = (mine_partner[pretile][:, None] == col_key[None, :]).astype(jnp.float32)
        weight = (row_ok[:, None] & col_ok[None, :]).astype(jnp.float32)
        loss_sum = loss_sum + pair_cost(raw_score, target, weight, heavy_weight)
        slope = pair_slope(raw_score, target, weight, heavy_weight, factor)
        query_grads.append(jnp.dot(slope, others, preferred_element_type=jnp.float32))
        back = jnp.einsum("rc,rf->cf", slope, queries, preferred_element_type=jnp.float32)
        back = back.reshape(ordered.shape)
        for p in range(3):
            post_grad_parts = post_grad_parts.at[:, :, order[p]].add(back[:, :, p])
    post_grad_parts = along_back(along_back(post_grad_parts, 1, grid_depth), y_stride, 4)
    back_x = lax.ppermute(post_grad_parts[0], "tile", x_pairs)
    post_back = jnp.stack(
        [
            post_grad_parts[1] + jnp.where(block_x == 1, back_x, 0.0),
            post_grad_parts[2] + jnp.where(block_x == 0, back_x, 0.0),
        ],
        1,
    )
    query_back = butterfly_scatter(jnp.stack(query_grads, 1), "mlp").astype(jnp.bfloat16)
    bilinear_part = jnp.einsum(
        "ruf,rug->fg", pre_local, query_back, preferred_element_type=jnp.float32
    )
    pre_back = jnp.einsum("rug,fg->ruf", query_back, bilinear, preferred_element_type=jnp.float32)
    embed_grad = jnp.stack(
        [pre_back[:, 0], post_back[:, 0], pre_back[:, 1], post_back[:, 1]], 1
    ).astype(jnp.bfloat16)
    whole_x = butterfly_gather(local_x, "mlp")
    hidden_pre = jnp.einsum("rcf,fh->rch", whole_x, w_in, preferred_element_type=jnp.float32)
    active = jax.nn.gelu(hidden_pre).astype(jnp.bfloat16)
    embed_whole = butterfly_gather(embed_grad, "mlp")
    active_grad = jnp.einsum("rcf,hf->rch", embed_whole, w_out, preferred_element_type=jnp.float32)
    unused, pullback = jax.vjp(jax.nn.gelu, hidden_pre)
    hidden_grad = pullback(active_grad)[0].astype(jnp.bfloat16)
    in_part = jnp.einsum("rcf,rch->fh", whole_x, hidden_grad, preferred_element_type=jnp.float32)
    out_part = jnp.einsum("rch,rcf->hf", active, embed_whole, preferred_element_type=jnp.float32)
    width = bilinear_part.shape[1]
    in_rows = in_part.size // width
    out_rows = out_part.size // width
    packed, loss_block = all_reduce(
        jnp.concatenate([bilinear_part, in_part.reshape(-1, width), out_part.reshape(-1, width)], 0),
        jnp.broadcast_to(loss_sum, (8, 128)),
    )
    grad_bilinear = packed[:width]
    loss_total = loss_block[0, 0]
    grad_in = packed[width : width + in_rows].reshape(in_part.shape)
    grad_out = packed[width + in_rows : width + in_rows + out_rows].reshape(out_part.shape)
    pair_loss = loss_total / (2.0 * tile_count * site_rows * 27 * site_rows)
    return (pair_loss, grad_in, grad_out, grad_bilinear)


def solution(mesh):
    placed = (P("tile", "mlp", None, None, None), P(None, "mlp"), P("mlp", None), P(), P(), P())
    return jax.shard_map(
        local,
        mesh=mesh,
        in_specs=placed,
        out_specs=(P(), P(None, "mlp"), P("mlp", None), P()),
        check_vma=False,
    )
```

```python
import functools

import jax
import jax.numpy as jnp
from jax import lax
from jax.experimental import pallas as pl
from jax.experimental.pallas import tpu as pltpu
from jax.sharding import PartitionSpec as P

column_plan = ((-1, 1), (0, 0), (0, 1), (1, 0))


def shifted(array, axis, by):
    peers = lax.axis_size(axis)
    pairs = [(i, i + by) for i in range(peers) if 0 <= i + by < peers]
    return lax.ppermute(array, axis, pairs)


def butterfly_sum(x, axis):
    peers = lax.axis_size(axis)
    step = 1
    while step < peers:
        x = x + lax.ppermute(x, axis, [(i, i ^ step) for i in range(peers)])
        step *= 2
    return x


def butterfly_gather(x, axis):
    peers = lax.axis_size(axis)
    me = lax.axis_index(axis)
    step = 1
    while step < peers:
        other = lax.ppermute(x, axis, [(i, i ^ step) for i in range(peers)])
        low = (me & step) == 0
        x = jnp.where(low, jnp.concatenate([x, other], 0), jnp.concatenate([other, x], 0))
        step *= 2
    return x


def butterfly_scatter(x, axis):
    peers = lax.axis_size(axis)
    me = lax.axis_index(axis)
    step = peers // 2
    while step >= 1:
        half = x.shape[0] // 2
        upper = (me & step) != 0
        send = jnp.where(upper, x[:half], x[half:])
        keep = jnp.where(upper, x[half:], x[:half])
        x = keep + lax.ppermute(send, axis, [(i, i ^ step) for i in range(peers)])
        step //= 2
    return x


MESH = pl.DeviceIdType.MESH


def flip(index, bit):
    return index + bit - 2 * bit * ((index // bit) % 2)


def reduce_kernel(x_ref, l_ref, o_ref, lo_ref, recv, lrecv, lbuf, send_sem, recv_sem, lsend_sem, lrecv_sem):
    coords = {axis: lax.axis_index(axis) for axis in ("tile", "mlp")}
    tile_groups = ((1,), (2,), (16, 4, 8))
    mlp_bits = (2, 1, 4)

    def partner(axis, bits, distance):
        index = coords[axis]
        for place, bit in enumerate(bits):
            if (distance >> place) & 1:
                index = flip(index, bit)
        return index

    def rank(axis, bits, distance=0):
        total = 0
        for place, bit in enumerate(bits):
            own = (coords[axis] // bit) % 2
            if (distance >> place) & 1:
                own = 1 - own
            total = total + own * (1 << place)
        return total

    def ordered_sum(blocks, axis, bits):
        fan = 1 << len(bits)
        if fan == 2:
            return blocks[0] + blocks[1]
        total = None
        for q in range(fan):
            pick = None
            for distance in range(fan):
                term = jnp.where(rank(axis, bits, distance) == q, blocks[distance], 0.0)
                pick = term if pick is None else pick + term
            total = pick if total is None else total + pick
        return total

    steps = [("tile", bits) for bits in tile_groups] + [("mlp", mlp_bits)]
    barrier = pltpu.get_barrier_semaphore()
    greeted = 0
    for axis, bits in steps:
        for distance in range(1, 1 << len(bits)):
            pl.semaphore_signal(
                barrier, inc=1, device_id={axis: partner(axis, bits, distance)}, device_id_type=MESH
            )
            greeted += 1
    pl.semaphore_wait(barrier, greeted)
    o_ref[...] = x_ref[...]

    def send_all(axis, bits, slot, sources, length, loss_slot=None):
        copies = []
        for distance in range(1, 1 << len(bits)):
            target = {axis: partner(axis, bits, distance)}
            copy = pltpu.make_async_remote_copy(
                src_ref=o_ref.at[pl.ds(pl.multiple_of(sources(distance), 8), length)],
                dst_ref=recv.at[slot + distance - 1, pl.ds(0, length)],
                send_sem=send_sem.at[slot + distance - 1],
                recv_sem=recv_sem.at[slot + distance - 1],
                device_id=target,
                device_id_type=MESH,
            )
            copy.start()
            copies.append(copy)
            if loss_slot is not None:
                copy = pltpu.make_async_remote_copy(
                    src_ref=lbuf.at[loss_slot[0]],
                    dst_ref=lrecv.at[loss_slot[1] + distance - 1],
                    send_sem=lsend_sem.at[loss_slot[1] + distance - 1],
                    recv_sem=lrecv_sem.at[loss_slot[1] + distance - 1],
                    device_id=target,
                    device_id_type=MESH,
                )
                copy.start()
                copies.append(copy)
        for copy in copies:
            copy.wait()

    loss = l_ref[...]
    slot = 0
    lslot = 0
    start = 0
    length = o_ref.shape[0]
    for stage, (axis, bits) in enumerate(steps):
        fan = 1 << len(bits)
        lbuf[stage] = loss
        if axis == "tile":
            length //= fan
            send_all(axis, bits, slot, lambda d: start + rank(axis, bits, d) * length, length, (stage, lslot))
            start = start + rank(axis, bits) * length
            mine = pl.ds(pl.multiple_of(start, 8), length)
            total = o_ref[mine]
            for distance in range(1, fan):
                total = total + recv[slot + distance - 1, pl.ds(0, length)]
            o_ref[mine] = total
        else:
            send_all(axis, bits, slot, lambda d: start, length, (stage, lslot))
            mine = pl.ds(pl.multiple_of(start, 8), length)
            own = o_ref[mine]
            blocks = [own] + [recv[slot + distance - 1, pl.ds(0, length)] for distance in range(1, fan)]
            o_ref[mine] = jnp.where(start < x_ref.shape[1], ordered_sum(blocks, axis, bits), own)
        loss = ordered_sum([loss] + [lrecv[lslot + distance - 1] for distance in range(1, fan)], axis, bits)
        slot += fan - 1
        lslot += fan - 1
    lo_ref[...] = loss
    for bits in reversed(tile_groups):
        fan = 1 << len(bits)
        send_all("tile", bits, slot, lambda d: start, length)
        base = start - rank("tile", bits) * length
        for distance in range(1, fan):
            spot = base + rank("tile", bits, distance) * length
            o_ref[pl.ds(pl.multiple_of(spot, 8), length)] = recv[slot + distance - 1, pl.ds(0, length)]
        start = base
        length *= fan
        slot += fan - 1


def all_reduce(packed, loss_block):
    slots = 2 * (1 + 1 + 7) + 7
    loss_slots = 1 + 1 + 7 + 7
    return pl.pallas_call(
        reduce_kernel,
        out_shape=(
            jax.ShapeDtypeStruct(packed.shape, packed.dtype),
            jax.ShapeDtypeStruct(loss_block.shape, loss_block.dtype),
        ),
        in_specs=[pl.BlockSpec(memory_space=pltpu.VMEM)] * 2,
        out_specs=(pl.BlockSpec(memory_space=pltpu.VMEM), pl.BlockSpec(memory_space=pltpu.VMEM)),
        scratch_shapes=[
            pltpu.VMEM((slots, packed.shape[0] // 2) + packed.shape[1:], packed.dtype),
            pltpu.VMEM((loss_slots,) + loss_block.shape, loss_block.dtype),
            pltpu.VMEM((4,) + loss_block.shape, loss_block.dtype),
            pltpu.SemaphoreType.DMA((slots,)),
            pltpu.SemaphoreType.DMA((slots,)),
            pltpu.SemaphoreType.DMA((loss_slots,)),
            pltpu.SemaphoreType.DMA((loss_slots,)),
        ],
        compiler_params=pltpu.CompilerParams(collective_id=0, has_side_effects=True),
    )(packed, loss_block)

def pair_slope(raw_score, target, weight, heavy_weight, factor):
    chance = jax.nn.sigmoid(raw_score)
    signed = (1.0 - target) * chance - heavy_weight * target * (1.0 - chance)
    return (weight * signed * factor).astype(jnp.bfloat16)


def pair_cost(raw_score, target, weight, heavy_weight):
    missed = heavy_weight * target * jnp.log1p(jnp.exp(-raw_score))
    spurious = (1.0 - target) * jnp.log1p(jnp.exp(raw_score))
    return jnp.sum(weight * (missed + spurious))


def local(features, w_in, w_out, bilinear, partner, counts):
    row_part = features.shape[1]
    feature_width = features.shape[4]
    groups = lax.axis_size("mlp")
    site_rows = row_part * groups
    tile_count = lax.axis_size("tile")
    grid_depth = tile_count // 8
    tile_here = lax.axis_index("tile")
    member = lax.axis_index("mlp")
    block_x = tile_here // (4 * grid_depth)
    block_y = tile_here // grid_depth % 4
    block_z = tile_here % grid_depth
    heavy_weight = 27 * site_rows // 4
    score_scale = feature_width ** (-0.5)
    factor = score_scale / (2 * tile_count * site_rows)
    own_rows = member * row_part + jnp.arange(row_part, dtype=jnp.int32)
    all_rows = jnp.arange(site_rows, dtype=jnp.int32)
    mine_counts = lax.dynamic_index_in_dim(counts, tile_here, 0, keepdims=False)
    mine_partner = lax.dynamic_index_in_dim(partner, tile_here, 0, keepdims=False)
    own_partner = lax.dynamic_slice_in_dim(mine_partner, member * row_part, row_part, 1)
    own_pre_ok = own_rows[None, :] < mine_counts[:, 0:1]
    own_post_ok = own_rows[None, :] < mine_counts[:, 1:2]
    local_x = features.reshape(row_part, 4, feature_width)
    weights = butterfly_gather(jnp.stack([w_in.T, w_out], 1), "mlp")
    own_hidden = jnp.einsum("rcf,hf->rch", local_x, weights[:, 0], preferred_element_type=jnp.float32)
    own_active = jax.nn.gelu(own_hidden).astype(jnp.bfloat16)
    mixed_rows = jnp.einsum("rch,hf->rcf", own_active, weights[:, 1], preferred_element_type=jnp.float32)
    embedded = (local_x.astype(jnp.float32) + mixed_rows).astype(jnp.bfloat16)
    pre_local = embedded[:, 0::2]
    post_local = embedded[:, 1::2]
    query_local = jnp.einsum(
        "ruf,fg->rug", pre_local, bilinear, preferred_element_type=jnp.float32
    ).astype(jnp.bfloat16)

    x_stride = 4 * grid_depth
    y_stride = grid_depth
    query_all = butterfly_gather(query_local, "mlp")
    facing = jnp.where(block_x == 0, post_local[:, 1], post_local[:, 0])
    x_pairs = [(s, (s + x_stride) % tile_count) for s in range(tile_count)]
    from_x = lax.ppermute(facing, "tile", x_pairs)
    halo = jnp.stack([from_x, post_local[:, 0], post_local[:, 1]], 0)

    def position(s, stride, extent):
        return (s // stride) % extent

    def along(arr, stride, extent):
        lower = [(s, s + stride) for s in range(tile_count) if position(s, stride, extent) < extent - 1]
        upper = [(s, s - stride) for s in range(tile_count) if position(s, stride, extent) > 0]
        return jnp.stack(
            [lax.ppermute(arr, "tile", lower), arr, lax.ppermute(arr, "tile", upper)], 0
        )

    def along_back(arr, stride, extent):
        lower = [(s, s - stride) for s in range(tile_count) if position(s, stride, extent) > 0]
        upper = [(s, s + stride) for s in range(tile_count) if position(s, stride, extent) < extent - 1]
        return arr[1] + lax.ppermute(arr[0], "tile", lower) + lax.ppermute(arr[2], "tile", upper)

    halo = along(along(halo, y_stride, 4), 1, grid_depth)
    steps = jnp.arange(3, dtype=jnp.int32) - 1
    dz_grid = steps[:, None]
    dy_grid = steps[None, :]
    inside = (
        (block_y + dy_grid >= 0)
        & (block_y + dy_grid < 4)
        & (block_z + dz_grid >= 0)
        & (block_z + dz_grid < grid_depth)
    )
    near = jnp.clip(tile_here + dy_grid * y_stride + dz_grid, 0, tile_count - 1)
    far = (near + x_stride) % tile_count
    col_counts = jnp.stack(
        [counts[far, block_x, 1], counts[near, 0, 1], counts[near, 1, 1]], -1
    )
    j_ok = inside[..., None, None] & (own_rows < col_counts[..., None])
    loss_sum = jnp.zeros((), jnp.float32)
    post_grad_parts = jnp.zeros(halo.shape, jnp.float32)
    query_grads = []
    place = jnp.arange(3, dtype=jnp.int32)
    code_base = (place[None, None, :] * 9 + (dy_grid[..., None] + 1) * 3 + dz_grid[..., None] + 1) * site_rows
    col_key = (code_base[..., None] + own_rows).reshape(-1)
    for pretile, order, edge in ((0, (0, 1, 2), 0), (1, (1, 2, 0), 2)):
        edge_ok = (block_x == 1) if pretile == 0 else (block_x == 0)
        ordered = halo[:, :, order]
        others = ordered.reshape(-1, feature_width)
        x_ok = jnp.stack([edge_ok if p == edge else jnp.bool_(True) for p in range(3)])
        col_ok = (j_ok[:, :, order] & x_ok[None, None, :, None]).reshape(-1)
        queries = query_all[:, pretile]
        raw_score = (
            jnp.einsum("rf,cf->rc", queries, others, preferred_element_type=jnp.float32)
            * score_scale
        )
        row_ok = all_rows < mine_counts[pretile, 0]
        target = (mine_partner[pretile][:, None] == col_key[None, :]).astype(jnp.float32)
        weight = (row_ok[:, None] & col_ok[None, :]).astype(jnp.float32)
        loss_sum = loss_sum + pair_cost(raw_score, target, weight, heavy_weight)
        slope = pair_slope(raw_score, target, weight, heavy_weight, factor)
        query_grads.append(jnp.dot(slope, others, preferred_element_type=jnp.float32))
        back = jnp.einsum("rc,rf->cf", slope, queries, preferred_element_type=jnp.float32)
        back = back.reshape(ordered.shape)
        for p in range(3):
            post_grad_parts = post_grad_parts.at[:, :, order[p]].add(back[:, :, p])
    post_grad_parts = along_back(along_back(post_grad_parts, 1, grid_depth), y_stride, 4)
    back_x = lax.ppermute(post_grad_parts[0], "tile", x_pairs)
    post_back = jnp.stack(
        [
            post_grad_parts[1] + jnp.where(block_x == 1, back_x, 0.0),
            post_grad_parts[2] + jnp.where(block_x == 0, back_x, 0.0),
        ],
        1,
    )
    query_back = butterfly_scatter(jnp.stack(query_grads, 1), "mlp").astype(jnp.bfloat16)
    bilinear_part = jnp.einsum(
        "ruf,rug->fg", pre_local, query_back, preferred_element_type=jnp.float32
    )
    pre_back = jnp.einsum("rug,fg->ruf", query_back, bilinear, preferred_element_type=jnp.float32)
    embed_grad = jnp.stack(
        [pre_back[:, 0], post_back[:, 0], pre_back[:, 1], post_back[:, 1]], 1
    ).astype(jnp.bfloat16)
    whole_x = butterfly_gather(local_x, "mlp")
    hidden_pre = jnp.einsum("rcf,fh->rch", whole_x, w_in, preferred_element_type=jnp.float32)
    active = jax.nn.gelu(hidden_pre).astype(jnp.bfloat16)
    pre_whole = butterfly_gather(pre_back.astype(jnp.bfloat16), "mlp")
    post_whole = butterfly_gather(post_back.astype(jnp.bfloat16), "mlp")
    embed_whole = jnp.stack([pre_whole[:, 0], post_whole[:, 0], pre_whole[:, 1], post_whole[:, 1]], 1)
    active_grad = jnp.einsum("rcf,hf->rch", embed_whole, w_out, preferred_element_type=jnp.float32)
    unused, pullback = jax.vjp(jax.nn.gelu, hidden_pre)
    hidden_grad = pullback(active_grad)[0].astype(jnp.bfloat16)
    in_part = jnp.einsum("rcf,rch->fh", whole_x, hidden_grad, preferred_element_type=jnp.float32)
    out_part = jnp.einsum("rch,rcf->hf", active, embed_whole, preferred_element_type=jnp.float32)
    width = bilinear_part.shape[1]
    in_rows = in_part.size // width
    out_rows = out_part.size // width
    packed, loss_block = all_reduce(
        jnp.concatenate([bilinear_part, in_part.reshape(-1, width), out_part.reshape(-1, width)], 0),
        jnp.broadcast_to(loss_sum, (8, 128)),
    )
    grad_bilinear = packed[:width]
    loss_total = loss_block[0, 0]
    grad_in = packed[width : width + in_rows].reshape(in_part.shape)
    grad_out = packed[width + in_rows : width + in_rows + out_rows].reshape(out_part.shape)
    pair_loss = loss_total / (2.0 * tile_count * site_rows * 27 * site_rows)
    return (pair_loss, grad_in, grad_out, grad_bilinear)


def solution(mesh):
    placed = (P("tile", "mlp", None, None, None), P(None, "mlp"), P("mlp", None), P(), P(), P())
    return jax.shard_map(
        local,
        mesh=mesh,
        in_specs=placed,
        out_specs=(P(), P(None, "mlp"), P("mlp", None), P()),
        check_vma=False,
    )
```

```python
import functools

import jax
import jax.numpy as jnp
from jax import lax
from jax.experimental import pallas as pl
from jax.experimental.pallas import tpu as pltpu
from jax.sharding import PartitionSpec as P

column_plan = ((-1, 1), (0, 0), (0, 1), (1, 0))


def shifted(array, axis, by):
    peers = lax.axis_size(axis)
    pairs = [(i, i + by) for i in range(peers) if 0 <= i + by < peers]
    return lax.ppermute(array, axis, pairs)


def butterfly_sum(x, axis):
    peers = lax.axis_size(axis)
    step = 1
    while step < peers:
        x = x + lax.ppermute(x, axis, [(i, i ^ step) for i in range(peers)])
        step *= 2
    return x


def butterfly_gather(x, axis):
    peers = lax.axis_size(axis)
    me = lax.axis_index(axis)
    step = 1
    while step < peers:
        other = lax.ppermute(x, axis, [(i, i ^ step) for i in range(peers)])
        low = (me & step) == 0
        x = jnp.where(low, jnp.concatenate([x, other], 0), jnp.concatenate([other, x], 0))
        step *= 2
    return x


def butterfly_scatter(x, axis):
    peers = lax.axis_size(axis)
    me = lax.axis_index(axis)
    step = peers // 2
    while step >= 1:
        half = x.shape[0] // 2
        upper = (me & step) != 0
        send = jnp.where(upper, x[:half], x[half:])
        keep = jnp.where(upper, x[half:], x[:half])
        x = keep + lax.ppermute(send, axis, [(i, i ^ step) for i in range(peers)])
        step //= 2
    return x


MESH = pl.DeviceIdType.MESH


def flip(index, bit):
    return index + bit - 2 * bit * ((index // bit) % 2)


def reduce_kernel(x_ref, l_ref, o_ref, lo_ref, recv, lrecv, lbuf, send_sem, recv_sem, lsend_sem, lrecv_sem):
    coords = {axis: lax.axis_index(axis) for axis in ("tile", "mlp")}
    tile_groups = ((1,), (2,), (16, 4, 8))
    mlp_bits = (2, 1, 4)

    def partner(axis, bits, distance):
        index = coords[axis]
        for place, bit in enumerate(bits):
            if (distance >> place) & 1:
                index = flip(index, bit)
        return index

    def rank(axis, bits, distance=0):
        total = 0
        for place, bit in enumerate(bits):
            own = (coords[axis] // bit) % 2
            if (distance >> place) & 1:
                own = 1 - own
            total = total + own * (1 << place)
        return total

    def ordered_sum(blocks, axis, bits):
        fan = 1 << len(bits)
        if fan == 2:
            return blocks[0] + blocks[1]
        total = None
        for q in range(fan):
            pick = None
            for distance in range(fan):
                term = jnp.where(rank(axis, bits, distance) == q, blocks[distance], 0.0)
                pick = term if pick is None else pick + term
            total = pick if total is None else total + pick
        return total

    steps = [("tile", bits) for bits in tile_groups] + [("mlp", mlp_bits)]
    barrier = pltpu.get_barrier_semaphore()
    greeted = 0
    for axis, bits in steps:
        for distance in range(1, 1 << len(bits)):
            pl.semaphore_signal(
                barrier, inc=1, device_id={axis: partner(axis, bits, distance)}, device_id_type=MESH
            )
            greeted += 1
    pl.semaphore_wait(barrier, greeted)
    o_ref[...] = x_ref[...]

    def send_all(axis, bits, slot, sources, length, loss_slot=None):
        copies = []
        for distance in range(1, 1 << len(bits)):
            target = {axis: partner(axis, bits, distance)}
            copy = pltpu.make_async_remote_copy(
                src_ref=o_ref.at[pl.ds(pl.multiple_of(sources(distance), 8), length)],
                dst_ref=recv.at[slot + distance - 1, pl.ds(0, length)],
                send_sem=send_sem.at[slot + distance - 1],
                recv_sem=recv_sem.at[slot + distance - 1],
                device_id=target,
                device_id_type=MESH,
            )
            copy.start()
            copies.append(copy)
            if loss_slot is not None:
                copy = pltpu.make_async_remote_copy(
                    src_ref=lbuf.at[loss_slot[0]],
                    dst_ref=lrecv.at[loss_slot[1] + distance - 1],
                    send_sem=lsend_sem.at[loss_slot[1] + distance - 1],
                    recv_sem=lrecv_sem.at[loss_slot[1] + distance - 1],
                    device_id=target,
                    device_id_type=MESH,
                )
                copy.start()
                copies.append(copy)
        for copy in copies:
            copy.wait()

    loss = l_ref[...]
    slot = 0
    lslot = 0
    start = 0
    length = o_ref.shape[0]
    for stage, (axis, bits) in enumerate(steps):
        fan = 1 << len(bits)
        lbuf[stage] = loss
        if axis == "tile":
            length //= fan
            send_all(axis, bits, slot, lambda d: start + rank(axis, bits, d) * length, length, (stage, lslot))
            start = start + rank(axis, bits) * length
            mine = pl.ds(pl.multiple_of(start, 8), length)
            total = o_ref[mine]
            for distance in range(1, fan):
                total = total + recv[slot + distance - 1, pl.ds(0, length)]
            o_ref[mine] = total
        else:
            send_all(axis, bits, slot, lambda d: start, length, (stage, lslot))
            mine = pl.ds(pl.multiple_of(start, 8), length)
            own = o_ref[mine]
            blocks = [own] + [recv[slot + distance - 1, pl.ds(0, length)] for distance in range(1, fan)]
            o_ref[mine] = jnp.where(start < x_ref.shape[1], ordered_sum(blocks, axis, bits), own)
        loss = ordered_sum([loss] + [lrecv[lslot + distance - 1] for distance in range(1, fan)], axis, bits)
        slot += fan - 1
        lslot += fan - 1
    lo_ref[...] = loss
    for bits in reversed(tile_groups):
        fan = 1 << len(bits)
        send_all("tile", bits, slot, lambda d: start, length)
        base = start - rank("tile", bits) * length
        for distance in range(1, fan):
            spot = base + rank("tile", bits, distance) * length
            o_ref[pl.ds(pl.multiple_of(spot, 8), length)] = recv[slot + distance - 1, pl.ds(0, length)]
        start = base
        length *= fan
        slot += fan - 1


def all_reduce(packed, loss_block):
    slots = 2 * (1 + 1 + 7) + 7
    loss_slots = 1 + 1 + 7 + 7
    return pl.pallas_call(
        reduce_kernel,
        out_shape=(
            jax.ShapeDtypeStruct(packed.shape, packed.dtype),
            jax.ShapeDtypeStruct(loss_block.shape, loss_block.dtype),
        ),
        in_specs=[pl.BlockSpec(memory_space=pltpu.VMEM)] * 2,
        out_specs=(pl.BlockSpec(memory_space=pltpu.VMEM), pl.BlockSpec(memory_space=pltpu.VMEM)),
        scratch_shapes=[
            pltpu.VMEM((slots, packed.shape[0] // 2) + packed.shape[1:], packed.dtype),
            pltpu.VMEM((loss_slots,) + loss_block.shape, loss_block.dtype),
            pltpu.VMEM((4,) + loss_block.shape, loss_block.dtype),
            pltpu.SemaphoreType.DMA((slots,)),
            pltpu.SemaphoreType.DMA((slots,)),
            pltpu.SemaphoreType.DMA((loss_slots,)),
            pltpu.SemaphoreType.DMA((loss_slots,)),
        ],
        compiler_params=pltpu.CompilerParams(collective_id=0, has_side_effects=True),
    )(packed, loss_block)

def pair_slope(raw_score, target, weight, heavy_weight, factor):
    chance = jax.nn.sigmoid(raw_score)
    signed = (1.0 - target) * chance - heavy_weight * target * (1.0 - chance)
    return (weight * signed * factor).astype(jnp.bfloat16)


def pair_cost(raw_score, target, weight, heavy_weight):
    missed = heavy_weight * target * jnp.log1p(jnp.exp(-raw_score))
    spurious = (1.0 - target) * jnp.log1p(jnp.exp(raw_score))
    return jnp.sum(weight * (missed + spurious))


def local(features, w_in, w_out, bilinear, partner, counts):
    row_part = features.shape[1]
    feature_width = features.shape[4]
    groups = lax.axis_size("mlp")
    site_rows = row_part * groups
    tile_count = lax.axis_size("tile")
    grid_depth = tile_count // 8
    tile_here = lax.axis_index("tile")
    member = lax.axis_index("mlp")
    block_x = tile_here // (4 * grid_depth)
    block_y = tile_here // grid_depth % 4
    block_z = tile_here % grid_depth
    heavy_weight = 27 * site_rows // 4
    score_scale = feature_width ** (-0.5)
    factor = score_scale / (2 * tile_count * site_rows)
    own_rows = member * row_part + jnp.arange(row_part, dtype=jnp.int32)
    all_rows = jnp.arange(site_rows, dtype=jnp.int32)
    mine_counts = lax.dynamic_index_in_dim(counts, tile_here, 0, keepdims=False)
    mine_partner = lax.dynamic_index_in_dim(partner, tile_here, 0, keepdims=False)
    own_partner = lax.dynamic_slice_in_dim(mine_partner, member * row_part, row_part, 1)
    own_pre_ok = own_rows[None, :] < mine_counts[:, 0:1]
    own_post_ok = own_rows[None, :] < mine_counts[:, 1:2]
    local_x = features.reshape(row_part, 4, feature_width)
    weights = butterfly_gather(jnp.stack([w_in.T, w_out], 1), "mlp")
    own_hidden = jnp.einsum("rcf,hf->rch", local_x, weights[:, 0], preferred_element_type=jnp.float32)
    own_active = jax.nn.gelu(own_hidden).astype(jnp.bfloat16)
    mixed_rows = jnp.einsum("rch,hf->rcf", own_active, weights[:, 1], preferred_element_type=jnp.float32)
    embedded = (local_x.astype(jnp.float32) + mixed_rows).astype(jnp.bfloat16)
    pre_local = embedded[:, 0::2]
    post_local = embedded[:, 1::2]
    query_local = jnp.einsum(
        "ruf,fg->rug", pre_local, bilinear, preferred_element_type=jnp.float32
    ).astype(jnp.bfloat16)

    x_stride = 4 * grid_depth
    y_stride = grid_depth
    query_all = butterfly_gather(query_local, "mlp")
    facing = jnp.where(block_x == 0, post_local[:, 1], post_local[:, 0])
    x_pairs = [(s, (s + x_stride) % tile_count) for s in range(tile_count)]
    from_x = lax.ppermute(facing, "tile", x_pairs)
    halo = jnp.stack([from_x, post_local[:, 0], post_local[:, 1]], 0)

    def position(s, stride, extent):
        return (s // stride) % extent

    def along(arr, stride, extent):
        lower = [(s, s + stride) for s in range(tile_count) if position(s, stride, extent) < extent - 1]
        upper = [(s, s - stride) for s in range(tile_count) if position(s, stride, extent) > 0]
        return jnp.stack(
            [lax.ppermute(arr, "tile", lower), arr, lax.ppermute(arr, "tile", upper)], 0
        )

    def along_back(arr, stride, extent):
        lower = [(s, s - stride) for s in range(tile_count) if position(s, stride, extent) > 0]
        upper = [(s, s + stride) for s in range(tile_count) if position(s, stride, extent) < extent - 1]
        return arr[1] + lax.ppermute(arr[0], "tile", lower) + lax.ppermute(arr[2], "tile", upper)

    halo = along(along(halo, y_stride, 4), 1, grid_depth)
    steps = jnp.arange(3, dtype=jnp.int32) - 1
    dz_grid = steps[:, None]
    dy_grid = steps[None, :]
    inside = (
        (block_y + dy_grid >= 0)
        & (block_y + dy_grid < 4)
        & (block_z + dz_grid >= 0)
        & (block_z + dz_grid < grid_depth)
    )
    near = jnp.clip(tile_here + dy_grid * y_stride + dz_grid, 0, tile_count - 1)
    far = (near + x_stride) % tile_count
    col_counts = jnp.stack(
        [counts[far, block_x, 1], counts[near, 0, 1], counts[near, 1, 1]], -1
    )
    j_ok = inside[..., None, None] & (own_rows < col_counts[..., None])
    loss_sum = jnp.zeros((), jnp.float32)
    post_grad_parts = jnp.zeros(halo.shape, jnp.float32)
    query_grads = []
    place = jnp.arange(3, dtype=jnp.int32)
    code_base = (place[None, None, :] * 9 + (dy_grid[..., None] + 1) * 3 + dz_grid[..., None] + 1) * site_rows
    col_key = (code_base[..., None] + own_rows).reshape(-1)
    for pretile, order, edge in ((0, (0, 1, 2), 0), (1, (1, 2, 0), 2)):
        edge_ok = (block_x == 1) if pretile == 0 else (block_x == 0)
        ordered = halo[:, :, order]
        others = ordered.reshape(-1, feature_width)
        x_ok = jnp.stack([edge_ok if p == edge else jnp.bool_(True) for p in range(3)])
        col_ok = (j_ok[:, :, order] & x_ok[None, None, :, None]).reshape(-1)
        queries = query_all[:, pretile]
        raw_score = (
            jnp.einsum("rf,cf->rc", queries, others, preferred_element_type=jnp.float32)
            * score_scale
        )
        row_ok = all_rows < mine_counts[pretile, 0]
        target = (mine_partner[pretile][:, None] == col_key[None, :]).astype(jnp.float32)
        weight = (row_ok[:, None] & col_ok[None, :]).astype(jnp.float32)
        loss_sum = loss_sum + pair_cost(raw_score, target, weight, heavy_weight)
        slope = pair_slope(raw_score, target, weight, heavy_weight, factor)
        query_grads.append(jnp.dot(slope, others, preferred_element_type=jnp.float32))
        back = jnp.einsum("rc,rf->cf", slope, queries, preferred_element_type=jnp.float32)
        back = back.reshape(ordered.shape)
        for p in range(3):
            post_grad_parts = post_grad_parts.at[:, :, order[p]].add(back[:, :, p])
    post_grad_parts = along_back(along_back(post_grad_parts, 1, grid_depth), y_stride, 4)
    back_x = lax.ppermute(post_grad_parts[0], "tile", x_pairs)
    post_back = jnp.stack(
        [
            post_grad_parts[1] + jnp.where(block_x == 1, back_x, 0.0),
            post_grad_parts[2] + jnp.where(block_x == 0, back_x, 0.0),
        ],
        1,
    )
    query_back = butterfly_scatter(jnp.stack(query_grads, 1), "mlp").astype(jnp.bfloat16)
    loss_sum, post_back = lax.optimization_barrier((loss_sum, post_back))
    bilinear_part = jnp.einsum(
        "ruf,rug->fg", pre_local, query_back, preferred_element_type=jnp.float32
    )
    pre_back = jnp.einsum("rug,fg->ruf", query_back, bilinear, preferred_element_type=jnp.float32)
    embed_grad = jnp.stack(
        [pre_back[:, 0], post_back[:, 0], pre_back[:, 1], post_back[:, 1]], 1
    ).astype(jnp.bfloat16)
    whole_x = butterfly_gather(local_x, "mlp")
    hidden_pre = jnp.einsum("rcf,fh->rch", whole_x, w_in, preferred_element_type=jnp.float32)
    active = jax.nn.gelu(hidden_pre).astype(jnp.bfloat16)
    embed_whole = butterfly_gather(embed_grad, "mlp")
    active_grad = jnp.einsum("rcf,hf->rch", embed_whole, w_out, preferred_element_type=jnp.float32)
    unused, pullback = jax.vjp(jax.nn.gelu, hidden_pre)
    hidden_grad = pullback(active_grad)[0].astype(jnp.bfloat16)
    in_part = jnp.einsum("rcf,rch->fh", whole_x, hidden_grad, preferred_element_type=jnp.float32)
    out_part = jnp.einsum("rch,rcf->hf", active, embed_whole, preferred_element_type=jnp.float32)
    width = bilinear_part.shape[1]
    in_rows = in_part.size // width
    out_rows = out_part.size // width
    packed, loss_block = all_reduce(
        jnp.concatenate([bilinear_part, in_part.reshape(-1, width), out_part.reshape(-1, width)], 0),
        jnp.broadcast_to(loss_sum, (8, 128)),
    )
    grad_bilinear = packed[:width]
    loss_total = loss_block[0, 0]
    grad_in = packed[width : width + in_rows].reshape(in_part.shape)
    grad_out = packed[width + in_rows : width + in_rows + out_rows].reshape(out_part.shape)
    pair_loss = loss_total / (2.0 * tile_count * site_rows * 27 * site_rows)
    return (pair_loss, grad_in, grad_out, grad_bilinear)


def solution(mesh):
    placed = (P("tile", "mlp", None, None, None), P(None, "mlp"), P("mlp", None), P(), P(), P())
    return jax.shard_map(
        local,
        mesh=mesh,
        in_specs=placed,
        out_specs=(P(), P(None, "mlp"), P("mlp", None), P()),
        check_vma=False,
    )
```

```python
import functools

import jax
import jax.numpy as jnp
from jax import lax
from jax.experimental import pallas as pl
from jax.experimental.pallas import tpu as pltpu
from jax.sharding import PartitionSpec as P

column_plan = ((-1, 1), (0, 0), (0, 1), (1, 0))


def shifted(array, axis, by):
    peers = lax.axis_size(axis)
    pairs = [(i, i + by) for i in range(peers) if 0 <= i + by < peers]
    return lax.ppermute(array, axis, pairs)


def butterfly_sum(x, axis):
    peers = lax.axis_size(axis)
    step = 1
    while step < peers:
        x = x + lax.ppermute(x, axis, [(i, i ^ step) for i in range(peers)])
        step *= 2
    return x


def butterfly_gather(x, axis):
    peers = lax.axis_size(axis)
    me = lax.axis_index(axis)
    step = 1
    while step < peers:
        other = lax.ppermute(x, axis, [(i, i ^ step) for i in range(peers)])
        low = (me & step) == 0
        x = jnp.where(low, jnp.concatenate([x, other], 0), jnp.concatenate([other, x], 0))
        step *= 2
    return x


def butterfly_scatter(x, axis, order=(4, 1, 2)):
    peers = lax.axis_size(axis)
    me = lax.axis_index(axis)
    bits = sorted(order, reverse=True)
    x = x.reshape((2,) * len(bits) + (x.shape[0] // peers,) + x.shape[1:])
    x = x.transpose([bits.index(bit) for bit in order] + list(range(len(bits), x.ndim)))
    x = x.reshape((-1,) + x.shape[len(bits) + 1 :])
    for bit in order:
        half = x.shape[0] // 2
        upper = (me // bit) % 2 != 0
        send = jnp.where(upper, x[:half], x[half:])
        keep = jnp.where(upper, x[half:], x[:half])
        x = keep + lax.ppermute(send, axis, [(i, i ^ bit) for i in range(peers)])
    return x

MESH = pl.DeviceIdType.MESH


def flip(index, bit):
    return index + bit - 2 * bit * ((index // bit) % 2)


def reduce_kernel(x_ref, l_ref, o_ref, lo_ref, recv, lrecv, lbuf, send_sem, recv_sem, lsend_sem, lrecv_sem):
    coords = {axis: lax.axis_index(axis) for axis in ("tile", "mlp")}
    tile_groups = ((1,), (2,), (16, 4, 8))
    mlp_bits = (2, 1, 4)

    def partner(axis, bits, distance):
        index = coords[axis]
        for place, bit in enumerate(bits):
            if (distance >> place) & 1:
                index = flip(index, bit)
        return index

    def rank(axis, bits, distance=0):
        total = 0
        for place, bit in enumerate(bits):
            own = (coords[axis] // bit) % 2
            if (distance >> place) & 1:
                own = 1 - own
            total = total + own * (1 << place)
        return total

    def ordered_sum(blocks, axis, bits):
        fan = 1 << len(bits)
        if fan == 2:
            return blocks[0] + blocks[1]
        total = None
        for q in range(fan):
            pick = None
            for distance in range(fan):
                term = jnp.where(rank(axis, bits, distance) == q, blocks[distance], 0.0)
                pick = term if pick is None else pick + term
            total = pick if total is None else total + pick
        return total

    steps = [("tile", bits) for bits in tile_groups] + [("mlp", mlp_bits)]
    barrier = pltpu.get_barrier_semaphore()
    greeted = 0
    for axis, bits in steps:
        for distance in range(1, 1 << len(bits)):
            pl.semaphore_signal(
                barrier, inc=1, device_id={axis: partner(axis, bits, distance)}, device_id_type=MESH
            )
            greeted += 1
    pl.semaphore_wait(barrier, greeted)
    o_ref[...] = x_ref[...]

    def send_all(axis, bits, slot, sources, length, loss_slot=None):
        copies = []
        for distance in range(1, 1 << len(bits)):
            target = {axis: partner(axis, bits, distance)}
            copy = pltpu.make_async_remote_copy(
                src_ref=o_ref.at[pl.ds(pl.multiple_of(sources(distance), 8), length)],
                dst_ref=recv.at[slot + distance - 1, pl.ds(0, length)],
                send_sem=send_sem.at[slot + distance - 1],
                recv_sem=recv_sem.at[slot + distance - 1],
                device_id=target,
                device_id_type=MESH,
            )
            copy.start()
            copies.append(copy)
            if loss_slot is not None:
                copy = pltpu.make_async_remote_copy(
                    src_ref=lbuf.at[loss_slot[0]],
                    dst_ref=lrecv.at[loss_slot[1] + distance - 1],
                    send_sem=lsend_sem.at[loss_slot[1] + distance - 1],
                    recv_sem=lrecv_sem.at[loss_slot[1] + distance - 1],
                    device_id=target,
                    device_id_type=MESH,
                )
                copy.start()
                copies.append(copy)
        for copy in copies:
            copy.wait()

    loss = l_ref[...]
    slot = 0
    lslot = 0
    start = 0
    length = o_ref.shape[0]
    for stage, (axis, bits) in enumerate(steps):
        fan = 1 << len(bits)
        lbuf[stage] = loss
        if axis == "tile":
            length //= fan
            send_all(axis, bits, slot, lambda d: start + rank(axis, bits, d) * length, length, (stage, lslot))
            start = start + rank(axis, bits) * length
            mine = pl.ds(pl.multiple_of(start, 8), length)
            total = o_ref[mine]
            for distance in range(1, fan):
                total = total + recv[slot + distance - 1, pl.ds(0, length)]
            o_ref[mine] = total
        else:
            send_all(axis, bits, slot, lambda d: start, length, (stage, lslot))
            mine = pl.ds(pl.multiple_of(start, 8), length)
            own = o_ref[mine]
            blocks = [own] + [recv[slot + distance - 1, pl.ds(0, length)] for distance in range(1, fan)]
            o_ref[mine] = jnp.where(start < x_ref.shape[1], ordered_sum(blocks, axis, bits), own)
        loss = ordered_sum([loss] + [lrecv[lslot + distance - 1] for distance in range(1, fan)], axis, bits)
        slot += fan - 1
        lslot += fan - 1
    lo_ref[...] = loss
    for bits in reversed(tile_groups):
        fan = 1 << len(bits)
        send_all("tile", bits, slot, lambda d: start, length)
        base = start - rank("tile", bits) * length
        for distance in range(1, fan):
            spot = base + rank("tile", bits, distance) * length
            o_ref[pl.ds(pl.multiple_of(spot, 8), length)] = recv[slot + distance - 1, pl.ds(0, length)]
        start = base
        length *= fan
        slot += fan - 1


def all_reduce(packed, loss_block):
    slots = 2 * (1 + 1 + 7) + 7
    loss_slots = 1 + 1 + 7 + 7
    return pl.pallas_call(
        reduce_kernel,
        out_shape=(
            jax.ShapeDtypeStruct(packed.shape, packed.dtype),
            jax.ShapeDtypeStruct(loss_block.shape, loss_block.dtype),
        ),
        in_specs=[pl.BlockSpec(memory_space=pltpu.VMEM)] * 2,
        out_specs=(pl.BlockSpec(memory_space=pltpu.VMEM), pl.BlockSpec(memory_space=pltpu.VMEM)),
        scratch_shapes=[
            pltpu.VMEM((slots, packed.shape[0] // 2) + packed.shape[1:], packed.dtype),
            pltpu.VMEM((loss_slots,) + loss_block.shape, loss_block.dtype),
            pltpu.VMEM((4,) + loss_block.shape, loss_block.dtype),
            pltpu.SemaphoreType.DMA((slots,)),
            pltpu.SemaphoreType.DMA((slots,)),
            pltpu.SemaphoreType.DMA((loss_slots,)),
            pltpu.SemaphoreType.DMA((loss_slots,)),
        ],
        compiler_params=pltpu.CompilerParams(collective_id=0, has_side_effects=True),
    )(packed, loss_block)

def pair_slope(raw_score, target, weight, heavy_weight, factor):
    chance = jax.nn.sigmoid(raw_score)
    signed = (1.0 - target) * chance - heavy_weight * target * (1.0 - chance)
    return (weight * signed * factor).astype(jnp.bfloat16)


def pair_cost(raw_score, target, weight, heavy_weight):
    missed = heavy_weight * target * jnp.log1p(jnp.exp(-raw_score))
    spurious = (1.0 - target) * jnp.log1p(jnp.exp(raw_score))
    return jnp.sum(weight * (missed + spurious))


def local(features, w_in, w_out, bilinear, partner, counts):
    row_part = features.shape[1]
    feature_width = features.shape[4]
    groups = lax.axis_size("mlp")
    site_rows = row_part * groups
    tile_count = lax.axis_size("tile")
    grid_depth = tile_count // 8
    tile_here = lax.axis_index("tile")
    member = lax.axis_index("mlp")
    block_x = tile_here // (4 * grid_depth)
    block_y = tile_here // grid_depth % 4
    block_z = tile_here % grid_depth
    heavy_weight = 27 * site_rows // 4
    score_scale = feature_width ** (-0.5)
    factor = score_scale / (2 * tile_count * site_rows)
    own_rows = member * row_part + jnp.arange(row_part, dtype=jnp.int32)
    all_rows = jnp.arange(site_rows, dtype=jnp.int32)
    mine_counts = lax.dynamic_index_in_dim(counts, tile_here, 0, keepdims=False)
    mine_partner = lax.dynamic_index_in_dim(partner, tile_here, 0, keepdims=False)
    own_partner = lax.dynamic_slice_in_dim(mine_partner, member * row_part, row_part, 1)
    own_pre_ok = own_rows[None, :] < mine_counts[:, 0:1]
    own_post_ok = own_rows[None, :] < mine_counts[:, 1:2]
    local_x = features.reshape(row_part, 4, feature_width)
    weights = butterfly_gather(jnp.stack([w_in.T, w_out], 1), "mlp")
    own_hidden = jnp.einsum("rcf,hf->rch", local_x, weights[:, 0], preferred_element_type=jnp.float32)
    own_active = jax.nn.gelu(own_hidden).astype(jnp.bfloat16)
    mixed_rows = jnp.einsum("rch,hf->rcf", own_active, weights[:, 1], preferred_element_type=jnp.float32)
    embedded = (local_x.astype(jnp.float32) + mixed_rows).astype(jnp.bfloat16)
    pre_local = embedded[:, 0::2]
    post_local = embedded[:, 1::2]
    query_local = jnp.einsum(
        "ruf,fg->rug", pre_local, bilinear, preferred_element_type=jnp.float32
    ).astype(jnp.bfloat16)

    x_stride = 4 * grid_depth
    y_stride = grid_depth
    query_all = butterfly_gather(query_local, "mlp")
    facing = jnp.where(block_x == 0, post_local[:, 1], post_local[:, 0])
    x_pairs = [(s, (s + x_stride) % tile_count) for s in range(tile_count)]
    from_x = lax.ppermute(facing, "tile", x_pairs)
    halo = jnp.stack([from_x, post_local[:, 0], post_local[:, 1]], 0)

    def position(s, stride, extent):
        return (s // stride) % extent

    def along(arr, stride, extent):
        lower = [(s, s + stride) for s in range(tile_count) if position(s, stride, extent) < extent - 1]
        upper = [(s, s - stride) for s in range(tile_count) if position(s, stride, extent) > 0]
        return jnp.stack(
            [lax.ppermute(arr, "tile", lower), arr, lax.ppermute(arr, "tile", upper)], 0
        )

    def along_back(arr, stride, extent):
        lower = [(s, s - stride) for s in range(tile_count) if position(s, stride, extent) > 0]
        upper = [(s, s + stride) for s in range(tile_count) if position(s, stride, extent) < extent - 1]
        return arr[1] + lax.ppermute(arr[0], "tile", lower) + lax.ppermute(arr[2], "tile", upper)

    halo = along(along(halo, y_stride, 4), 1, grid_depth)
    steps = jnp.arange(3, dtype=jnp.int32) - 1
    dz_grid = steps[:, None]
    dy_grid = steps[None, :]
    inside = (
        (block_y + dy_grid >= 0)
        & (block_y + dy_grid < 4)
        & (block_z + dz_grid >= 0)
        & (block_z + dz_grid < grid_depth)
    )
    near = jnp.clip(tile_here + dy_grid * y_stride + dz_grid, 0, tile_count - 1)
    far = (near + x_stride) % tile_count
    col_counts = jnp.stack(
        [counts[far, block_x, 1], counts[near, 0, 1], counts[near, 1, 1]], -1
    )
    j_ok = inside[..., None, None] & (own_rows < col_counts[..., None])
    loss_sum = jnp.zeros((), jnp.float32)
    post_grad_parts = jnp.zeros(halo.shape, jnp.float32)
    query_grads = []
    place = jnp.arange(3, dtype=jnp.int32)
    code_base = (place[None, None, :] * 9 + (dy_grid[..., None] + 1) * 3 + dz_grid[..., None] + 1) * site_rows
    col_key = (code_base[..., None] + own_rows).reshape(-1)
    for pretile, order, edge in ((0, (0, 1, 2), 0), (1, (1, 2, 0), 2)):
        edge_ok = (block_x == 1) if pretile == 0 else (block_x == 0)
        ordered = halo[:, :, order]
        others = ordered.reshape(-1, feature_width)
        x_ok = jnp.stack([edge_ok if p == edge else jnp.bool_(True) for p in range(3)])
        col_ok = (j_ok[:, :, order] & x_ok[None, None, :, None]).reshape(-1)
        queries = query_all[:, pretile]
        raw_score = (
            jnp.einsum("rf,cf->rc", queries, others, preferred_element_type=jnp.float32)
            * score_scale
        )
        row_ok = all_rows < mine_counts[pretile, 0]
        target = (mine_partner[pretile][:, None] == col_key[None, :]).astype(jnp.float32)
        weight = (row_ok[:, None] & col_ok[None, :]).astype(jnp.float32)
        loss_sum = loss_sum + pair_cost(raw_score, target, weight, heavy_weight)
        slope = pair_slope(raw_score, target, weight, heavy_weight, factor)
        query_grads.append(jnp.dot(slope, others, preferred_element_type=jnp.float32))
        back = jnp.einsum("rc,rf->cf", slope, queries, preferred_element_type=jnp.float32)
        back = back.reshape(ordered.shape)
        for p in range(3):
            post_grad_parts = post_grad_parts.at[:, :, order[p]].add(back[:, :, p])
    post_grad_parts = along_back(along_back(post_grad_parts, 1, grid_depth), y_stride, 4)
    back_x = lax.ppermute(post_grad_parts[0], "tile", x_pairs)
    post_back = jnp.stack(
        [
            post_grad_parts[1] + jnp.where(block_x == 1, back_x, 0.0),
            post_grad_parts[2] + jnp.where(block_x == 0, back_x, 0.0),
        ],
        1,
    )
    query_back = butterfly_scatter(jnp.stack(query_grads, 1), "mlp").astype(jnp.bfloat16)
    bilinear_part = jnp.einsum(
        "ruf,rug->fg", pre_local, query_back, preferred_element_type=jnp.float32
    )
    pre_back = jnp.einsum("rug,fg->ruf", query_back, bilinear, preferred_element_type=jnp.float32)
    embed_grad = jnp.stack(
        [pre_back[:, 0], post_back[:, 0], pre_back[:, 1], post_back[:, 1]], 1
    ).astype(jnp.bfloat16)
    whole_x = butterfly_gather(local_x, "mlp")
    hidden_pre = jnp.einsum("rcf,fh->rch", whole_x, w_in, preferred_element_type=jnp.float32)
    active = jax.nn.gelu(hidden_pre).astype(jnp.bfloat16)
    embed_whole = butterfly_gather(embed_grad, "mlp")
    active_grad = jnp.einsum("rcf,hf->rch", embed_whole, w_out, preferred_element_type=jnp.float32)
    unused, pullback = jax.vjp(jax.nn.gelu, hidden_pre)
    hidden_grad = pullback(active_grad)[0].astype(jnp.bfloat16)
    in_part = jnp.einsum("rcf,rch->fh", whole_x, hidden_grad, preferred_element_type=jnp.float32)
    out_part = jnp.einsum("rch,rcf->hf", active, embed_whole, preferred_element_type=jnp.float32)
    width = bilinear_part.shape[1]
    in_rows = in_part.size // width
    out_rows = out_part.size // width
    packed, loss_block = all_reduce(
        jnp.concatenate([bilinear_part, in_part.reshape(-1, width), out_part.reshape(-1, width)], 0),
        jnp.broadcast_to(loss_sum, (8, 128)),
    )
    grad_bilinear = packed[:width]
    loss_total = loss_block[0, 0]
    grad_in = packed[width : width + in_rows].reshape(in_part.shape)
    grad_out = packed[width + in_rows : width + in_rows + out_rows].reshape(out_part.shape)
    pair_loss = loss_total / (2.0 * tile_count * site_rows * 27 * site_rows)
    return (pair_loss, grad_in, grad_out, grad_bilinear)


def solution(mesh):
    placed = (P("tile", "mlp", None, None, None), P(None, "mlp"), P("mlp", None), P(), P(), P())
    return jax.shard_map(
        local,
        mesh=mesh,
        in_specs=placed,
        out_specs=(P(), P(None, "mlp"), P("mlp", None), P()),
        check_vma=False,
    )
```

```python
import functools

import jax
import jax.numpy as jnp
from jax import lax
from jax.experimental import pallas as pl
from jax.experimental.pallas import tpu as pltpu
from jax.sharding import PartitionSpec as P

column_plan = ((-1, 1), (0, 0), (0, 1), (1, 0))


def shifted(array, axis, by):
    peers = lax.axis_size(axis)
    pairs = [(i, i + by) for i in range(peers) if 0 <= i + by < peers]
    return lax.ppermute(array, axis, pairs)


def butterfly_sum(x, axis):
    peers = lax.axis_size(axis)
    step = 1
    while step < peers:
        x = x + lax.ppermute(x, axis, [(i, i ^ step) for i in range(peers)])
        step *= 2
    return x


def butterfly_gather(x, axis, order=(4, 1, 2)):
    peers = lax.axis_size(axis)
    me = lax.axis_index(axis)
    done = []
    for bit in order:
        other = lax.ppermute(x, axis, [(i, i ^ bit) for i in range(peers)])
        low = (me // bit) % 2 == 0
        x = jnp.where(low, jnp.stack([x, other], 0), jnp.stack([other, x], 0))
        done.insert(0, bit)
    count = len(done)
    axes = sorted(range(count), key=lambda place: -done[place])
    x = x.transpose(axes + list(range(count, x.ndim)))
    return x.reshape((-1,) + x.shape[count + 1 :])

def butterfly_scatter(x, axis):
    peers = lax.axis_size(axis)
    me = lax.axis_index(axis)
    step = peers // 2
    while step >= 1:
        half = x.shape[0] // 2
        upper = (me & step) != 0
        send = jnp.where(upper, x[:half], x[half:])
        keep = jnp.where(upper, x[half:], x[:half])
        x = keep + lax.ppermute(send, axis, [(i, i ^ step) for i in range(peers)])
        step //= 2
    return x


MESH = pl.DeviceIdType.MESH


def flip(index, bit):
    return index + bit - 2 * bit * ((index // bit) % 2)


def reduce_kernel(x_ref, l_ref, o_ref, lo_ref, recv, lrecv, lbuf, send_sem, recv_sem, lsend_sem, lrecv_sem):
    coords = {axis: lax.axis_index(axis) for axis in ("tile", "mlp")}
    tile_groups = ((1,), (2,), (16, 4, 8))
    mlp_bits = (2, 1, 4)

    def partner(axis, bits, distance):
        index = coords[axis]
        for place, bit in enumerate(bits):
            if (distance >> place) & 1:
                index = flip(index, bit)
        return index

    def rank(axis, bits, distance=0):
        total = 0
        for place, bit in enumerate(bits):
            own = (coords[axis] // bit) % 2
            if (distance >> place) & 1:
                own = 1 - own
            total = total + own * (1 << place)
        return total

    def ordered_sum(blocks, axis, bits):
        fan = 1 << len(bits)
        if fan == 2:
            return blocks[0] + blocks[1]
        total = None
        for q in range(fan):
            pick = None
            for distance in range(fan):
                term = jnp.where(rank(axis, bits, distance) == q, blocks[distance], 0.0)
                pick = term if pick is None else pick + term
            total = pick if total is None else total + pick
        return total

    steps = [("tile", bits) for bits in tile_groups] + [("mlp", mlp_bits)]
    barrier = pltpu.get_barrier_semaphore()
    greeted = 0
    for axis, bits in steps:
        for distance in range(1, 1 << len(bits)):
            pl.semaphore_signal(
                barrier, inc=1, device_id={axis: partner(axis, bits, distance)}, device_id_type=MESH
            )
            greeted += 1
    pl.semaphore_wait(barrier, greeted)
    o_ref[...] = x_ref[...]

    def send_all(axis, bits, slot, sources, length, loss_slot=None):
        copies = []
        for distance in range(1, 1 << len(bits)):
            target = {axis: partner(axis, bits, distance)}
            copy = pltpu.make_async_remote_copy(
                src_ref=o_ref.at[pl.ds(pl.multiple_of(sources(distance), 8), length)],
                dst_ref=recv.at[slot + distance - 1, pl.ds(0, length)],
                send_sem=send_sem.at[slot + distance - 1],
                recv_sem=recv_sem.at[slot + distance - 1],
                device_id=target,
                device_id_type=MESH,
            )
            copy.start()
            copies.append(copy)
            if loss_slot is not None:
                copy = pltpu.make_async_remote_copy(
                    src_ref=lbuf.at[loss_slot[0]],
                    dst_ref=lrecv.at[loss_slot[1] + distance - 1],
                    send_sem=lsend_sem.at[loss_slot[1] + distance - 1],
                    recv_sem=lrecv_sem.at[loss_slot[1] + distance - 1],
                    device_id=target,
                    device_id_type=MESH,
                )
                copy.start()
                copies.append(copy)
        for copy in copies:
            copy.wait()

    loss = l_ref[...]
    slot = 0
    lslot = 0
    start = 0
    length = o_ref.shape[0]
    for stage, (axis, bits) in enumerate(steps):
        fan = 1 << len(bits)
        lbuf[stage] = loss
        if axis == "tile":
            length //= fan
            send_all(axis, bits, slot, lambda d: start + rank(axis, bits, d) * length, length, (stage, lslot))
            start = start + rank(axis, bits) * length
            mine = pl.ds(pl.multiple_of(start, 8), length)
            total = o_ref[mine]
            for distance in range(1, fan):
                total = total + recv[slot + distance - 1, pl.ds(0, length)]
            o_ref[mine] = total
        else:
            send_all(axis, bits, slot, lambda d: start, length, (stage, lslot))
            mine = pl.ds(pl.multiple_of(start, 8), length)
            own = o_ref[mine]
            blocks = [own] + [recv[slot + distance - 1, pl.ds(0, length)] for distance in range(1, fan)]
            o_ref[mine] = jnp.where(start < x_ref.shape[1], ordered_sum(blocks, axis, bits), own)
        loss = ordered_sum([loss] + [lrecv[lslot + distance - 1] for distance in range(1, fan)], axis, bits)
        slot += fan - 1
        lslot += fan - 1
    lo_ref[...] = loss
    for bits in reversed(tile_groups):
        fan = 1 << len(bits)
        send_all("tile", bits, slot, lambda d: start, length)
        base = start - rank("tile", bits) * length
        for distance in range(1, fan):
            spot = base + rank("tile", bits, distance) * length
            o_ref[pl.ds(pl.multiple_of(spot, 8), length)] = recv[slot + distance - 1, pl.ds(0, length)]
        start = base
        length *= fan
        slot += fan - 1


def all_reduce(packed, loss_block):
    slots = 2 * (1 + 1 + 7) + 7
    loss_slots = 1 + 1 + 7 + 7
    return pl.pallas_call(
        reduce_kernel,
        out_shape=(
            jax.ShapeDtypeStruct(packed.shape, packed.dtype),
            jax.ShapeDtypeStruct(loss_block.shape, loss_block.dtype),
        ),
        in_specs=[pl.BlockSpec(memory_space=pltpu.VMEM)] * 2,
        out_specs=(pl.BlockSpec(memory_space=pltpu.VMEM), pl.BlockSpec(memory_space=pltpu.VMEM)),
        scratch_shapes=[
            pltpu.VMEM((slots, packed.shape[0] // 2) + packed.shape[1:], packed.dtype),
            pltpu.VMEM((loss_slots,) + loss_block.shape, loss_block.dtype),
            pltpu.VMEM((4,) + loss_block.shape, loss_block.dtype),
            pltpu.SemaphoreType.DMA((slots,)),
            pltpu.SemaphoreType.DMA((slots,)),
            pltpu.SemaphoreType.DMA((loss_slots,)),
            pltpu.SemaphoreType.DMA((loss_slots,)),
        ],
        compiler_params=pltpu.CompilerParams(collective_id=0, has_side_effects=True),
    )(packed, loss_block)

def pair_slope(raw_score, target, weight, heavy_weight, factor):
    chance = jax.nn.sigmoid(raw_score)
    signed = (1.0 - target) * chance - heavy_weight * target * (1.0 - chance)
    return (weight * signed * factor).astype(jnp.bfloat16)


def pair_cost(raw_score, target, weight, heavy_weight):
    missed = heavy_weight * target * jnp.log1p(jnp.exp(-raw_score))
    spurious = (1.0 - target) * jnp.log1p(jnp.exp(raw_score))
    return jnp.sum(weight * (missed + spurious))


def local(features, w_in, w_out, bilinear, partner, counts):
    row_part = features.shape[1]
    feature_width = features.shape[4]
    groups = lax.axis_size("mlp")
    site_rows = row_part * groups
    tile_count = lax.axis_size("tile")
    grid_depth = tile_count // 8
    tile_here = lax.axis_index("tile")
    member = lax.axis_index("mlp")
    block_x = tile_here // (4 * grid_depth)
    block_y = tile_here // grid_depth % 4
    block_z = tile_here % grid_depth
    heavy_weight = 27 * site_rows // 4
    score_scale = feature_width ** (-0.5)
    factor = score_scale / (2 * tile_count * site_rows)
    own_rows = member * row_part + jnp.arange(row_part, dtype=jnp.int32)
    all_rows = jnp.arange(site_rows, dtype=jnp.int32)
    mine_counts = lax.dynamic_index_in_dim(counts, tile_here, 0, keepdims=False)
    mine_partner = lax.dynamic_index_in_dim(partner, tile_here, 0, keepdims=False)
    own_partner = lax.dynamic_slice_in_dim(mine_partner, member * row_part, row_part, 1)
    own_pre_ok = own_rows[None, :] < mine_counts[:, 0:1]
    own_post_ok = own_rows[None, :] < mine_counts[:, 1:2]
    local_x = features.reshape(row_part, 4, feature_width)
    weights = butterfly_gather(jnp.stack([w_in.T, w_out], 1), "mlp")
    own_hidden = jnp.einsum("rcf,hf->rch", local_x, weights[:, 0], preferred_element_type=jnp.float32)
    own_active = jax.nn.gelu(own_hidden).astype(jnp.bfloat16)
    mixed_rows = jnp.einsum("rch,hf->rcf", own_active, weights[:, 1], preferred_element_type=jnp.float32)
    embedded = (local_x.astype(jnp.float32) + mixed_rows).astype(jnp.bfloat16)
    pre_local = embedded[:, 0::2]
    post_local = embedded[:, 1::2]
    query_local = jnp.einsum(
        "ruf,fg->rug", pre_local, bilinear, preferred_element_type=jnp.float32
    ).astype(jnp.bfloat16)

    x_stride = 4 * grid_depth
    y_stride = grid_depth
    query_all = butterfly_gather(query_local, "mlp")
    facing = jnp.where(block_x == 0, post_local[:, 1], post_local[:, 0])
    x_pairs = [(s, (s + x_stride) % tile_count) for s in range(tile_count)]
    from_x = lax.ppermute(facing, "tile", x_pairs)
    halo = jnp.stack([from_x, post_local[:, 0], post_local[:, 1]], 0)

    def position(s, stride, extent):
        return (s // stride) % extent

    def along(arr, stride, extent):
        lower = [(s, s + stride) for s in range(tile_count) if position(s, stride, extent) < extent - 1]
        upper = [(s, s - stride) for s in range(tile_count) if position(s, stride, extent) > 0]
        return jnp.stack(
            [lax.ppermute(arr, "tile", lower), arr, lax.ppermute(arr, "tile", upper)], 0
        )

    def along_back(arr, stride, extent):
        lower = [(s, s - stride) for s in range(tile_count) if position(s, stride, extent) > 0]
        upper = [(s, s + stride) for s in range(tile_count) if position(s, stride, extent) < extent - 1]
        return arr[1] + lax.ppermute(arr[0], "tile", lower) + lax.ppermute(arr[2], "tile", upper)

    halo = along(along(halo, y_stride, 4), 1, grid_depth)
    steps = jnp.arange(3, dtype=jnp.int32) - 1
    dz_grid = steps[:, None]
    dy_grid = steps[None, :]
    inside = (
        (block_y + dy_grid >= 0)
        & (block_y + dy_grid < 4)
        & (block_z + dz_grid >= 0)
        & (block_z + dz_grid < grid_depth)
    )
    near = jnp.clip(tile_here + dy_grid * y_stride + dz_grid, 0, tile_count - 1)
    far = (near + x_stride) % tile_count
    col_counts = jnp.stack(
        [counts[far, block_x, 1], counts[near, 0, 1], counts[near, 1, 1]], -1
    )
    j_ok = inside[..., None, None] & (own_rows < col_counts[..., None])
    loss_sum = jnp.zeros((), jnp.float32)
    post_grad_parts = jnp.zeros(halo.shape, jnp.float32)
    query_grads = []
    place = jnp.arange(3, dtype=jnp.int32)
    code_base = (place[None, None, :] * 9 + (dy_grid[..., None] + 1) * 3 + dz_grid[..., None] + 1) * site_rows
    col_key = (code_base[..., None] + own_rows).reshape(-1)
    for pretile, order, edge in ((0, (0, 1, 2), 0), (1, (1, 2, 0), 2)):
        edge_ok = (block_x == 1) if pretile == 0 else (block_x == 0)
        ordered = halo[:, :, order]
        others = ordered.reshape(-1, feature_width)
        x_ok = jnp.stack([edge_ok if p == edge else jnp.bool_(True) for p in range(3)])
        col_ok = (j_ok[:, :, order] & x_ok[None, None, :, None]).reshape(-1)
        queries = query_all[:, pretile]
        raw_score = (
            jnp.einsum("rf,cf->rc", queries, others, preferred_element_type=jnp.float32)
            * score_scale
        )
        row_ok = all_rows < mine_counts[pretile, 0]
        target = (mine_partner[pretile][:, None] == col_key[None, :]).astype(jnp.float32)
        weight = (row_ok[:, None] & col_ok[None, :]).astype(jnp.float32)
        loss_sum = loss_sum + pair_cost(raw_score, target, weight, heavy_weight)
        slope = pair_slope(raw_score, target, weight, heavy_weight, factor)
        query_grads.append(jnp.dot(slope, others, preferred_element_type=jnp.float32))
        back = jnp.einsum("rc,rf->cf", slope, queries, preferred_element_type=jnp.float32)
        back = back.reshape(ordered.shape)
        for p in range(3):
            post_grad_parts = post_grad_parts.at[:, :, order[p]].add(back[:, :, p])
    post_grad_parts = along_back(along_back(post_grad_parts, 1, grid_depth), y_stride, 4)
    back_x = lax.ppermute(post_grad_parts[0], "tile", x_pairs)
    post_back = jnp.stack(
        [
            post_grad_parts[1] + jnp.where(block_x == 1, back_x, 0.0),
            post_grad_parts[2] + jnp.where(block_x == 0, back_x, 0.0),
        ],
        1,
    )
    query_back = butterfly_scatter(jnp.stack(query_grads, 1), "mlp").astype(jnp.bfloat16)
    bilinear_part = jnp.einsum(
        "ruf,rug->fg", pre_local, query_back, preferred_element_type=jnp.float32
    )
    pre_back = jnp.einsum("rug,fg->ruf", query_back, bilinear, preferred_element_type=jnp.float32)
    embed_grad = jnp.stack(
        [pre_back[:, 0], post_back[:, 0], pre_back[:, 1], post_back[:, 1]], 1
    ).astype(jnp.bfloat16)
    whole_x = butterfly_gather(local_x, "mlp")
    hidden_pre = jnp.einsum("rcf,fh->rch", whole_x, w_in, preferred_element_type=jnp.float32)
    active = jax.nn.gelu(hidden_pre).astype(jnp.bfloat16)
    embed_whole = butterfly_gather(embed_grad, "mlp")
    active_grad = jnp.einsum("rcf,hf->rch", embed_whole, w_out, preferred_element_type=jnp.float32)
    unused, pullback = jax.vjp(jax.nn.gelu, hidden_pre)
    hidden_grad = pullback(active_grad)[0].astype(jnp.bfloat16)
    in_part = jnp.einsum("rcf,rch->fh", whole_x, hidden_grad, preferred_element_type=jnp.float32)
    out_part = jnp.einsum("rch,rcf->hf", active, embed_whole, preferred_element_type=jnp.float32)
    width = bilinear_part.shape[1]
    in_rows = in_part.size // width
    out_rows = out_part.size // width
    packed, loss_block = all_reduce(
        jnp.concatenate([bilinear_part, in_part.reshape(-1, width), out_part.reshape(-1, width)], 0),
        jnp.broadcast_to(loss_sum, (8, 128)),
    )
    grad_bilinear = packed[:width]
    loss_total = loss_block[0, 0]
    grad_in = packed[width : width + in_rows].reshape(in_part.shape)
    grad_out = packed[width + in_rows : width + in_rows + out_rows].reshape(out_part.shape)
    pair_loss = loss_total / (2.0 * tile_count * site_rows * 27 * site_rows)
    return (pair_loss, grad_in, grad_out, grad_bilinear)


def solution(mesh):
    placed = (P("tile", "mlp", None, None, None), P(None, "mlp"), P("mlp", None), P(), P(), P())
    return jax.shard_map(
        local,
        mesh=mesh,
        in_specs=placed,
        out_specs=(P(), P(None, "mlp"), P("mlp", None), P()),
        check_vma=False,
    )
```

```python
import functools

import jax
import jax.numpy as jnp
from jax import lax
from jax.experimental import pallas as pl
from jax.experimental.pallas import tpu as pltpu
from jax.sharding import PartitionSpec as P

column_plan = ((-1, 1), (0, 0), (0, 1), (1, 0))


def shifted(array, axis, by):
    peers = lax.axis_size(axis)
    pairs = [(i, i + by) for i in range(peers) if 0 <= i + by < peers]
    return lax.ppermute(array, axis, pairs)


def butterfly_sum(x, axis):
    peers = lax.axis_size(axis)
    step = 1
    while step < peers:
        x = x + lax.ppermute(x, axis, [(i, i ^ step) for i in range(peers)])
        step *= 2
    return x


def butterfly_gather(x, axis):
    peers = lax.axis_size(axis)
    me = lax.axis_index(axis)
    step = 1
    while step < peers:
        other = lax.ppermute(x, axis, [(i, i ^ step) for i in range(peers)])
        low = (me & step) == 0
        x = jnp.where(low, jnp.concatenate([x, other], 0), jnp.concatenate([other, x], 0))
        step *= 2
    return x


def butterfly_scatter(x, axis):
    peers = lax.axis_size(axis)
    me = lax.axis_index(axis)
    step = peers // 2
    while step >= 1:
        half = x.shape[0] // 2
        upper = (me & step) != 0
        send = jnp.where(upper, x[:half], x[half:])
        keep = jnp.where(upper, x[half:], x[:half])
        x = keep + lax.ppermute(send, axis, [(i, i ^ step) for i in range(peers)])
        step //= 2
    return x


MESH = pl.DeviceIdType.MESH


def flip(index, bit):
    return index + bit - 2 * bit * ((index // bit) % 2)


def reduce_kernel(b_ref, i_ref, u_ref, l_ref, gb_ref, gi_ref, gu_ref, lo_ref, o_ref, recv, lrecv, lbuf, send_sem, recv_sem, lsend_sem, lrecv_sem):
    coords = {axis: lax.axis_index(axis) for axis in ("tile", "mlp")}
    tile_groups = ((1,), (2,), (16, 4, 8))
    mlp_bits = (2, 1, 4)

    def partner(axis, bits, distance):
        index = coords[axis]
        for place, bit in enumerate(bits):
            if (distance >> place) & 1:
                index = flip(index, bit)
        return index

    def rank(axis, bits, distance=0):
        total = 0
        for place, bit in enumerate(bits):
            own = (coords[axis] // bit) % 2
            if (distance >> place) & 1:
                own = 1 - own
            total = total + own * (1 << place)
        return total

    def ordered_sum(blocks, axis, bits):
        fan = 1 << len(bits)
        if fan == 2:
            return blocks[0] + blocks[1]
        total = None
        for q in range(fan):
            pick = None
            for distance in range(fan):
                term = jnp.where(rank(axis, bits, distance) == q, blocks[distance], 0.0)
                pick = term if pick is None else pick + term
            total = pick if total is None else total + pick
        return total

    steps = [("tile", bits) for bits in tile_groups] + [("mlp", mlp_bits)]
    barrier = pltpu.get_barrier_semaphore()
    greeted = 0
    for axis, bits in steps:
        for distance in range(1, 1 << len(bits)):
            pl.semaphore_signal(
                barrier, inc=1, device_id={axis: partner(axis, bits, distance)}, device_id_type=MESH
            )
            greeted += 1
    width = b_ref.shape[0]
    half = i_ref.shape[1]
    o_ref[pl.ds(0, width)] = b_ref[...]
    o_ref[pl.ds(width, half), pl.ds(0, half)] = i_ref[pl.ds(0, half)]
    o_ref[pl.ds(width, half), pl.ds(half, half)] = i_ref[pl.ds(half, half)]
    o_ref[pl.ds(width + half, half)] = u_ref[...]
    pl.semaphore_wait(barrier, greeted)

    def send_all(axis, bits, slot, sources, length, loss_slot=None):
        copies = []
        for distance in range(1, 1 << len(bits)):
            target = {axis: partner(axis, bits, distance)}
            copy = pltpu.make_async_remote_copy(
                src_ref=o_ref.at[pl.ds(pl.multiple_of(sources(distance), 8), length)],
                dst_ref=recv.at[slot + distance - 1, pl.ds(0, length)],
                send_sem=send_sem.at[slot + distance - 1],
                recv_sem=recv_sem.at[slot + distance - 1],
                device_id=target,
                device_id_type=MESH,
            )
            copy.start()
            copies.append(copy)
            if loss_slot is not None:
                copy = pltpu.make_async_remote_copy(
                    src_ref=lbuf.at[loss_slot[0]],
                    dst_ref=lrecv.at[loss_slot[1] + distance - 1],
                    send_sem=lsend_sem.at[loss_slot[1] + distance - 1],
                    recv_sem=lrecv_sem.at[loss_slot[1] + distance - 1],
                    device_id=target,
                    device_id_type=MESH,
                )
                copy.start()
                copies.append(copy)
        for copy in copies:
            copy.wait()

    loss = l_ref[...]
    slot = 0
    lslot = 0
    start = 0
    length = o_ref.shape[0]
    for stage, (axis, bits) in enumerate(steps):
        fan = 1 << len(bits)
        lbuf[stage] = loss
        if axis == "tile":
            length //= fan
            send_all(axis, bits, slot, lambda d: start + rank(axis, bits, d) * length, length, (stage, lslot))
            start = start + rank(axis, bits) * length
            mine = pl.ds(pl.multiple_of(start, 8), length)
            total = o_ref[mine]
            for distance in range(1, fan):
                total = total + recv[slot + distance - 1, pl.ds(0, length)]
            o_ref[mine] = total
        else:
            send_all(axis, bits, slot, lambda d: start, length, (stage, lslot))
            mine = pl.ds(pl.multiple_of(start, 8), length)
            own = o_ref[mine]
            blocks = [own] + [recv[slot + distance - 1, pl.ds(0, length)] for distance in range(1, fan)]
            o_ref[mine] = jnp.where(start < width, ordered_sum(blocks, axis, bits), own)
        loss = ordered_sum([loss] + [lrecv[lslot + distance - 1] for distance in range(1, fan)], axis, bits)
        slot += fan - 1
        lslot += fan - 1
    lo_ref[...] = loss
    for bits in reversed(tile_groups):
        fan = 1 << len(bits)
        send_all("tile", bits, slot, lambda d: start, length)
        base = start - rank("tile", bits) * length
        for distance in range(1, fan):
            spot = base + rank("tile", bits, distance) * length
            o_ref[pl.ds(pl.multiple_of(spot, 8), length)] = recv[slot + distance - 1, pl.ds(0, length)]
        start = base
        length *= fan
        slot += fan - 1
    gb_ref[...] = o_ref[pl.ds(0, width)]
    gi_ref[pl.ds(0, half)] = o_ref[pl.ds(width, half), pl.ds(0, half)]
    gi_ref[pl.ds(half, half)] = o_ref[pl.ds(width, half), pl.ds(half, half)]
    gu_ref[...] = o_ref[pl.ds(width + half, half)]


def all_reduce(bilinear_part, in_part, out_part, loss_block):
    packed = jax.ShapeDtypeStruct((bilinear_part.shape[0] * 2,) + bilinear_part.shape[1:], bilinear_part.dtype)
    slots = 2 * (1 + 1 + 7) + 7
    loss_slots = 1 + 1 + 7 + 7
    return pl.pallas_call(
        reduce_kernel,
        out_shape=tuple(
            jax.ShapeDtypeStruct(part.shape, part.dtype)
            for part in (bilinear_part, in_part, out_part, loss_block)
        ),
        in_specs=[pl.BlockSpec(memory_space=pltpu.VMEM)] * 4,
        out_specs=tuple(pl.BlockSpec(memory_space=pltpu.VMEM) for _ in range(4)),
        scratch_shapes=[
            pltpu.VMEM(packed.shape, packed.dtype),
            pltpu.VMEM((slots, packed.shape[0] // 2) + packed.shape[1:], packed.dtype),
            pltpu.VMEM((loss_slots,) + loss_block.shape, loss_block.dtype),
            pltpu.VMEM((4,) + loss_block.shape, loss_block.dtype),
            pltpu.SemaphoreType.DMA((slots,)),
            pltpu.SemaphoreType.DMA((slots,)),
            pltpu.SemaphoreType.DMA((loss_slots,)),
            pltpu.SemaphoreType.DMA((loss_slots,)),
        ],
        compiler_params=pltpu.CompilerParams(collective_id=0, has_side_effects=True),
    )(bilinear_part, in_part, out_part, loss_block)

def pair_slope(raw_score, target, weight, heavy_weight, factor):
    chance = jax.nn.sigmoid(raw_score)
    signed = (1.0 - target) * chance - heavy_weight * target * (1.0 - chance)
    return (weight * signed * factor).astype(jnp.bfloat16)


def pair_cost(raw_score, target, weight, heavy_weight):
    missed = heavy_weight * target * jnp.log1p(jnp.exp(-raw_score))
    spurious = (1.0 - target) * jnp.log1p(jnp.exp(raw_score))
    return jnp.sum(weight * (missed + spurious))


def local(features, w_in, w_out, bilinear, partner, counts):
    row_part = features.shape[1]
    feature_width = features.shape[4]
    groups = lax.axis_size("mlp")
    site_rows = row_part * groups
    tile_count = lax.axis_size("tile")
    grid_depth = tile_count // 8
    tile_here = lax.axis_index("tile")
    member = lax.axis_index("mlp")
    block_x = tile_here // (4 * grid_depth)
    block_y = tile_here // grid_depth % 4
    block_z = tile_here % grid_depth
    heavy_weight = 27 * site_rows // 4
    score_scale = feature_width ** (-0.5)
    factor = score_scale / (2 * tile_count * site_rows)
    own_rows = member * row_part + jnp.arange(row_part, dtype=jnp.int32)
    all_rows = jnp.arange(site_rows, dtype=jnp.int32)
    mine_counts = lax.dynamic_index_in_dim(counts, tile_here, 0, keepdims=False)
    mine_partner = lax.dynamic_index_in_dim(partner, tile_here, 0, keepdims=False)
    own_partner = lax.dynamic_slice_in_dim(mine_partner, member * row_part, row_part, 1)
    own_pre_ok = own_rows[None, :] < mine_counts[:, 0:1]
    own_post_ok = own_rows[None, :] < mine_counts[:, 1:2]
    local_x = features.reshape(row_part, 4, feature_width)
    weights = butterfly_gather(jnp.stack([w_in.T, w_out], 1), "mlp")
    own_hidden = jnp.einsum("rcf,hf->rch", local_x, weights[:, 0], preferred_element_type=jnp.float32)
    own_active = jax.nn.gelu(own_hidden).astype(jnp.bfloat16)
    mixed_rows = jnp.einsum("rch,hf->rcf", own_active, weights[:, 1], preferred_element_type=jnp.float32)
    embedded = (local_x.astype(jnp.float32) + mixed_rows).astype(jnp.bfloat16)
    pre_local = embedded[:, 0::2]
    post_local = embedded[:, 1::2]
    query_local = jnp.einsum(
        "ruf,fg->rug", pre_local, bilinear, preferred_element_type=jnp.float32
    ).astype(jnp.bfloat16)

    x_stride = 4 * grid_depth
    y_stride = grid_depth
    query_all = butterfly_gather(query_local, "mlp")
    facing = jnp.where(block_x == 0, post_local[:, 1], post_local[:, 0])
    x_pairs = [(s, (s + x_stride) % tile_count) for s in range(tile_count)]
    from_x = lax.ppermute(facing, "tile", x_pairs)
    halo = jnp.stack([from_x, post_local[:, 0], post_local[:, 1]], 0)

    def position(s, stride, extent):
        return (s // stride) % extent

    def along(arr, stride, extent):
        lower = [(s, s + stride) for s in range(tile_count) if position(s, stride, extent) < extent - 1]
        upper = [(s, s - stride) for s in range(tile_count) if position(s, stride, extent) > 0]
        return jnp.stack(
            [lax.ppermute(arr, "tile", lower), arr, lax.ppermute(arr, "tile", upper)], 0
        )

    def along_back(arr, stride, extent):
        lower = [(s, s - stride) for s in range(tile_count) if position(s, stride, extent) > 0]
        upper = [(s, s + stride) for s in range(tile_count) if position(s, stride, extent) < extent - 1]
        return arr[1] + lax.ppermute(arr[0], "tile", lower) + lax.ppermute(arr[2], "tile", upper)

    halo = along(along(halo, y_stride, 4), 1, grid_depth)
    steps = jnp.arange(3, dtype=jnp.int32) - 1
    dz_grid = steps[:, None]
    dy_grid = steps[None, :]
    inside = (
        (block_y + dy_grid >= 0)
        & (block_y + dy_grid < 4)
        & (block_z + dz_grid >= 0)
        & (block_z + dz_grid < grid_depth)
    )
    near = jnp.clip(tile_here + dy_grid * y_stride + dz_grid, 0, tile_count - 1)
    far = (near + x_stride) % tile_count
    col_counts = jnp.stack(
        [counts[far, block_x, 1], counts[near, 0, 1], counts[near, 1, 1]], -1
    )
    j_ok = inside[..., None, None] & (own_rows < col_counts[..., None])
    loss_sum = jnp.zeros((), jnp.float32)
    post_grad_parts = jnp.zeros(halo.shape, jnp.float32)
    query_grads = []
    place = jnp.arange(3, dtype=jnp.int32)
    code_base = (place[None, None, :] * 9 + (dy_grid[..., None] + 1) * 3 + dz_grid[..., None] + 1) * site_rows
    col_key = (code_base[..., None] + own_rows).reshape(-1)
    for pretile, order, edge in ((0, (0, 1, 2), 0), (1, (1, 2, 0), 2)):
        edge_ok = (block_x == 1) if pretile == 0 else (block_x == 0)
        ordered = halo[:, :, order]
        others = ordered.reshape(-1, feature_width)
        x_ok = jnp.stack([edge_ok if p == edge else jnp.bool_(True) for p in range(3)])
        col_ok = (j_ok[:, :, order] & x_ok[None, None, :, None]).reshape(-1)
        queries = query_all[:, pretile]
        raw_score = (
            jnp.einsum("rf,cf->rc", queries, others, preferred_element_type=jnp.float32)
            * score_scale
        )
        row_ok = all_rows < mine_counts[pretile, 0]
        target = (mine_partner[pretile][:, None] == col_key[None, :]).astype(jnp.float32)
        weight = (row_ok[:, None] & col_ok[None, :]).astype(jnp.float32)
        loss_sum = loss_sum + pair_cost(raw_score, target, weight, heavy_weight)
        slope = pair_slope(raw_score, target, weight, heavy_weight, factor)
        query_grads.append(jnp.dot(slope, others, preferred_element_type=jnp.float32))
        back = jnp.einsum("rc,rf->cf", slope, queries, preferred_element_type=jnp.float32)
        back = back.reshape(ordered.shape)
        for p in range(3):
            post_grad_parts = post_grad_parts.at[:, :, order[p]].add(back[:, :, p])
    post_grad_parts = along_back(along_back(post_grad_parts, 1, grid_depth), y_stride, 4)
    back_x = lax.ppermute(post_grad_parts[0], "tile", x_pairs)
    post_back = jnp.stack(
        [
            post_grad_parts[1] + jnp.where(block_x == 1, back_x, 0.0),
            post_grad_parts[2] + jnp.where(block_x == 0, back_x, 0.0),
        ],
        1,
    )
    query_back = butterfly_scatter(jnp.stack(query_grads, 1), "mlp").astype(jnp.bfloat16)
    bilinear_part = jnp.einsum(
        "ruf,rug->fg", pre_local, query_back, preferred_element_type=jnp.float32
    )
    pre_back = jnp.einsum("rug,fg->ruf", query_back, bilinear, preferred_element_type=jnp.float32)
    embed_grad = jnp.stack(
        [pre_back[:, 0], post_back[:, 0], pre_back[:, 1], post_back[:, 1]], 1
    ).astype(jnp.bfloat16)
    whole_x = butterfly_gather(local_x, "mlp")
    hidden_pre = jnp.einsum("rcf,fh->rch", whole_x, w_in, preferred_element_type=jnp.float32)
    active = jax.nn.gelu(hidden_pre).astype(jnp.bfloat16)
    embed_whole = butterfly_gather(embed_grad, "mlp")
    active_grad = jnp.einsum("rcf,hf->rch", embed_whole, w_out, preferred_element_type=jnp.float32)
    unused, pullback = jax.vjp(jax.nn.gelu, hidden_pre)
    hidden_grad = pullback(active_grad)[0].astype(jnp.bfloat16)
    in_part = jnp.einsum("rcf,rch->fh", whole_x, hidden_grad, preferred_element_type=jnp.float32)
    out_part = jnp.einsum("rch,rcf->hf", active, embed_whole, preferred_element_type=jnp.float32)
    grad_bilinear, grad_in, grad_out, loss_block = all_reduce(
        bilinear_part, in_part, out_part, jnp.broadcast_to(loss_sum, (8, 128))
    )
    loss_total = loss_block[0, 0]
    pair_loss = loss_total / (2.0 * tile_count * site_rows * 27 * site_rows)
    return (pair_loss, grad_in, grad_out, grad_bilinear)


def solution(mesh):
    placed = (P("tile", "mlp", None, None, None), P(None, "mlp"), P("mlp", None), P(), P(), P())
    return jax.shard_map(
        local,
        mesh=mesh,
        in_specs=placed,
        out_specs=(P(), P(None, "mlp"), P("mlp", None), P()),
        check_vma=False,
    )
```

```python
import functools

import jax
import jax.numpy as jnp
from jax import lax
from jax.experimental import pallas as pl
from jax.experimental.pallas import tpu as pltpu
from jax.sharding import PartitionSpec as P

column_plan = ((-1, 1), (0, 0), (0, 1), (1, 0))


def shifted(array, axis, by):
    peers = lax.axis_size(axis)
    pairs = [(i, i + by) for i in range(peers) if 0 <= i + by < peers]
    return lax.ppermute(array, axis, pairs)


def butterfly_sum(x, axis):
    peers = lax.axis_size(axis)
    step = 1
    while step < peers:
        x = x + lax.ppermute(x, axis, [(i, i ^ step) for i in range(peers)])
        step *= 2
    return x


def butterfly_gather(x, axis):
    peers = lax.axis_size(axis)
    me = lax.axis_index(axis)
    step = 1
    while step < peers:
        other = lax.ppermute(x, axis, [(i, i ^ step) for i in range(peers)])
        low = (me & step) == 0
        x = jnp.where(low, jnp.concatenate([x, other], 0), jnp.concatenate([other, x], 0))
        step *= 2
    return x


def butterfly_scatter(x, axis):
    peers = lax.axis_size(axis)
    me = lax.axis_index(axis)
    step = peers // 2
    while step >= 1:
        half = x.shape[0] // 2
        upper = (me & step) != 0
        send = jnp.where(upper, x[:half], x[half:])
        keep = jnp.where(upper, x[half:], x[:half])
        x = keep + lax.ppermute(send, axis, [(i, i ^ step) for i in range(peers)])
        step //= 2
    return x


MESH = pl.DeviceIdType.MESH


def flip(index, bit):
    return index + bit - 2 * bit * ((index // bit) % 2)


def reduce_kernel(b_ref, i_ref, u_ref, l_ref, gb_ref, gi_ref, gu_ref, lo_ref, o_ref, recv, lrecv, lbuf, send_sem, recv_sem, lsend_sem, lrecv_sem):
    coords = {axis: lax.axis_index(axis) for axis in ("tile", "mlp")}
    tile_groups = ((1,), (2,), (16, 4, 8))
    mlp_bits = (2, 1, 4)

    def partner(axis, bits, distance):
        index = coords[axis]
        for place, bit in enumerate(bits):
            if (distance >> place) & 1:
                index = flip(index, bit)
        return index

    def rank(axis, bits, distance=0):
        total = 0
        for place, bit in enumerate(bits):
            own = (coords[axis] // bit) % 2
            if (distance >> place) & 1:
                own = 1 - own
            total = total + own * (1 << place)
        return total

    def ordered_sum(blocks, axis, bits):
        fan = 1 << len(bits)
        if fan == 2:
            return blocks[0] + blocks[1]
        total = None
        for q in range(fan):
            pick = None
            for distance in range(fan):
                term = jnp.where(rank(axis, bits, distance) == q, blocks[distance], 0.0)
                pick = term if pick is None else pick + term
            total = pick if total is None else total + pick
        return total

    steps = [("tile", bits) for bits in tile_groups] + [("mlp", mlp_bits)]
    barrier = pltpu.get_barrier_semaphore()
    greeted = 0
    for axis, bits in steps:
        for distance in range(1, 1 << len(bits)):
            pl.semaphore_signal(
                barrier, inc=1, device_id={axis: partner(axis, bits, distance)}, device_id_type=MESH
            )
            greeted += 1
    width = b_ref.shape[0]
    half = i_ref.shape[1]
    o_ref[pl.ds(0, width)] = b_ref[...]
    o_ref[pl.ds(width, half), pl.ds(0, half)] = i_ref[pl.ds(0, half)]
    o_ref[pl.ds(width, half), pl.ds(half, half)] = i_ref[pl.ds(half, half)]
    o_ref[pl.ds(width + half, half)] = u_ref[...]
    pl.semaphore_wait(barrier, greeted)

    def send_all(axis, bits, slot, sources, length, loss_slot=None):
        copies = []
        for distance in range(1, 1 << len(bits)):
            target = {axis: partner(axis, bits, distance)}
            copy = pltpu.make_async_remote_copy(
                src_ref=o_ref.at[pl.ds(pl.multiple_of(sources(distance), 8), length)],
                dst_ref=recv.at[slot + distance - 1, pl.ds(0, length)],
                send_sem=send_sem.at[slot + distance - 1],
                recv_sem=recv_sem.at[slot + distance - 1],
                device_id=target,
                device_id_type=MESH,
            )
            copy.start()
            copies.append(copy)
            if loss_slot is not None:
                copy = pltpu.make_async_remote_copy(
                    src_ref=lbuf.at[loss_slot[0]],
                    dst_ref=lrecv.at[loss_slot[1] + distance - 1],
                    send_sem=lsend_sem.at[loss_slot[1] + distance - 1],
                    recv_sem=lrecv_sem.at[loss_slot[1] + distance - 1],
                    device_id=target,
                    device_id_type=MESH,
                )
                copy.start()
                copies.append(copy)
        for copy in copies:
            copy.wait()

    loss = l_ref[...]
    slot = 0
    lslot = 0
    start = 0
    length = o_ref.shape[0]
    for stage, (axis, bits) in enumerate(steps):
        fan = 1 << len(bits)
        lbuf[stage] = loss
        if axis == "tile":
            length //= fan
            send_all(axis, bits, slot, lambda d: start + rank(axis, bits, d) * length, length, (stage, lslot))
            start = start + rank(axis, bits) * length
            mine = pl.ds(pl.multiple_of(start, 8), length)
            total = o_ref[mine]
            for distance in range(1, fan):
                total = total + recv[slot + distance - 1, pl.ds(0, length)]
            o_ref[mine] = total
        else:
            send_all(axis, bits, slot, lambda d: start, length, (stage, lslot))
            mine = pl.ds(pl.multiple_of(start, 8), length)
            own = o_ref[mine]
            blocks = [own] + [recv[slot + distance - 1, pl.ds(0, length)] for distance in range(1, fan)]
            o_ref[mine] = jnp.where(start < width, ordered_sum(blocks, axis, bits), own)
        loss = ordered_sum([loss] + [lrecv[lslot + distance - 1] for distance in range(1, fan)], axis, bits)
        slot += fan - 1
        lslot += fan - 1
    lo_ref[...] = loss
    for bits in reversed(tile_groups):
        fan = 1 << len(bits)
        send_all("tile", bits, slot, lambda d: start, length)
        base = start - rank("tile", bits) * length
        for distance in range(1, fan):
            spot = base + rank("tile", bits, distance) * length
            o_ref[pl.ds(pl.multiple_of(spot, 8), length)] = recv[slot + distance - 1, pl.ds(0, length)]
        start = base
        length *= fan
        slot += fan - 1
    gb_ref[...] = o_ref[pl.ds(0, width)]
    gi_ref[pl.ds(0, half)] = o_ref[pl.ds(width, half), pl.ds(0, half)]
    gi_ref[pl.ds(half, half)] = o_ref[pl.ds(width, half), pl.ds(half, half)]
    gu_ref[...] = o_ref[pl.ds(width + half, half)]


def all_reduce(bilinear_part, in_part, out_part, loss_block):
    packed = jax.ShapeDtypeStruct((bilinear_part.shape[0] * 2,) + bilinear_part.shape[1:], bilinear_part.dtype)
    slots = 2 * (1 + 1 + 7) + 7
    loss_slots = 1 + 1 + 7 + 7
    return pl.pallas_call(
        reduce_kernel,
        out_shape=tuple(
            jax.ShapeDtypeStruct(part.shape, part.dtype)
            for part in (bilinear_part, in_part, out_part, loss_block)
        ),
        in_specs=[pl.BlockSpec(memory_space=pltpu.VMEM)] * 4,
        out_specs=tuple(pl.BlockSpec(memory_space=pltpu.VMEM) for _ in range(4)),
        scratch_shapes=[
            pltpu.VMEM(packed.shape, packed.dtype),
            pltpu.VMEM((slots, packed.shape[0] // 2) + packed.shape[1:], packed.dtype),
            pltpu.VMEM((loss_slots,) + loss_block.shape, loss_block.dtype),
            pltpu.VMEM((4,) + loss_block.shape, loss_block.dtype),
            pltpu.SemaphoreType.DMA((slots,)),
            pltpu.SemaphoreType.DMA((slots,)),
            pltpu.SemaphoreType.DMA((loss_slots,)),
            pltpu.SemaphoreType.DMA((loss_slots,)),
        ],
        compiler_params=pltpu.CompilerParams(collective_id=0, has_side_effects=True),
    )(bilinear_part, in_part, out_part, loss_block)

def pair_slope(raw_score, target, weight, heavy_weight, factor):
    chance = jax.nn.sigmoid(raw_score)
    signed = (1.0 - target) * chance - heavy_weight * target * (1.0 - chance)
    return (weight * signed * factor).astype(jnp.bfloat16)


def pair_cost(raw_score, target, weight, heavy_weight):
    missed = heavy_weight * target * jnp.log1p(jnp.exp(-raw_score))
    spurious = (1.0 - target) * jnp.log1p(jnp.exp(raw_score))
    return jnp.sum(weight * (missed + spurious))


def local(features, w_in, w_out, bilinear, partner, counts):
    row_part = features.shape[1]
    feature_width = features.shape[4]
    groups = lax.axis_size("mlp")
    site_rows = row_part * groups
    tile_count = lax.axis_size("tile")
    grid_depth = tile_count // 8
    tile_here = lax.axis_index("tile")
    member = lax.axis_index("mlp")
    block_x = tile_here // (4 * grid_depth)
    block_y = tile_here // grid_depth % 4
    block_z = tile_here % grid_depth
    heavy_weight = 27 * site_rows // 4
    score_scale = feature_width ** (-0.5)
    factor = score_scale / (2 * tile_count * site_rows)
    own_rows = member * row_part + jnp.arange(row_part, dtype=jnp.int32)
    all_rows = jnp.arange(site_rows, dtype=jnp.int32)
    mine_counts = lax.dynamic_index_in_dim(counts, tile_here, 0, keepdims=False)
    mine_partner = lax.dynamic_index_in_dim(partner, tile_here, 0, keepdims=False)
    own_partner = lax.dynamic_slice_in_dim(mine_partner, member * row_part, row_part, 1)
    own_pre_ok = own_rows[None, :] < mine_counts[:, 0:1]
    own_post_ok = own_rows[None, :] < mine_counts[:, 1:2]
    local_x = features.reshape(row_part, 4, feature_width)
    weights = butterfly_gather(jnp.stack([w_in.T, w_out], 1), "mlp")
    own_hidden = jnp.einsum("rcf,hf->rch", local_x, weights[:, 0], preferred_element_type=jnp.float32)
    own_active = jax.nn.gelu(own_hidden).astype(jnp.bfloat16)
    mixed_rows = jnp.einsum("rch,hf->rcf", own_active, weights[:, 1], preferred_element_type=jnp.float32)
    embedded = (local_x.astype(jnp.float32) + mixed_rows).astype(jnp.bfloat16)
    pre_local = embedded[:, 0::2]
    post_local = embedded[:, 1::2]
    query_local = jnp.einsum(
        "ruf,fg->rug", pre_local, bilinear, preferred_element_type=jnp.float32
    ).astype(jnp.bfloat16)

    x_stride = 4 * grid_depth
    y_stride = grid_depth
    query_all = butterfly_gather(query_local, "mlp")
    facing = jnp.where(block_x == 0, post_local[:, 1], post_local[:, 0])
    x_pairs = [(s, (s + x_stride) % tile_count) for s in range(tile_count)]
    from_x = lax.ppermute(facing, "tile", x_pairs)
    halo = jnp.stack([from_x, post_local[:, 0], post_local[:, 1]], 0)

    def position(s, stride, extent):
        return (s // stride) % extent

    def along(arr, stride, extent):
        lower = [(s, s + stride) for s in range(tile_count) if position(s, stride, extent) < extent - 1]
        upper = [(s, s - stride) for s in range(tile_count) if position(s, stride, extent) > 0]
        return jnp.stack(
            [lax.ppermute(arr, "tile", lower), arr, lax.ppermute(arr, "tile", upper)], 0
        )

    def along_back(arr, stride, extent):
        lower = [(s, s - stride) for s in range(tile_count) if position(s, stride, extent) > 0]
        upper = [(s, s + stride) for s in range(tile_count) if position(s, stride, extent) < extent - 1]
        return arr[1] + lax.ppermute(arr[0], "tile", lower) + lax.ppermute(arr[2], "tile", upper)

    halo = along(along(halo, y_stride, 4), 1, grid_depth)
    steps = jnp.arange(3, dtype=jnp.int32) - 1
    dz_grid = steps[:, None]
    dy_grid = steps[None, :]
    inside = (
        (block_y + dy_grid >= 0)
        & (block_y + dy_grid < 4)
        & (block_z + dz_grid >= 0)
        & (block_z + dz_grid < grid_depth)
    )
    near = jnp.clip(tile_here + dy_grid * y_stride + dz_grid, 0, tile_count - 1)
    far = (near + x_stride) % tile_count
    col_counts = jnp.stack(
        [counts[far, block_x, 1], counts[near, 0, 1], counts[near, 1, 1]], -1
    )
    j_ok = inside[..., None, None] & (own_rows < col_counts[..., None])
    loss_sum = jnp.zeros((), jnp.float32)
    post_grad_parts = jnp.zeros(halo.shape, jnp.float32)
    query_grads = []
    place = jnp.arange(3, dtype=jnp.int32)
    code_base = (place[None, None, :] * 9 + (dy_grid[..., None] + 1) * 3 + dz_grid[..., None] + 1) * site_rows
    col_key = (code_base[..., None] + own_rows).reshape(-1)
    for pretile, order, edge in ((0, (0, 1, 2), 0), (1, (1, 2, 0), 2)):
        edge_ok = (block_x == 1) if pretile == 0 else (block_x == 0)
        ordered = halo[:, :, order]
        others = ordered.reshape(-1, feature_width)
        x_ok = jnp.stack([edge_ok if p == edge else jnp.bool_(True) for p in range(3)])
        col_ok = (j_ok[:, :, order] & x_ok[None, None, :, None]).reshape(-1)
        queries = query_all[:, pretile]
        raw_score = (
            jnp.einsum("rf,cf->rc", queries, others, preferred_element_type=jnp.float32)
            * score_scale
        )
        row_ok = all_rows < mine_counts[pretile, 0]
        target = (mine_partner[pretile][:, None] == col_key[None, :]).astype(jnp.float32)
        weight = (row_ok[:, None] & col_ok[None, :]).astype(jnp.float32)
        decay = jnp.exp(-jnp.abs(raw_score))
        soft = jnp.log1p(decay)
        inverse = 1.0 / (1.0 + decay)
        ahead = raw_score >= 0
        missed = heavy_weight * target * (jnp.maximum(-raw_score, 0.0) + soft)
        spurious = (1.0 - target) * (jnp.maximum(raw_score, 0.0) + soft)
        loss_sum = loss_sum + jnp.sum(weight * (missed + spurious))
        chance = jnp.where(ahead, inverse, decay * inverse)
        doubt = jnp.where(ahead, decay * inverse, inverse)
        signed = (1.0 - target) * chance - heavy_weight * target * doubt
        slope = (weight * signed * factor).astype(jnp.bfloat16)
        query_grads.append(jnp.dot(slope, others, preferred_element_type=jnp.float32))
        back = jnp.einsum("rc,rf->cf", slope, queries, preferred_element_type=jnp.float32)
        back = back.reshape(ordered.shape)
        for p in range(3):
            post_grad_parts = post_grad_parts.at[:, :, order[p]].add(back[:, :, p])
    post_grad_parts = along_back(along_back(post_grad_parts, 1, grid_depth), y_stride, 4)
    back_x = lax.ppermute(post_grad_parts[0], "tile", x_pairs)
    post_back = jnp.stack(
        [
            post_grad_parts[1] + jnp.where(block_x == 1, back_x, 0.0),
            post_grad_parts[2] + jnp.where(block_x == 0, back_x, 0.0),
        ],
        1,
    )
    query_back = butterfly_scatter(jnp.stack(query_grads, 1), "mlp").astype(jnp.bfloat16)
    bilinear_part = jnp.einsum(
        "ruf,rug->fg", pre_local, query_back, preferred_element_type=jnp.float32
    )
    pre_back = jnp.einsum("rug,fg->ruf", query_back, bilinear, preferred_element_type=jnp.float32)
    embed_grad = jnp.stack(
        [pre_back[:, 0], post_back[:, 0], pre_back[:, 1], post_back[:, 1]], 1
    ).astype(jnp.bfloat16)
    whole_x = butterfly_gather(local_x, "mlp")
    hidden_pre = jnp.einsum("rcf,fh->rch", whole_x, w_in, preferred_element_type=jnp.float32)
    active = jax.nn.gelu(hidden_pre).astype(jnp.bfloat16)
    embed_whole = butterfly_gather(embed_grad, "mlp")
    active_grad = jnp.einsum("rcf,hf->rch", embed_whole, w_out, preferred_element_type=jnp.float32)
    unused, pullback = jax.vjp(jax.nn.gelu, hidden_pre)
    hidden_grad = pullback(active_grad)[0].astype(jnp.bfloat16)
    in_part = jnp.einsum("rcf,rch->fh", whole_x, hidden_grad, preferred_element_type=jnp.float32)
    out_part = jnp.einsum("rch,rcf->hf", active, embed_whole, preferred_element_type=jnp.float32)
    grad_bilinear, grad_in, grad_out, loss_block = all_reduce(
        bilinear_part, in_part, out_part, jnp.broadcast_to(loss_sum, (8, 128))
    )
    loss_total = loss_block[0, 0]
    pair_loss = loss_total / (2.0 * tile_count * site_rows * 27 * site_rows)
    return (pair_loss, grad_in, grad_out, grad_bilinear)


def solution(mesh):
    placed = (P("tile", "mlp", None, None, None), P(None, "mlp"), P("mlp", None), P(), P(), P())
    return jax.shard_map(
        local,
        mesh=mesh,
        in_specs=placed,
        out_specs=(P(), P(None, "mlp"), P("mlp", None), P()),
        check_vma=False,
    )
```

```python
import functools

import jax
import jax.numpy as jnp
from jax import lax
from jax.experimental import pallas as pl
from jax.experimental.pallas import tpu as pltpu
from jax.sharding import PartitionSpec as P

column_plan = ((-1, 1), (0, 0), (0, 1), (1, 0))


def shifted(array, axis, by):
    peers = lax.axis_size(axis)
    pairs = [(i, i + by) for i in range(peers) if 0 <= i + by < peers]
    return lax.ppermute(array, axis, pairs)


def butterfly_sum(x, axis):
    peers = lax.axis_size(axis)
    step = 1
    while step < peers:
        x = x + lax.ppermute(x, axis, [(i, i ^ step) for i in range(peers)])
        step *= 2
    return x


def butterfly_gather(x, axis):
    peers = lax.axis_size(axis)
    me = lax.axis_index(axis)
    step = 1
    while step < peers:
        other = lax.ppermute(x, axis, [(i, i ^ step) for i in range(peers)])
        low = (me & step) == 0
        x = jnp.where(low, jnp.concatenate([x, other], 0), jnp.concatenate([other, x], 0))
        step *= 2
    return x


def butterfly_scatter(x, axis):
    peers = lax.axis_size(axis)
    me = lax.axis_index(axis)
    step = peers // 2
    while step >= 1:
        half = x.shape[0] // 2
        upper = (me & step) != 0
        send = jnp.where(upper, x[:half], x[half:])
        keep = jnp.where(upper, x[half:], x[:half])
        x = keep + lax.ppermute(send, axis, [(i, i ^ step) for i in range(peers)])
        step //= 2
    return x


MESH = pl.DeviceIdType.MESH


def flip(index, bit):
    return index + bit - 2 * bit * ((index // bit) % 2)


def reduce_kernel(b_ref, i_ref, u_ref, l_ref, gb_ref, gi_ref, gu_ref, lo_ref, o_ref, recv, lrecv, lbuf, send_sem, recv_sem, lsend_sem, lrecv_sem):
    coords = {axis: lax.axis_index(axis) for axis in ("tile", "mlp")}
    tile_groups = ((1,), (2,), (16, 4, 8))
    mlp_bits = (2, 1, 4)

    def partner(axis, bits, distance):
        index = coords[axis]
        for place, bit in enumerate(bits):
            if (distance >> place) & 1:
                index = flip(index, bit)
        return index

    def rank(axis, bits, distance=0):
        total = 0
        for place, bit in enumerate(bits):
            own = (coords[axis] // bit) % 2
            if (distance >> place) & 1:
                own = 1 - own
            total = total + own * (1 << place)
        return total

    def ordered_sum(blocks, axis, bits):
        fan = 1 << len(bits)
        if fan == 2:
            return blocks[0] + blocks[1]
        total = None
        for q in range(fan):
            pick = None
            for distance in range(fan):
                term = jnp.where(rank(axis, bits, distance) == q, blocks[distance], 0.0)
                pick = term if pick is None else pick + term
            total = pick if total is None else total + pick
        return total

    steps = [("tile", bits) for bits in tile_groups] + [("mlp", mlp_bits)]
    barrier = pltpu.get_barrier_semaphore()
    greeted = 0
    for axis, bits in steps:
        for distance in range(1, 1 << len(bits)):
            pl.semaphore_signal(
                barrier, inc=1, device_id={axis: partner(axis, bits, distance)}, device_id_type=MESH
            )
            greeted += 1
    width = b_ref.shape[0]
    half = i_ref.shape[1]
    o_ref[pl.ds(0, width)] = b_ref[...]
    o_ref[pl.ds(width, half), pl.ds(0, half)] = i_ref[pl.ds(0, half)]
    o_ref[pl.ds(width, half), pl.ds(half, half)] = i_ref[pl.ds(half, half)]
    o_ref[pl.ds(width + half, half)] = u_ref[...]
    pl.semaphore_wait(barrier, greeted)

    def send_all(axis, bits, slot, sources, length, loss_slot=None):
        copies = []
        for distance in range(1, 1 << len(bits)):
            target = {axis: partner(axis, bits, distance)}
            copy = pltpu.make_async_remote_copy(
                src_ref=o_ref.at[pl.ds(pl.multiple_of(sources(distance), 8), length)],
                dst_ref=recv.at[slot + distance - 1, pl.ds(0, length)],
                send_sem=send_sem.at[slot + distance - 1],
                recv_sem=recv_sem.at[slot + distance - 1],
                device_id=target,
                device_id_type=MESH,
            )
            copy.start()
            copies.append(copy)
            if loss_slot is not None:
                copy = pltpu.make_async_remote_copy(
                    src_ref=lbuf.at[loss_slot[0]],
                    dst_ref=lrecv.at[loss_slot[1] + distance - 1],
                    send_sem=lsend_sem.at[loss_slot[1] + distance - 1],
                    recv_sem=lrecv_sem.at[loss_slot[1] + distance - 1],
                    device_id=target,
                    device_id_type=MESH,
                )
                copy.start()
                copies.append(copy)
        for copy in copies:
            copy.wait()

    loss = l_ref[...]
    slot = 0
    lslot = 0
    start = 0
    length = o_ref.shape[0]
    for stage, (axis, bits) in enumerate(steps):
        fan = 1 << len(bits)
        lbuf[stage] = loss
        if axis == "tile":
            length //= fan
            send_all(axis, bits, slot, lambda d: start + rank(axis, bits, d) * length, length, (stage, lslot))
            start = start + rank(axis, bits) * length
            mine = pl.ds(pl.multiple_of(start, 8), length)
            total = o_ref[mine]
            for distance in range(1, fan):
                total = total + recv[slot + distance - 1, pl.ds(0, length)]
            o_ref[mine] = total
        else:
            send_all(axis, bits, slot, lambda d: start, length, (stage, lslot))
            mine = pl.ds(pl.multiple_of(start, 8), length)
            own = o_ref[mine]
            blocks = [own] + [recv[slot + distance - 1, pl.ds(0, length)] for distance in range(1, fan)]
            o_ref[mine] = jnp.where(start < width, ordered_sum(blocks, axis, bits), own)
        loss = ordered_sum([loss] + [lrecv[lslot + distance - 1] for distance in range(1, fan)], axis, bits)
        slot += fan - 1
        lslot += fan - 1
    lo_ref[...] = loss
    for bits in reversed(tile_groups):
        fan = 1 << len(bits)
        send_all("tile", bits, slot, lambda d: start, length)
        base = start - rank("tile", bits) * length
        for distance in range(1, fan):
            spot = base + rank("tile", bits, distance) * length
            o_ref[pl.ds(pl.multiple_of(spot, 8), length)] = recv[slot + distance - 1, pl.ds(0, length)]
        start = base
        length *= fan
        slot += fan - 1
    gb_ref[...] = o_ref[pl.ds(0, width)]
    gi_ref[pl.ds(0, half)] = o_ref[pl.ds(width, half), pl.ds(0, half)]
    gi_ref[pl.ds(half, half)] = o_ref[pl.ds(width, half), pl.ds(half, half)]
    gu_ref[...] = o_ref[pl.ds(width + half, half)]


def all_reduce(bilinear_part, in_part, out_part, loss_block):
    packed = jax.ShapeDtypeStruct((bilinear_part.shape[0] * 2,) + bilinear_part.shape[1:], bilinear_part.dtype)
    slots = 2 * (1 + 1 + 7) + 7
    loss_slots = 1 + 1 + 7 + 7
    return pl.pallas_call(
        reduce_kernel,
        out_shape=tuple(
            jax.ShapeDtypeStruct(part.shape, part.dtype)
            for part in (bilinear_part, in_part, out_part, loss_block)
        ),
        in_specs=[pl.BlockSpec(memory_space=pltpu.VMEM)] * 4,
        out_specs=tuple(pl.BlockSpec(memory_space=pltpu.VMEM) for _ in range(4)),
        scratch_shapes=[
            pltpu.VMEM(packed.shape, packed.dtype),
            pltpu.VMEM((slots, packed.shape[0] // 2) + packed.shape[1:], packed.dtype),
            pltpu.VMEM((loss_slots,) + loss_block.shape, loss_block.dtype),
            pltpu.VMEM((4,) + loss_block.shape, loss_block.dtype),
            pltpu.SemaphoreType.DMA((slots,)),
            pltpu.SemaphoreType.DMA((slots,)),
            pltpu.SemaphoreType.DMA((loss_slots,)),
            pltpu.SemaphoreType.DMA((loss_slots,)),
        ],
        compiler_params=pltpu.CompilerParams(collective_id=0, has_side_effects=True),
    )(bilinear_part, in_part, out_part, loss_block)

def pair_slope(raw_score, target, weight, heavy_weight, factor):
    chance = jax.nn.sigmoid(raw_score)
    signed = (1.0 - target) * chance - heavy_weight * target * (1.0 - chance)
    return (weight * signed * factor).astype(jnp.bfloat16)


def pair_cost(raw_score, target, weight, heavy_weight):
    missed = heavy_weight * target * jnp.log1p(jnp.exp(-raw_score))
    spurious = (1.0 - target) * jnp.log1p(jnp.exp(raw_score))
    return jnp.sum(weight * (missed + spurious))


def local(features, w_in, w_out, bilinear, partner, counts):
    row_part = features.shape[1]
    feature_width = features.shape[4]
    groups = lax.axis_size("mlp")
    site_rows = row_part * groups
    tile_count = lax.axis_size("tile")
    grid_depth = tile_count // 8
    tile_here = lax.axis_index("tile")
    member = lax.axis_index("mlp")
    block_x = tile_here // (4 * grid_depth)
    block_y = tile_here // grid_depth % 4
    block_z = tile_here % grid_depth
    heavy_weight = 27 * site_rows // 4
    score_scale = feature_width ** (-0.5)
    factor = score_scale / (2 * tile_count * site_rows)
    own_rows = member * row_part + jnp.arange(row_part, dtype=jnp.int32)
    all_rows = jnp.arange(site_rows, dtype=jnp.int32)
    mine_counts = lax.dynamic_index_in_dim(counts, tile_here, 0, keepdims=False)
    mine_partner = lax.dynamic_index_in_dim(partner, tile_here, 0, keepdims=False)
    own_partner = lax.dynamic_slice_in_dim(mine_partner, member * row_part, row_part, 1)
    own_pre_ok = own_rows[None, :] < mine_counts[:, 0:1]
    own_post_ok = own_rows[None, :] < mine_counts[:, 1:2]
    local_x = features.reshape(row_part, 4, feature_width)
    weights = butterfly_gather(jnp.stack([w_in.T, w_out], 1), "mlp")
    own_hidden = jnp.einsum("rcf,hf->rch", local_x, weights[:, 0], preferred_element_type=jnp.float32)
    own_active = jax.nn.gelu(own_hidden).astype(jnp.bfloat16)
    mixed_rows = jnp.einsum("rch,hf->rcf", own_active, weights[:, 1], preferred_element_type=jnp.float32)
    embedded = (local_x.astype(jnp.float32) + mixed_rows).astype(jnp.bfloat16)
    pre_local = embedded[:, 0::2]
    post_local = embedded[:, 1::2]
    query_local = jnp.einsum(
        "ruf,fg->rug", pre_local, bilinear, preferred_element_type=jnp.float32
    ).astype(jnp.bfloat16)

    x_stride = 4 * grid_depth
    y_stride = grid_depth
    query_all = butterfly_gather(query_local, "mlp")
    facing = jnp.where(block_x == 0, post_local[:, 1], post_local[:, 0])
    x_pairs = [(s, (s + x_stride) % tile_count) for s in range(tile_count)]
    from_x = lax.ppermute(facing, "tile", x_pairs)
    halo = jnp.stack([from_x, post_local[:, 0], post_local[:, 1]], 0)

    def position(s, stride, extent):
        return (s // stride) % extent

    def along(arr, stride, extent):
        lower = [(s, s + stride) for s in range(tile_count) if position(s, stride, extent) < extent - 1]
        upper = [(s, s - stride) for s in range(tile_count) if position(s, stride, extent) > 0]
        return jnp.stack(
            [lax.ppermute(arr, "tile", lower), arr, lax.ppermute(arr, "tile", upper)], 0
        )

    def along_back(arr, stride, extent):
        lower = [(s, s - stride) for s in range(tile_count) if position(s, stride, extent) > 0]
        upper = [(s, s + stride) for s in range(tile_count) if position(s, stride, extent) < extent - 1]
        return arr[1] + lax.ppermute(arr[0], "tile", lower) + lax.ppermute(arr[2], "tile", upper)

    halo = along(along(halo, y_stride, 4), 1, grid_depth)
    steps = jnp.arange(3, dtype=jnp.int32) - 1
    dz_grid = steps[:, None]
    dy_grid = steps[None, :]
    inside = (
        (block_y + dy_grid >= 0)
        & (block_y + dy_grid < 4)
        & (block_z + dz_grid >= 0)
        & (block_z + dz_grid < grid_depth)
    )
    near = jnp.clip(tile_here + dy_grid * y_stride + dz_grid, 0, tile_count - 1)
    far = (near + x_stride) % tile_count
    col_counts = jnp.stack(
        [counts[far, block_x, 1], counts[near, 0, 1], counts[near, 1, 1]], -1
    )
    j_ok = inside[..., None, None] & (own_rows < col_counts[..., None])
    loss_sum = jnp.zeros((), jnp.float32)
    post_grad_parts = jnp.zeros(halo.shape, jnp.float32)
    query_grads = []
    place = jnp.arange(3, dtype=jnp.int32)
    code_base = (place[None, None, :] * 9 + (dy_grid[..., None] + 1) * 3 + dz_grid[..., None] + 1) * site_rows
    col_key = (code_base[..., None] + own_rows).reshape(-1)
    for pretile, order, edge in ((0, (0, 1, 2), 0), (1, (1, 2, 0), 2)):
        edge_ok = (block_x == 1) if pretile == 0 else (block_x == 0)
        ordered = halo[:, :, order]
        others = ordered.reshape(-1, feature_width)
        x_ok = jnp.stack([edge_ok if p == edge else jnp.bool_(True) for p in range(3)])
        col_ok = (j_ok[:, :, order] & x_ok[None, None, :, None]).reshape(-1)
        queries = query_all[:, pretile]
        raw_score = (
            jnp.einsum("rf,cf->rc", queries, others, preferred_element_type=jnp.float32)
            * score_scale
        )
        row_ok = all_rows < mine_counts[pretile, 0]
        target = (mine_partner[pretile][:, None] == col_key[None, :]).astype(jnp.float32)
        weight = (row_ok[:, None] & col_ok[None, :]).astype(jnp.float32)
        loss_sum = loss_sum + pair_cost(raw_score, target, weight, heavy_weight)
        slope = pair_slope(raw_score, target, weight, heavy_weight, factor)
        query_grads.append(jnp.dot(slope, others, preferred_element_type=jnp.float32))
        back = jnp.einsum("rc,rf->cf", slope, queries, preferred_element_type=jnp.float32)
        back = back.reshape(ordered.shape)
        for p in range(3):
            post_grad_parts = post_grad_parts.at[:, :, order[p]].add(back[:, :, p])
    post_grad_parts = along_back(along_back(post_grad_parts, 1, grid_depth), y_stride, 4)
    back_x = lax.ppermute(post_grad_parts[0], "tile", x_pairs)
    post_back = jnp.stack(
        [
            post_grad_parts[1] + jnp.where(block_x == 1, back_x, 0.0),
            post_grad_parts[2] + jnp.where(block_x == 0, back_x, 0.0),
        ],
        1,
    )
    query_back = butterfly_scatter(jnp.stack(query_grads, 1), "mlp").astype(jnp.bfloat16)
    bilinear_part = jnp.einsum(
        "ruf,rug->fg", pre_local, query_back, preferred_element_type=jnp.float32
    )
    pre_back = jnp.einsum("rug,fg->ruf", query_back, bilinear, preferred_element_type=jnp.float32)
    embed_grad = jnp.stack(
        [pre_back[:, 0], post_back[:, 0], pre_back[:, 1], post_back[:, 1]], 1
    ).astype(jnp.bfloat16)
    whole_x = butterfly_gather(local_x, "mlp")
    hidden_pre = jnp.einsum("rcf,fh->rch", whole_x, w_in, preferred_element_type=jnp.float32)
    active = jax.nn.gelu(hidden_pre).astype(jnp.bfloat16)
    pre_whole = butterfly_gather(pre_back.astype(jnp.bfloat16), "mlp")
    post_whole = butterfly_gather(post_back.astype(jnp.bfloat16), "mlp")
    embed_whole = jnp.stack([pre_whole[:, 0], post_whole[:, 0], pre_whole[:, 1], post_whole[:, 1]], 1)
    active_grad = jnp.einsum("rcf,hf->rch", embed_whole, w_out, preferred_element_type=jnp.float32)
    unused, pullback = jax.vjp(jax.nn.gelu, hidden_pre)
    hidden_grad = pullback(active_grad)[0].astype(jnp.bfloat16)
    in_part = jnp.einsum("rcf,rch->fh", whole_x, hidden_grad, preferred_element_type=jnp.float32)
    out_part = jnp.einsum("rch,rcf->hf", active, embed_whole, preferred_element_type=jnp.float32)
    grad_bilinear, grad_in, grad_out, loss_block = all_reduce(
        bilinear_part, in_part, out_part, jnp.broadcast_to(loss_sum, (8, 128))
    )
    loss_total = loss_block[0, 0]
    pair_loss = loss_total / (2.0 * tile_count * site_rows * 27 * site_rows)
    return (pair_loss, grad_in, grad_out, grad_bilinear)


def solution(mesh):
    placed = (P("tile", "mlp", None, None, None), P(None, "mlp"), P("mlp", None), P(), P(), P())
    return jax.shard_map(
        local,
        mesh=mesh,
        in_specs=placed,
        out_specs=(P(), P(None, "mlp"), P("mlp", None), P()),
        check_vma=False,
    )
```
